32 devices in a mesh: rep: 4 (over y, core), shard: 4 (over z), ctx: 2 (over x).
Axes of the slice: x: 2, y: 2, z: 4, core: 2. Of those that a mesh axis runs over, the one named last changes fastest.
Arguments:
- tokens: bfloat16 [2, 4, 512, 2048], P(None, 'rep', ('shard', 'ctx')), may hold values from -6 to 6
- span_starts: int32 [2, 4], P(None, 'rep'), may hold values from 0 to 256
- cotangent: bfloat16 [2, 4, 512, 2048], P(None, 'rep', ('shard', 'ctx')), may hold values from -6 to 6
- w_query: bfloat16 [2048, 2048], P('shard'), may hold values from -0.125 to 0.125
- key_weight: bfloat16 [2048, 1024], P('shard'), may hold values from -0.125 to 0.125
- value_weight: bfloat16 [2048, 1024], P('shard'), may hold values from -0.125 to 0.125
- w_out: bfloat16 [2048, 2048], P('shard'), may hold values from -0.75 to 0.75
- attn_gain: bfloat16 [2048], P('shard'), may hold values from 0.099609375 to 1.8984375
- query_gain: bfloat16 [128], P('shard'), may hold values from 0.099609375 to 1.8984375
- key_gain: bfloat16 [128], P('shard'), may hold values from 0.099609375 to 1.8984375
- w_gate: bfloat16 [2048, 6144], P('shard'), may hold values from -0.125 to 0.125
- w_up: bfloat16 [2048, 6144], P('shard'), may hold values from -0.125 to 0.125
- w_down: bfloat16 [6144, 2048], P('shard'), may hold values from -0.078125 to 0.078125
- ffn_gain: bfloat16 [2048], P('shard'), may hold values from 0.099609375 to 1.8984375
Outputs:
- output: bfloat16 [2, 4, 512, 2048], P(None, 'rep', ('shard', 'ctx'))
- input_grad: float32 [2, 4, 512, 2048], P(None, 'rep', ('shard', 'ctx'))
- grad_query: float32 [2048, 2048], P('shard')
- grad_key: float32 [2048, 1024], P('shard')
- grad_value: float32 [2048, 1024], P('shard')
- grad_out: float32 [2048, 2048], P('shard')
- grad_attn_gain: float32 [2048], P('shard')
- grad_query_gain: float32 [128], P('shard')
- grad_key_gain: float32 [128], P('shard')
- grad_gate: float32 [2048, 6144], P('shard')
- grad_up: float32 [2048, 6144], P('shard')
- grad_down: float32 [6144, 2048], P('shard')
- grad_ffn_gain: float32 [2048], P('shard')
The draws below stay inside these ranges and needn't reach their ends.
Inputs may be any that keep to these rules, and one draw needn't show every extreme that they name: `span_starts`: each sequence's picture span covers positions start to start + 255 of that sequence.
All inputs are finite; a program needn't handle non-finite values.
Results may differ from the reference program's by a relative error of at most 0.023.
Values may be sent and summed in bfloat16 or wider, within the bound.
No kernel may reach another device: no remote copies, remote signals or barrier semaphores. Data moves between devices by JAX's collectives and lax.ppermute only.
A program may use at most 448 MiB of HBM per device.

```python
import jax
import jax.numpy as jnp
from jax import lax

MODEL_WIDTH = 2048
QUERY_HEADS = 16
KEY_VALUE_HEADS = 8
HEAD_SIZE = 128
FF = 6144
CT = 64
MB = 2
PIC = 256
GROUPS = 4
SEQ = 512
N_SHARD = 4
N_CTX = 2


def touch_ends(values, key, smallest, top_value):
    dims = values.shape
    spot = [jax.random.randint(jax.random.fold_in(key, axis), (), 0, dims[axis]) for axis in range(len(dims))]
    values = values.at[tuple(spot)].set(smallest)
    longest = dims.index(max(dims))
    spot[longest] = (spot[longest] + 1) % dims[longest]
    return values.at[tuple(spot)].set(top_value)


def level_of(key, shape, cuts, least, high):
    def one(position, shards_of):
        heights = jax.random.uniform(jax.random.fold_in(jax.random.fold_in(key, 6), position), (shards_of,), jnp.float32, least / len(cuts), high / len(cuts))
        return jnp.repeat(jnp.exp(heights), shape[position] // shards_of).reshape((-1,) + (1,) * (len(shape) - position - 1))

    factor_of = one(*cuts[0])
    for cut in cuts[1:]:
        factor_of = factor_of * one(*cut)
    return factor_of


def scatter_about(key, extent, width, bound, shards=(), kind=jnp.bfloat16):
    loudness = level_of(key, extent, shards, -0.22, 0.18) if shards else 1.0
    array = jax.random.normal(key, extent, jnp.float32) * width * loudness
    return jnp.minimum(jnp.maximum(array, -bound), bound).astype(kind)


def setup_inputs(seed: int = 0) -> dict:
    key_of = jax.random.split(jax.random.key(seed), 15)
    tokens = scatter_about(key_of[0], (MB, GROUPS, SEQ, MODEL_WIDTH), 1.0, 6.0, ((1, 4), (2, 8)))
    span_starts = touch_ends(jax.random.randint(key_of[1], (MB, GROUPS), 0, CT * N_SHARD * N_CTX - PIC + 1), jax.random.fold_in(key_of[1], 1), 0, CT * N_SHARD * N_CTX - PIC).astype(jnp.int32)
    cotangent = scatter_about(key_of[2], (MB, GROUPS, SEQ, MODEL_WIDTH), 1.0, 6.0, ((1, 4), (2, 8)))
    w_query = scatter_about(key_of[3], (MODEL_WIDTH, QUERY_HEADS * HEAD_SIZE), MODEL_WIDTH ** -0.5, 0.125, ((0, 4),))
    key_weight = scatter_about(key_of[4], (MODEL_WIDTH, KEY_VALUE_HEADS * HEAD_SIZE), MODEL_WIDTH ** -0.5, 0.125, ((0, 4),))
    value_weight = scatter_about(key_of[5], (MODEL_WIDTH, KEY_VALUE_HEADS * HEAD_SIZE), MODEL_WIDTH ** -0.5, 0.125, ((0, 4),))
    w_out = scatter_about(key_of[6], (QUERY_HEADS * HEAD_SIZE, MODEL_WIDTH), (max(1, QUERY_HEADS * HEAD_SIZE * 16 // (CT * N_SHARD * N_CTX))) ** -0.5, 0.75, ((0, 4),))
    attn_gain = jnp.clip(1.0 + 0.18 * jax.random.normal(key_of[7], (MODEL_WIDTH,), jnp.float32), 0.099609375, 1.8984375).astype(jnp.bfloat16)
    query_gain = jnp.clip(1.0 + 0.18 * jax.random.normal(key_of[8], (HEAD_SIZE,), jnp.float32), 0.099609375, 1.8984375).astype(jnp.bfloat16)
    key_gain = jnp.clip(1.0 + 0.18 * jax.random.normal(key_of[9], (HEAD_SIZE,), jnp.float32), 0.099609375, 1.8984375).astype(jnp.bfloat16)
    w_gate = scatter_about(key_of[10], (MODEL_WIDTH, FF), MODEL_WIDTH ** -0.5, 0.125, ((0, 4),))
    w_up = scatter_about(key_of[11], (MODEL_WIDTH, FF), MODEL_WIDTH ** -0.5, 0.125, ((0, 4),))
    w_down = scatter_about(key_of[12], (FF, MODEL_WIDTH), FF ** -0.5, 0.078125, ((0, 4),))
    ffn_gain = jnp.clip(1.0 + 0.18 * jax.random.normal(key_of[13], (MODEL_WIDTH,), jnp.float32), 0.099609375, 1.8984375).astype(jnp.bfloat16)
    return dict(tokens=tokens, span_starts=span_starts, cotangent=cotangent, w_query=w_query, key_weight=key_weight, value_weight=value_weight, w_out=w_out, attn_gain=attn_gain, query_gain=query_gain, key_gain=key_gain, w_gate=w_gate, w_up=w_up, w_down=w_down, ffn_gain=ffn_gain)


@jax.custom_vjp
def reduced_precision(v):
    return lax.optimization_barrier(v.astype(jnp.bfloat16)).astype(jnp.float32)

@jax.custom_vjp
def reduced_backward(v):
    return v

def low_keep(v):
    return (reduced_precision(v), None)

def low_pass(kept, grad):
    return (grad,)

def back_keep(v):
    return (v, None)

def back_low(kept, grad):
    return (reduced_precision(grad),)
reduced_precision.defvjp(low_keep, low_pass)
reduced_backward.defvjp(back_keep, back_low)
EPSILON = 1e-06
THETA = 1000000.0
HIGHEST_ACCURACY = lax.Precision.HIGHEST

def norm_rows(values, gain):
    return values * lax.rsqrt(lax.optimization_barrier(jnp.mean(values * values, axis=-1, keepdims=True)) + EPSILON) * gain

def apply_rotation(values):
    half_width = values.shape[-1] // 2
    return jnp.concatenate([-values[..., half_width:], values[..., :half_width]], axis=-1)

def head_mix(allowed, pieces):
    q_head, k_head, v_head = pieces
    scores = jnp.einsum('tgd,sd->gts', q_head, k_head, precision=HIGHEST_ACCURACY) * HEAD_SIZE ** (-0.5)
    scores = jnp.where(allowed, reduced_backward(scores), -1e+30)
    probs_low = reduced_precision(jax.nn.softmax(scores, axis=-1))
    return jnp.einsum('gts,sd->tgd', probs_low, v_head, precision=HIGHEST_ACCURACY)

def sequence(hidden_in, span_start, w_query, key_weight, value_weight, w_out, attn_gain, query_gain, key_gain, w_gate, w_up, w_down, ffn_gain):
    token_length = hidden_in.shape[0]
    group_width = QUERY_HEADS // KEY_VALUE_HEADS
    positions = jnp.arange(token_length, dtype=jnp.int32)
    inverse = THETA ** (-jnp.arange(HEAD_SIZE // 2, dtype=jnp.float32) * 2.0 / HEAD_SIZE)
    angles = positions.astype(jnp.float32)[:, None] * inverse[None, :]
    cosine_table = jnp.concatenate([jnp.cos(angles), jnp.cos(angles)], axis=-1)[:, None, :]
    sine_values = jnp.concatenate([jnp.sin(angles), jnp.sin(angles)], axis=-1)[:, None, :]
    normalized_rows = reduced_precision(norm_rows(hidden_in, attn_gain))
    q_pre = reduced_backward(jnp.dot(normalized_rows, w_query, precision=HIGHEST_ACCURACY)).reshape(token_length, QUERY_HEADS, HEAD_SIZE)
    key_before_rotation = reduced_backward(jnp.dot(normalized_rows, key_weight, precision=HIGHEST_ACCURACY)).reshape(token_length, KEY_VALUE_HEADS, HEAD_SIZE)
    value_matrix = reduced_backward(reduced_precision(jnp.dot(normalized_rows, value_weight, precision=HIGHEST_ACCURACY))).reshape(token_length, KEY_VALUE_HEADS, HEAD_SIZE)
    unit_query = norm_rows(q_pre, query_gain)
    unit_k = norm_rows(key_before_rotation, key_gain)
    query_rows = reduced_precision(unit_query * cosine_table + apply_rotation(unit_query) * sine_values).reshape(token_length, KEY_VALUE_HEADS, group_width, HEAD_SIZE)
    key_rows = reduced_precision(unit_k * cosine_table + apply_rotation(unit_k) * sine_values)
    inside = (positions >= span_start) & (positions < span_start + PIC)
    allowed = (positions[None, :] <= positions[:, None]) | inside[:, None] & inside[None, :]
    mixed_split = lax.map(jax.checkpoint(lambda pieces: head_mix(allowed, pieces)), (jnp.transpose(query_rows, (1, 0, 2, 3)), jnp.transpose(key_rows, (1, 0, 2)), jnp.transpose(value_matrix, (1, 0, 2))))
    mixed_heads = jnp.transpose(mixed_split, (1, 0, 2, 3)).reshape(token_length, QUERY_HEADS * HEAD_SIZE)
    mixed_heads = reduced_backward(reduced_precision(mixed_heads))
    branch = reduced_backward(jnp.dot(mixed_heads, w_out, precision=HIGHEST_ACCURACY))
    middle = hidden_in + branch
    ffn_in = reduced_precision(norm_rows(middle, ffn_gain))
    gate_pre = reduced_backward(jnp.dot(ffn_in, w_gate, precision=HIGHEST_ACCURACY))
    up_pre = reduced_backward(jnp.dot(ffn_in, w_up, precision=HIGHEST_ACCURACY))
    inner_act = reduced_precision(jax.nn.silu(gate_pre) * up_pre)
    return middle + reduced_backward(jnp.dot(inner_act, w_down, precision=HIGHEST_ACCURACY))

def reference(tokens, span_starts, cotangent, w_query, key_weight, value_weight, w_out, attn_gain, query_gain, key_gain, w_gate, w_up, w_down, ffn_gain):
    params = tuple((weight.astype(jnp.float32) for weight in (w_query, key_weight, value_weight, w_out, attn_gain, query_gain, key_gain, w_gate, w_up, w_down, ffn_gain)))
    flat_in = tokens.astype(jnp.float32).reshape(MB * GROUPS, SEQ, MODEL_WIDTH)
    flat_starts = span_starts.reshape(MB * GROUPS).astype(jnp.int32)
    flat_cot = cotangent.astype(jnp.float32).reshape(MB * GROUPS, SEQ, MODEL_WIDTH)

    def forward(layer_in, *weight_set):

        def per_sequence(pair):
            return sequence(pair[0], pair[1], *weight_set)
        return lax.map(jax.checkpoint(per_sequence), (layer_in, flat_starts))
    layer_out, pullback = jax.vjp(forward, flat_in, *params)
    grads = pullback(flat_cot)
    full_shape = tokens.shape
    return (layer_out.astype(jnp.bfloat16).reshape(full_shape), grads[0].reshape(full_shape), grads[1], grads[2], grads[3], grads[4], grads[5], grads[6], grads[7], grads[8], grads[9], grads[10], grads[11])
```

```python
from functools import partial

import jax
import jax.numpy as jnp
from jax import lax
from jax.experimental import pallas as pl
from jax.experimental.pallas import tpu as pltpu
from jax.sharding import Mesh
from jax.sharding import PartitionSpec as P

QUERY_HEADS = 16
KEY_VALUE_HEADS = 8
HEAD_SIZE = 128
PIC = 256


EPSILON = 1e-06
THETA = 1000000.0


def apply_rotation(values):
    half_width = values.shape[-1] // 2
    return jnp.concatenate([-values[..., half_width:], values[..., :half_width]], axis=-1)


def rotate_back(values):
    half_width = values.shape[-1] // 2
    return jnp.concatenate([values[..., half_width:], -values[..., :half_width]], axis=-1)


def spin_tables(positions):
    inverse = THETA ** (-jnp.arange(HEAD_SIZE // 2, dtype=jnp.float32) * 2.0 / HEAD_SIZE)
    angles = positions.astype(jnp.float32)[:, None] * inverse[None, :]
    cosine_table = jnp.concatenate([jnp.cos(angles), jnp.cos(angles)], axis=-1)[:, None, :]
    sine_values = jnp.concatenate([jnp.sin(angles), jnp.sin(angles)], axis=-1)[:, None, :]
    return (cosine_table, sine_values)


def recip_rms(values):
    return lax.rsqrt(jnp.mean(values * values, axis=-1, keepdims=True) + EPSILON)


def norm_back(unit, recip, gain, d_normed):
    d_unit = d_normed * gain
    return recip * (d_unit - unit * jnp.mean(d_unit * unit, axis=-1, keepdims=True))


def over_rows(left, right):
    return lax.dot_general(
        left, right, (((0,), (0,)), ((), ())), preferred_element_type=jnp.float32
    )


def compared_to(left, right):
    return lax.dot_general(
        left, right, (((1,), (1,)), ((), ())), preferred_element_type=jnp.float32
    )


def attention_set(w_query, key_weight, value_weight, w_out, attn_gain, query_gain, key_gain):
    return (
        lax.all_gather(w_query, "shard", axis=0, tiled=True),
        lax.all_gather(key_weight, "shard", axis=0, tiled=True),
        lax.all_gather(value_weight, "shard", axis=0, tiled=True),
        lax.all_gather(w_out, "shard", axis=0, tiled=True),
        lax.all_gather(attn_gain, "shard", axis=0, tiled=True),
        lax.all_gather(query_gain, "shard", axis=0, tiled=True),
        lax.all_gather(key_gain, "shard", axis=0, tiled=True),
    )


def feedforward_set(w_gate, w_up, w_down, ffn_gain):
    return (
        lax.all_gather(w_gate, "shard", axis=0, tiled=True),
        lax.all_gather(w_up, "shard", axis=0, tiled=True),
        lax.all_gather(w_down, "shard", axis=0, tiled=True),
        lax.all_gather(ffn_gain, "shard", axis=0, tiled=True),
    )


def masked_scores(allowed, q_head, k_head):
    scores = jnp.einsum(
        "tgd,sd->gts", q_head, k_head, preferred_element_type=jnp.float32
    ) * HEAD_SIZE ** (-0.5)
    return jnp.where(allowed, scores, -1e30)


def head_forward(allowed, pieces):
    q_head, k_head, v_head = pieces
    scores = masked_scores(allowed, q_head, k_head)
    highest = jnp.max(scores, axis=-1, keepdims=True)
    log_total = highest + jnp.log(jnp.sum(jnp.exp(scores - highest), axis=-1, keepdims=True))
    probs_low = jnp.exp(scores - log_total).astype(jnp.bfloat16)
    mixed = jnp.einsum("gts,sd->tgd", probs_low, v_head, preferred_element_type=jnp.float32)
    return (mixed, log_total)


def head_backward(allowed, pieces):
    q_head, k_head, v_head, d_mix_head, log_total = pieces
    probs = jnp.exp(masked_scores(allowed, q_head, k_head) - log_total)
    probs_low = probs.astype(jnp.bfloat16)
    d_probs = jnp.einsum("tgd,sd->gts", d_mix_head, v_head, preferred_element_type=jnp.float32)
    d_values = jnp.einsum("gts,tgd->sd", probs_low, d_mix_head, preferred_element_type=jnp.float32)
    row_dot = jnp.sum(probs * d_probs, axis=-1, keepdims=True)
    d_scores = (probs * (d_probs - row_dot)).astype(jnp.bfloat16)
    d_queries = jnp.einsum(
        "gts,sd->tgd", d_scores, k_head, preferred_element_type=jnp.float32
    ) * HEAD_SIZE ** (-0.5)
    d_keys = jnp.einsum(
        "gts,tgd->sd", d_scores, q_head, preferred_element_type=jnp.float32
    ) * HEAD_SIZE ** (-0.5)
    return (d_queries, d_keys, d_values)


def shards_general(
    tokens,
    span_starts,
    cotangent,
    w_query,
    key_weight,
    value_weight,
    w_out,
    attn_gain,
    query_gain,
    key_gain,
    w_gate,
    w_up,
    w_down,
    ffn_gain,
):
    seq_count = lax.axis_size(("shard", "ctx"))
    seq_rank = lax.axis_index(("shard", "ctx"))
    token_rows = tokens.shape[2]
    token_length = token_rows * seq_count
    group_width = QUERY_HEADS // KEY_VALUE_HEADS
    local_pos = seq_rank * token_rows + jnp.arange(token_rows, dtype=jnp.int32)
    key_pos = jnp.arange(token_length, dtype=jnp.int32)
    cosine_table, sine_values = spin_tables(local_pos)
    cos_keys = cosine_table[:, 0, :][None]
    sin_keys = sine_values[:, 0, :][None]
    out_list = []
    grad_list = []
    stored = []
    totals = None
    for micro_index in range(tokens.shape[0]):
        span_start = span_starts[micro_index, 0]
        inside_q = (local_pos >= span_start) & (local_pos < span_start + PIC)
        inside_k = (key_pos >= span_start) & (key_pos < span_start + PIC)
        allowed = (key_pos[None, :] <= local_pos[:, None]) | inside_q[:, None] & inside_k[None, :]
        hidden_in = tokens[micro_index, 0].astype(jnp.float32)
        full_query, full_key, full_value, complete_output, gain_attn, gain_query, gain_key = (
            attention_set(w_query, key_weight, value_weight, w_out, attn_gain, query_gain, key_gain)
        )
        gain_attn = gain_attn.astype(jnp.float32)
        gain_query = gain_query.astype(jnp.float32)
        gain_key = gain_key.astype(jnp.float32)
        recip_h = recip_rms(hidden_in)
        unit_h = hidden_in * recip_h
        normalized_rows = (unit_h * gain_attn).astype(jnp.bfloat16)
        q_pre = jnp.dot(normalized_rows, full_query, preferred_element_type=jnp.float32).reshape(
            token_rows, QUERY_HEADS, HEAD_SIZE
        )
        key_before_rotation = jnp.transpose(
            jnp.dot(normalized_rows, full_key, preferred_element_type=jnp.float32).reshape(
                token_rows, KEY_VALUE_HEADS, HEAD_SIZE
            ),
            (1, 0, 2),
        )
        value_local = jnp.transpose(
            jnp.dot(normalized_rows, full_value, preferred_element_type=jnp.float32)
            .astype(jnp.bfloat16)
            .reshape(token_rows, KEY_VALUE_HEADS, HEAD_SIZE),
            (1, 0, 2),
        )
        recip_q = recip_rms(q_pre)
        unit_query = q_pre * recip_q
        recip_k = recip_rms(key_before_rotation)
        unit_k = key_before_rotation * recip_k
        scaled_q = unit_query * gain_query
        scaled_k = unit_k * gain_key
        query_rows = jnp.transpose(
            (scaled_q * cosine_table + apply_rotation(scaled_q) * sine_values)
            .astype(jnp.bfloat16)
            .reshape(token_rows, KEY_VALUE_HEADS, group_width, HEAD_SIZE),
            (1, 0, 2, 3),
        )
        key_local = (scaled_k * cos_keys + apply_rotation(scaled_k) * sin_keys).astype(jnp.bfloat16)
        key_rows, value_matrix = (
            lax.all_gather(key_local, ("shard", "ctx"), axis=1, tiled=True),
            lax.all_gather(value_local, ("shard", "ctx"), axis=1, tiled=True),
        )
        mixed_split, log_total = lax.map(
            partial(head_forward, allowed), (query_rows, key_rows, value_matrix)
        )
        mixed_heads = (
            jnp.transpose(mixed_split, (1, 0, 2, 3))
            .reshape(token_rows, QUERY_HEADS * HEAD_SIZE)
            .astype(jnp.bfloat16)
        )
        middle = hidden_in + jnp.dot(
            mixed_heads, complete_output, preferred_element_type=jnp.float32
        )
        full_gate, full_up, full_down, gain_ffn = feedforward_set(w_gate, w_up, w_down, ffn_gain)
        gain_ffn = gain_ffn.astype(jnp.float32)
        recip_m = recip_rms(middle)
        unit_m = middle * recip_m
        ffn_in = (unit_m * gain_ffn).astype(jnp.bfloat16)
        gate_pre = jnp.dot(ffn_in, full_gate, preferred_element_type=jnp.float32)
        up_pre = jnp.dot(ffn_in, full_up, preferred_element_type=jnp.float32)
        sigma = jax.nn.sigmoid(gate_pre)
        act_gate = gate_pre * sigma
        inner_act = (act_gate * up_pre).astype(jnp.bfloat16)
        result = middle + jnp.dot(inner_act, full_down, preferred_element_type=jnp.float32)
        out_list.append(result.astype(jnp.bfloat16))
        cot_rows = cotangent[micro_index, 0]
        cot_float = cot_rows.astype(jnp.float32)
        d_inner = compared_to(cot_rows, full_down)
        d_gate = (d_inner * up_pre * sigma * (1.0 + gate_pre * (1.0 - sigma))).astype(jnp.bfloat16)
        d_up = (d_inner * act_gate).astype(jnp.bfloat16)
        d_ffn_in = compared_to(d_gate, full_gate) + compared_to(d_up, full_up)
        ffn_gain_part = jnp.sum(d_ffn_in * unit_m, axis=0)
        d_middle = cot_float + norm_back(unit_m, recip_m, gain_ffn, d_ffn_in)
        branch_gradient = d_middle.astype(jnp.bfloat16)
        d_mixed = jnp.transpose(
            compared_to(branch_gradient, complete_output)
            .astype(jnp.bfloat16)
            .reshape(token_rows, KEY_VALUE_HEADS, group_width, HEAD_SIZE),
            (1, 0, 2, 3),
        )
        d_split_q, d_keys, d_values = lax.map(
            partial(head_backward, allowed),
            (query_rows, key_rows, value_matrix, d_mixed, log_total),
        )
        d_queries = jnp.transpose(d_split_q, (1, 0, 2, 3)).reshape(
            token_rows, QUERY_HEADS, HEAD_SIZE
        )
        d_key_local, d_value_local = (
            lax.psum_scatter(
                d_keys.astype(jnp.bfloat16), ("shard", "ctx"), scatter_dimension=1, tiled=True
            ).astype(jnp.float32),
            lax.psum_scatter(
                d_values.astype(jnp.bfloat16), ("shard", "ctx"), scatter_dimension=1, tiled=True
            ).astype(jnp.float32),
        )
        d_unit_q = d_queries * cosine_table + rotate_back(d_queries * sine_values)
        d_unit_k = d_key_local * cos_keys + rotate_back(d_key_local * sin_keys)
        query_gain_part = jnp.sum(d_unit_q * unit_query, axis=(0, 1))
        key_gain_part = jnp.sum(d_unit_k * unit_k, axis=(0, 1))
        d_q_pre = (
            norm_back(unit_query, recip_q, gain_query, d_unit_q)
            .astype(jnp.bfloat16)
            .reshape(token_rows, QUERY_HEADS * HEAD_SIZE)
        )
        d_k_pre = jnp.transpose(
            norm_back(unit_k, recip_k, gain_key, d_unit_k).astype(jnp.bfloat16), (1, 0, 2)
        ).reshape(token_rows, KEY_VALUE_HEADS * HEAD_SIZE)
        d_v_pre = jnp.transpose(d_value_local.astype(jnp.bfloat16), (1, 0, 2)).reshape(
            token_rows, KEY_VALUE_HEADS * HEAD_SIZE
        )
        d_normed = (
            compared_to(d_q_pre, full_query)
            + compared_to(d_k_pre, full_key)
            + compared_to(d_v_pre, full_value)
        )
        attn_gain_part = jnp.sum(d_normed * unit_h, axis=0)
        grad_list.append(d_middle + norm_back(unit_h, recip_h, gain_attn, d_normed))
        stored.append(
            (
                normalized_rows,
                d_q_pre,
                d_k_pre,
                d_v_pre,
                mixed_heads,
                branch_gradient,
                ffn_in,
                d_gate,
                d_up,
                inner_act,
                cot_rows,
            )
        )
        parts = (attn_gain_part, query_gain_part, key_gain_part, ffn_gain_part)
        if totals is None:
            totals = parts
        else:
            totals = tuple((older + newer for older, newer in zip(totals, parts)))
    joined = [
        jnp.concatenate([saved_set[member] for saved_set in stored], axis=0) for member in range(11)
    ]
    (
        normed_all,
        dq_all,
        dk_all,
        dv_all,
        mixed_all,
        branch_all,
        ffn_all,
        gate_all,
        up_all,
        inner_all,
        cot_all,
    ) = joined
    totals = (
        lax.psum_scatter(
            over_rows(normed_all, dq_all).astype(jnp.bfloat16),
            "shard",
            scatter_dimension=0,
            tiled=True,
        ).astype(jnp.float32),
        lax.psum_scatter(
            over_rows(normed_all, dk_all).astype(jnp.bfloat16),
            "shard",
            scatter_dimension=0,
            tiled=True,
        ).astype(jnp.float32),
        lax.psum_scatter(
            over_rows(normed_all, dv_all).astype(jnp.bfloat16),
            "shard",
            scatter_dimension=0,
            tiled=True,
        ).astype(jnp.float32),
        lax.psum_scatter(
            over_rows(mixed_all, branch_all).astype(jnp.bfloat16),
            "shard",
            scatter_dimension=0,
            tiled=True,
        ).astype(jnp.float32),
        lax.psum_scatter(
            totals[0].astype(jnp.bfloat16), "shard", scatter_dimension=0, tiled=True
        ).astype(jnp.float32),
        lax.psum_scatter(
            totals[1].astype(jnp.bfloat16), "shard", scatter_dimension=0, tiled=True
        ).astype(jnp.float32),
        lax.psum_scatter(
            totals[2].astype(jnp.bfloat16), "shard", scatter_dimension=0, tiled=True
        ).astype(jnp.float32),
        lax.psum_scatter(
            over_rows(ffn_all, gate_all).astype(jnp.bfloat16),
            "shard",
            scatter_dimension=0,
            tiled=True,
        ).astype(jnp.float32),
        lax.psum_scatter(
            over_rows(ffn_all, up_all).astype(jnp.bfloat16),
            "shard",
            scatter_dimension=0,
            tiled=True,
        ).astype(jnp.float32),
        lax.psum_scatter(
            over_rows(inner_all, cot_all).astype(jnp.bfloat16),
            "shard",
            scatter_dimension=0,
            tiled=True,
        ).astype(jnp.float32),
        lax.psum_scatter(
            totals[3].astype(jnp.bfloat16), "shard", scatter_dimension=0, tiled=True
        ).astype(jnp.float32),
    )
    summed = (
        lax.psum(totals[0].astype(jnp.bfloat16), ("rep", "ctx")).astype(jnp.float32),
        lax.psum(totals[1].astype(jnp.bfloat16), ("rep", "ctx")).astype(jnp.float32),
        lax.psum(totals[2].astype(jnp.bfloat16), ("rep", "ctx")).astype(jnp.float32),
        lax.psum(totals[3].astype(jnp.bfloat16), ("rep", "ctx")).astype(jnp.float32),
        lax.psum(totals[4].astype(jnp.bfloat16), ("rep", "ctx")).astype(jnp.float32),
        lax.psum(totals[5].astype(jnp.bfloat16), ("rep", "ctx")).astype(jnp.float32),
        lax.psum(totals[6].astype(jnp.bfloat16), ("rep", "ctx")).astype(jnp.float32),
        lax.psum(totals[7].astype(jnp.bfloat16), ("rep", "ctx")).astype(jnp.float32),
        lax.psum(totals[8].astype(jnp.bfloat16), ("rep", "ctx")).astype(jnp.float32),
        lax.psum(totals[9].astype(jnp.bfloat16), ("rep", "ctx")).astype(jnp.float32),
        lax.psum(totals[10].astype(jnp.bfloat16), ("rep", "ctx")).astype(jnp.float32),
    )
    output = jnp.stack(out_list)[:, None]
    input_grad = jnp.stack(grad_list)[:, None]
    return (
        output,
        input_grad,
        summed[0],
        summed[1],
        summed[2],
        summed[3],
        summed[4],
        summed[5],
        summed[6],
        summed[7],
        summed[8],
        summed[9],
        summed[10],
    )


def from_ring(block, axis, count):
    return [block] + [
        lax.ppermute(block, axis, [(i, (i + k) % count) for i in range(count)])
        for k in range(1, count)
    ]


def send_terms(pieces, axis, count):
    return [pieces[0]] + [
        lax.ppermute(
            pieces[count - k].astype(jnp.bfloat16),
            axis,
            [(i, (i + k) % count) for i in range(count)],
        )
        for k in range(1, count)
    ]


def sum_terms(terms):
    return sum(term.astype(jnp.float32) for term in terms)


def swap(values, axis):
    return lax.ppermute(values, axis, [(0, 1), (1, 0)])


def after(value, *others):
    return lax.optimization_barrier((value,) + others)[0] if others else value


def in_order(blocks, rank):
    count = len(blocks)
    twice = jnp.stack(blocks[::-1] + blocks[:0:-1])
    return lax.dynamic_slice_in_dim(twice, count - 1 - rank, count, axis=0)


def lane_sums(values):
    return sum(
        values[:, start : start + 128] for start in range(0, values.shape[1], 128)
    )


def add_sums(step, sums_ref, values):
    @pl.when(step == 0)
    def _():
        sums_ref[...] = values

    @pl.when(step > 0)
    def _():
        sums_ref[...] += values


def lay_in_kernel(z_ref, full_ref, gate_ref, up_ref, d_gate_ref, d_up_ref, sums_ref):
    columns = gate_ref.shape[1] // 2
    total = None
    for core in range(2):
        full = full_ref[0, core, 0, 0].astype(jnp.float32)
        span = slice(core * columns, (core + 1) * columns)
        d_gate = full[:, :columns]
        d_up = full[:, columns:]
        d_gate_ref[:, span] = d_gate
        d_up_ref[:, span] = d_up
        both = d_gate * gate_ref[:, span].astype(jnp.float32)
        both = lane_sums(both + d_up * up_ref[:, span].astype(jnp.float32))
        total = both if total is None else total + both
    add_sums(pl.program_id(1), sums_ref, total)


def lay_in(rank, full, w_gate, w_up):
    n_hi, _, n_ctx, n_shard, rows, both = full.shape
    shape = jax.ShapeDtypeStruct(w_gate.shape, jnp.float32)
    block = pl.BlockSpec((rows, both), lambda i, j, z: (i, (z[0] - j + n_shard) % n_shard))
    return pl.pallas_call(
        lay_in_kernel,
        grid_spec=pltpu.PrefetchScalarGridSpec(
            num_scalar_prefetch=1,
            grid=(n_hi * n_ctx, n_shard),
            in_specs=[
                pl.BlockSpec(
                    (1, 2, 1, 1, rows, both),
                    lambda i, j, z: (i // n_ctx, 0, i % n_ctx, j, 0, 0),
                ),
                block,
                block,
            ],
            out_specs=[block, block, pl.BlockSpec((rows, 128), lambda i, j, z: (i, 0))],
        ),
        out_shape=[shape, shape, jax.ShapeDtypeStruct((w_gate.shape[0], 128), jnp.float32)],
        compiler_params=pltpu.CompilerParams(vmem_limit_bytes=40 << 20),
        name="lay_in",
    )(rank.reshape(1), full, w_gate, w_up)


def lay_rows_kernel(full_ref, out_ref):
    out_ref[...] = full_ref[...].reshape(out_ref.shape).astype(jnp.float32)


def lay_rows(full):
    n_hi, _, n_ctx, rows, columns = full.shape
    n_part = n_hi * n_ctx
    return pl.pallas_call(
        lay_rows_kernel,
        grid=(2, n_part),
        in_specs=[
            pl.BlockSpec(
                (1, 1, 1, rows, columns), lambda i, j: (j // n_ctx, i, j % n_ctx, 0, 0)
            )
        ],
        out_specs=pl.BlockSpec((rows, columns), lambda i, j: (i * n_part + j, 0)),
        out_shape=jax.ShapeDtypeStruct((2 * n_part * rows, columns), jnp.float32),
        name="lay_rows",
    )(full)


def lay_heads_kernel(count, at_ref, *refs):
    mine, theirs = refs[:count], refs[count : 2 * count]
    wq_ref, wk_ref, wv_ref, dq_ref, dk_ref, dv_ref, d_out_ref, sums_ref = refs[2 * count :]
    q_cols, kv_cols = wq_ref.shape[1] // 2, wk_ref.shape[1] // 2
    out_rows = d_out_ref.shape[0] // 2
    rows = mine[0].shape[1]

    @pl.when(pl.program_id(0) == 0)
    def _():
        sums_ref[...] = jnp.zeros_like(sums_ref)

    for k in range(count):
        part = lax.rem(at_ref[0] - k + count, count)
        here = pl.ds(pl.multiple_of(part * rows, rows), rows)
        total = sums_ref[here, :]
        for core, full_ref in ((at_ref[1], mine[k]), (1 - at_ref[1], theirs[k])):
            full = full_ref[0].astype(jnp.float32)
            start = 0
            for weight_ref, grad_ref, columns in (
                (wq_ref, dq_ref, q_cols),
                (wk_ref, dk_ref, kv_cols),
                (wv_ref, dv_ref, kv_cols),
            ):
                grad = full[:, start : start + columns]
                span = pl.ds(pl.multiple_of(core * columns, 128), columns)
                grad_ref[here, span] = grad
                total += lane_sums(grad * weight_ref[here, span].astype(jnp.float32))
                start += columns
            d_out_ref[pl.ds(pl.multiple_of(core * out_rows, 128), out_rows), here] = full[
                :, start:
            ].T
        sums_ref[here, :] = total


def lay_heads(at, mine, theirs, w_query, key_weight, value_weight):
    n_part = len(mine)
    n_shard, rows, columns = mine[0].shape
    q_cols = w_query.shape[1] // n_shard
    kv_cols = key_weight.shape[1] // n_shard
    out_rows = 2 * columns - q_cols - 2 * kv_cols
    block = pl.BlockSpec((1, rows, columns), lambda j, at: (j, 0, 0))

    def spec(width):
        return pl.BlockSpec(
            (n_part * rows, width), lambda j, at: (0, lax.rem(at[2] - j + n_shard, n_shard))
        )

    return pl.pallas_call(
        partial(lay_heads_kernel, n_part),
        grid_spec=pltpu.PrefetchScalarGridSpec(
            num_scalar_prefetch=1,
            grid=(n_shard,),
            in_specs=[block] * (2 * n_part) + [spec(q_cols), spec(kv_cols), spec(kv_cols)],
            out_specs=[
                spec(q_cols),
                spec(kv_cols),
                spec(kv_cols),
                pl.BlockSpec((out_rows, n_part * rows), lambda j, at: (0, j)),
                pl.BlockSpec((n_part * rows, 128), lambda j, at: (0, 0)),
            ],
        ),
        out_shape=[
            jax.ShapeDtypeStruct(w_query.shape, jnp.float32),
            jax.ShapeDtypeStruct(key_weight.shape, jnp.float32),
            jax.ShapeDtypeStruct(value_weight.shape, jnp.float32),
            jax.ShapeDtypeStruct((out_rows, n_shard * n_part * rows), jnp.float32),
            jax.ShapeDtypeStruct((n_part * rows, 128), jnp.float32),
        ],
        compiler_params=pltpu.CompilerParams(vmem_limit_bytes=48 << 20),
        name="lay_heads",
    )(at, *mine, *theirs, w_query, key_weight, value_weight)


def exchange_ring(pieces, rank, count):
    def piece_for(k):
        return lax.dynamic_index_in_dim(pieces, (rank + k) % count, axis=0, keepdims=False)

    return [piece_for(0)] + [
        lax.ppermute(piece_for(k), "shard", [(i, (i + k) % count) for i in range(count)])
        for k in range(1, count)
    ]


def take_columns_kernel(at_ref, *refs):
    out_ref = refs[-1]
    start = 0
    for ref in refs[:-1]:
        columns = ref.shape[1]
        out_ref[0, :, start : start + columns] = ref[...]
        start += columns


def take_columns(at, n_part, n_shard, weights):
    rows = weights[0].shape[0] // n_part
    widths = [weight.shape[1] // (2 * n_shard) for weight in weights]
    return pl.pallas_call(
        take_columns_kernel,
        grid_spec=pltpu.PrefetchScalarGridSpec(
            num_scalar_prefetch=1,
            grid=(n_shard,),
            in_specs=[
                pl.BlockSpec((rows, width), lambda j, at: (at[0], 2 * j + at[1]))
                for width in widths
            ],
            out_specs=pl.BlockSpec((1, rows, sum(widths)), lambda j, at: (j, 0, 0)),
        ),
        out_shape=jax.ShapeDtypeStruct((n_shard, rows, sum(widths)), weights[0].dtype),
        name="take_columns",
    )(at, *weights)


def lay_order_kernel(at_ref, *refs):
    out_ref = refs[-1]
    count = len(refs) - 1
    rows = refs[0].shape[1]
    for k, ref in enumerate(refs[:-1]):
        owner = lax.rem(at_ref[0] - k + count, count)
        out_ref[pl.ds(pl.multiple_of(owner * rows, rows), rows), :] = ref[0]


def lay_order(at, pieces):
    n_shard, rows, columns = pieces[0].shape
    block = len(pieces) * rows
    return pl.pallas_call(
        lay_order_kernel,
        grid_spec=pltpu.PrefetchScalarGridSpec(
            num_scalar_prefetch=1,
            grid=(n_shard,),
            in_specs=[pl.BlockSpec((1, rows, columns), lambda j, at: (j, 0, 0))] * len(pieces),
            out_specs=pl.BlockSpec((block, columns), lambda j, at: (j, 0)),
        ),
        out_shape=jax.ShapeDtypeStruct((n_shard * block, columns), pieces[0].dtype),
        name="lay_order",
    )(at, *pieces)


def norm_kernel(z_ref, tokens_ref, gain_ref, out_ref):
    values = tokens_ref[0].astype(jnp.float32)
    out_ref[...] = (values * recip_rms(values) * gain_ref[...]).astype(jnp.bfloat16)


def norm_group(rank, gathered, gain):
    count, rows, width = gathered.shape
    return pl.pallas_call(
        norm_kernel,
        grid_spec=pltpu.PrefetchScalarGridSpec(
            num_scalar_prefetch=1,
            grid=(count,),
            in_specs=[
                pl.BlockSpec(
                    (1, rows, width), lambda k, z: (lax.rem(z[0] - k + count, count), 0, 0)
                ),
                pl.BlockSpec((1, width), lambda k, z: (0, 0)),
            ],
            out_specs=pl.BlockSpec((rows, width), lambda k, z: (k, 0)),
        ),
        out_shape=jax.ShapeDtypeStruct((count * rows, width), jnp.bfloat16),
        name="norm_group",
    )(rank.reshape(1), gathered, gain.reshape(1, width))


def turn(values, table):
    return pltpu.roll(values, HEAD_SIZE // 2, 1) * table


def project_kernel(n_part, q_cols, at_ref, *refs):
    tokens = refs[:n_part]
    pieces = refs[n_part : 2 * n_part]
    cos_ref, sin_ref, gain_q_ref, gain_k_ref, queries_ref, kv_ref, pre_ref, acc_ref = refs[
        2 * n_part :
    ]
    step = pl.program_id(0)
    columns = acc_ref.shape[1]
    kv_cols = (columns - q_cols) // 2
    total = sum(
        jnp.dot(block[...], piece[0], preferred_element_type=jnp.float32)
        for block, piece in zip(tokens, pieces)
    )
    add_sums(step, acc_ref, total)

    @pl.when(step == pl.num_programs(0) - 1)
    def _():
        rows = 64

        def body(chunk, carry):
            span = pl.ds(pl.multiple_of(chunk * rows, rows), rows)
            cosine, sine = cos_ref[span, :], sin_ref[span, :]
            for start in range(0, q_cols + kv_cols, HEAD_SIZE):
                values = acc_ref[span, start : start + HEAD_SIZE]
                pre_ref[span, start : start + HEAD_SIZE] = values
                gain = gain_q_ref[...] if start < q_cols else gain_k_ref[...]
                scaled = values * recip_rms(values) * gain
                turned = (scaled * cosine + turn(scaled, sine)).astype(jnp.bfloat16)
                if start < q_cols:
                    queries_ref[span, start : start + HEAD_SIZE] = turned
                else:
                    kv_ref[span, start - q_cols : start - q_cols + HEAD_SIZE] = turned
            kv_ref[span, kv_cols:] = acc_ref[span, q_cols + kv_cols :].astype(jnp.bfloat16)
            return carry

        lax.fori_loop(0, acc_ref.shape[0] // rows, body, 0)


def project(at, q_cols, tokens, pieces, cosine, sine, gain_q, gain_k):
    n_part = len(pieces)
    n_shard, slice_rows, columns = pieces[0].shape
    group, width = tokens.shape
    kv_cols = (columns - q_cols) // 2

    def token_spec(k):
        return pl.BlockSpec(
            (group, slice_rows),
            lambda j, at: (0, j * n_part + lax.rem(at[0] - k + n_part, n_part)),
        )

    def whole(shape):
        return pl.BlockSpec(shape, lambda j, at: (0, 0))

    head = (1, HEAD_SIZE)
    return pl.pallas_call(
        partial(project_kernel, n_part, q_cols),
        grid_spec=pltpu.PrefetchScalarGridSpec(
            num_scalar_prefetch=1,
            grid=(n_shard,),
            in_specs=[token_spec(k) for k in range(n_part)]
            + [pl.BlockSpec((1, slice_rows, columns), lambda j, at: (j, 0, 0))] * n_part
            + [whole(cosine.shape), whole(sine.shape), whole(head), whole(head)],
            out_specs=[
                whole((group, q_cols)),
                whole((group, 2 * kv_cols)),
                whole((group, q_cols + kv_cols)),
            ],
            scratch_shapes=[pltpu.VMEM((group, columns), jnp.float32)],
        ),
        out_shape=[
            jax.ShapeDtypeStruct((group, q_cols), jnp.bfloat16),
            jax.ShapeDtypeStruct((group, 2 * kv_cols), jnp.bfloat16),
            jax.ShapeDtypeStruct((group, q_cols + kv_cols), jnp.float32),
        ],
        compiler_params=pltpu.CompilerParams(vmem_limit_bytes=48 << 20),
        name="project",
    )(
        at,
        *([tokens] * n_part),
        *pieces,
        cosine,
        sine,
        gain_q.reshape(head),
        gain_k.reshape(head),
    )


def head_probs(start, q_pos_ref, k_pos_ref, query, keys):
    scores = [
        lax.dot_general(
            query, key, (((1,), (1,)), ((), ())), preferred_element_type=jnp.float32
        )
        for key in keys
    ]
    scores = jnp.concatenate(scores, axis=1) * HEAD_SIZE ** (-0.5)
    q_pos, k_pos = q_pos_ref[...], k_pos_ref[...]
    inside_q = (q_pos >= start) & (q_pos < start + PIC)
    inside_k = (k_pos >= start) & (k_pos < start + PIC)
    allowed = (k_pos <= q_pos) | (inside_q & inside_k)
    scores = jnp.where(allowed, scores, -1e30)
    powers = jnp.exp(scores - jnp.max(scores, axis=1, keepdims=True))
    return powers / jnp.sum(powers, axis=1, keepdims=True)


def attend_kernel(n_ctx, core, starts_ref, *refs):
    kv_refs = refs[:n_ctx]
    queries_ref, q_pos_ref, k_pos_ref, mixed_ref = refs[n_ctx:]
    block = queries_ref.shape
    tokens = block[1] * block[3]
    start = starts_ref[core, pl.program_id(0)]
    queries = queries_ref[...].reshape(tokens, block[4])
    kv = [ref[...].reshape(tokens, ref.shape[4]) for ref in kv_refs]
    kv_cols = kv[0].shape[1] // 2
    group_width = block[4] // kv_cols
    out = []
    for head in range(block[4] // HEAD_SIZE):
        key_start = head // group_width * HEAD_SIZE
        query = queries[:, head * HEAD_SIZE : (head + 1) * HEAD_SIZE]
        keys = [part[:, key_start : key_start + HEAD_SIZE] for part in kv]
        values = [
            part[:, kv_cols + key_start : kv_cols + key_start + HEAD_SIZE] for part in kv
        ]
        probs = head_probs(start, q_pos_ref, k_pos_ref, query, keys).astype(jnp.bfloat16)
        mixed = sum(
            jnp.dot(
                probs[:, i * tokens : (i + 1) * tokens], part, preferred_element_type=jnp.float32
            )
            for i, part in enumerate(values)
        )
        out.append(mixed.astype(jnp.bfloat16))
    mixed_ref[...] = jnp.concatenate(out, axis=1).reshape(mixed_ref.shape)


def sequence_view(values, count, micro, rows):
    return values.reshape(1, count, micro, rows, values.shape[-1])


def attend(core, starts, count, micro, rows, queries, kv_parts, q_pos, k_pos):
    n_ctx = len(kv_parts)

    def spec(columns):
        return pl.BlockSpec((1, count, 1, rows, columns), lambda m, s: (0, 0, m, 0, 0))

    view = partial(sequence_view, count=count, micro=micro, rows=rows)
    columns = queries.shape[1]
    mixed = pl.pallas_call(
        partial(attend_kernel, n_ctx, core),
        grid_spec=pltpu.PrefetchScalarGridSpec(
            num_scalar_prefetch=1,
            grid=(micro,),
            in_specs=[spec(kv_parts[0].shape[1])] * n_ctx
            + [
                spec(columns),
                pl.BlockSpec(q_pos.shape, lambda m, s: (0, 0)),
                pl.BlockSpec(k_pos.shape, lambda m, s: (0, 0)),
            ],
            out_specs=spec(columns),
        ),
        out_shape=jax.ShapeDtypeStruct(view(queries).shape, jnp.bfloat16),
        compiler_params=pltpu.CompilerParams(vmem_limit_bytes=48 << 20),
        name="attend",
    )(starts, *[view(part) for part in kv_parts], view(queries), q_pos, k_pos)
    return mixed.reshape(queries.shape)


def norm_turn_back(pre, d_turned, cosine, sine, gain):
    recip = recip_rms(pre)
    unit = pre * recip
    d_unit = d_turned * cosine + pltpu.roll(d_turned * sine, HEAD_SIZE // 2, 1)
    d_gain = jnp.sum(d_unit * unit, axis=0, keepdims=True)
    return norm_back(unit, recip, gain, d_unit), d_gain


def attend_back_kernel(n_ctx, core, starts_ref, *refs):
    kv_refs = refs[:n_ctx]
    queries_ref, pre_ref, d_mixed_ref, q_pos_ref, k_pos_ref, cos_ref, sin_ref, gain_ref = refs[
        n_ctx : n_ctx + 8
    ]
    d_queries_ref, sums_ref = refs[n_ctx + 8 : n_ctx + 10]
    d_kv_refs = refs[n_ctx + 10 :]
    block = queries_ref.shape
    tokens = block[1] * block[3]
    start = starts_ref[core, pl.program_id(0)]
    queries = queries_ref[...].reshape(tokens, block[4])
    d_mixed = d_mixed_ref[...].reshape(tokens, block[4])
    pre = pre_ref[...].reshape(tokens, pre_ref.shape[4])
    kv = [ref[...].reshape(tokens, ref.shape[4]) for ref in kv_refs]
    kv_cols = kv[0].shape[1] // 2
    group_width = block[4] // kv_cols
    scale = HEAD_SIZE ** (-0.5)
    down = (((0,), (0,)), ((), ()))
    across = (((1,), (1,)), ((), ()))
    f32 = jnp.float32
    d_queries, sums = [], 0.0
    d_keys, d_values = {}, {}
    for head in range(block[4] // HEAD_SIZE):
        key_start = head // group_width * HEAD_SIZE
        span = slice(head * HEAD_SIZE, (head + 1) * HEAD_SIZE)
        query, d_mix = queries[:, span], d_mixed[:, span]
        keys = [part[:, key_start : key_start + HEAD_SIZE] for part in kv]
        values = [
            part[:, kv_cols + key_start : kv_cols + key_start + HEAD_SIZE] for part in kv
        ]
        probs = head_probs(start, q_pos_ref, k_pos_ref, query, keys)
        d_probs = jnp.concatenate(
            [lax.dot_general(d_mix, part, across, preferred_element_type=f32) for part in values],
            axis=1,
        )
        row_dot = jnp.sum(probs * d_probs, axis=1, keepdims=True)
        d_scores = (probs * (d_probs - row_dot)).astype(jnp.bfloat16)
        probs_low = probs.astype(jnp.bfloat16)
        d_query = 0.0
        for i, key in enumerate(keys):
            piece = slice(i * tokens, (i + 1) * tokens)
            d_query += jnp.dot(d_scores[:, piece], key, preferred_element_type=f32)
            d_key = lax.dot_general(d_scores[:, piece], query, down, preferred_element_type=f32)
            d_value = lax.dot_general(
                probs_low[:, piece], d_mix, down, preferred_element_type=f32
            )
            at = (i, key_start)
            d_keys[at] = d_keys.get(at, 0.0) + d_key * scale
            d_values[at] = d_values.get(at, 0.0) + d_value
        d_pre, d_gain = norm_turn_back(
            pre[:, span],
            d_query * scale,
            cos_ref[...].reshape(tokens, HEAD_SIZE),
            sin_ref[...].reshape(tokens, HEAD_SIZE),
            gain_ref[...],
        )
        d_queries.append(d_pre.astype(jnp.bfloat16))
        sums += d_gain
    d_queries_ref[...] = jnp.concatenate(d_queries, axis=1).reshape(d_queries_ref.shape)
    for i, ref in enumerate(d_kv_refs):
        parts = [d_keys[at] for at in sorted(d_keys) if at[0] == i]
        parts += [d_values[at] for at in sorted(d_values) if at[0] == i]
        ref[...] = jnp.concatenate(parts, axis=1).astype(ref.dtype).reshape(ref.shape)
    add_sums(pl.program_id(0), sums_ref, jnp.broadcast_to(sums, sums_ref.shape))


def attend_back(
    core, starts, count, micro, rows, queries, pre, kv_parts, d_mixed, q_pos, k_pos, cosine, sine, gain
):
    n_ctx = len(kv_parts)
    view = partial(sequence_view, count=count, micro=micro, rows=rows)

    def spec(columns):
        return pl.BlockSpec((1, count, 1, rows, columns), lambda m, s: (0, 0, m, 0, 0))

    def whole(values):
        return pl.BlockSpec(values.shape, lambda m, s: (0, 0))

    columns, kv_columns = queries.shape[1], kv_parts[0].shape[1]
    gain = gain.reshape(1, HEAD_SIZE)
    view_shape = view(d_mixed).shape
    outs = pl.pallas_call(
        partial(attend_back_kernel, n_ctx, core),
        grid_spec=pltpu.PrefetchScalarGridSpec(
            num_scalar_prefetch=1,
            grid=(micro,),
            in_specs=[spec(kv_columns)] * n_ctx
            + [spec(columns), spec(pre.shape[1]), spec(columns)]
            + [whole(q_pos), whole(k_pos), spec(HEAD_SIZE), spec(HEAD_SIZE), whole(gain)],
            out_specs=[spec(columns), pl.BlockSpec((8, HEAD_SIZE), lambda m, s: (0, 0))]
            + [spec(kv_columns)] * n_ctx,
        ),
        out_shape=[
            jax.ShapeDtypeStruct(view_shape, jnp.bfloat16),
            jax.ShapeDtypeStruct((8, HEAD_SIZE), jnp.float32),
        ]
        + [
            jax.ShapeDtypeStruct(
                view_shape[:-1] + (kv_columns,), jnp.float32 if i == 0 else jnp.bfloat16
            )
            for i in range(n_ctx)
        ],
        compiler_params=pltpu.CompilerParams(vmem_limit_bytes=48 << 20),
        name="attend_back",
    )(
        starts,
        *[view(part) for part in kv_parts],
        view(queries),
        view(pre),
        view(d_mixed),
        q_pos,
        k_pos,
        view(cosine),
        view(sine),
        gain,
    )
    flat = [values.reshape(d_mixed.shape[0], -1) for values in outs[:1] + outs[2:]]
    return flat[0], outs[1][0], flat[1:]


def keys_back_kernel(n_got, q_cols, *refs):
    d_q_ref, own_ref = refs[:2]
    got_refs = refs[2 : 2 + n_got]
    pre_ref, cos_ref, sin_ref, gain_ref, out_ref, sums_ref = refs[2 + n_got :]
    total = own_ref[...]
    for ref in got_refs:
        total += ref[...].astype(jnp.float32)
    kv_cols = total.shape[1] // 2
    out_ref[:, :q_cols] = d_q_ref[...]
    out_ref[:, q_cols + kv_cols :] = total[:, kv_cols:].astype(jnp.bfloat16)
    sums = 0.0
    for start in range(0, kv_cols, HEAD_SIZE):
        span = slice(start, start + HEAD_SIZE)
        at = slice(q_cols + start, q_cols + start + HEAD_SIZE)
        d_pre, d_gain = norm_turn_back(
            pre_ref[:, at], total[:, span], cos_ref[...], sin_ref[...], gain_ref[...]
        )
        out_ref[:, at] = d_pre.astype(jnp.bfloat16)
        sums += d_gain
    sums_ref[...] = jnp.broadcast_to(sums, sums_ref.shape)


def keys_back(d_queries, own, got, pre, cosine, sine, gain):
    rows, q_cols = d_queries.shape
    out, sums = pl.pallas_call(
        partial(keys_back_kernel, len(got), q_cols),
        out_shape=[
            jax.ShapeDtypeStruct((rows, q_cols + own.shape[1]), jnp.bfloat16),
            jax.ShapeDtypeStruct((8, HEAD_SIZE), jnp.float32),
        ],
        name="keys_back",
    )(d_queries, own, *got, pre, cosine, sine, gain.reshape(1, HEAD_SIZE))
    return out, sums[0]


def head_gradients_kernel(count, at_ref, *refs):
    normed, branch = refs[: 2 * count], refs[2 * count : 4 * count]
    d_qkv, mixed = refs[4 * count : 4 * count + 2], refs[4 * count + 2 : 4 * count + 4]
    down = (((0,), (0,)), ((), ()))
    for k, out_ref in enumerate(refs[4 * count + 4 :]):
        split = d_qkv[0].shape[1]
        for columns, left, right in (
            (slice(0, split), normed, d_qkv),
            (slice(split, out_ref.shape[2]), branch, mixed),
        ):
            out_ref[0, :, columns] = sum(
                lax.dot_general(
                    left[core * count + k][...],
                    right[core][...],
                    down,
                    preferred_element_type=jnp.float32,
                )
                for core in range(2)
            ).astype(jnp.bfloat16)


def head_gradients(at, n_part, n_shard, normed, d_branch, d_qkv, mixed):
    rows, width = normed[0].shape
    slice_rows = width // (n_part * n_shard)
    columns = d_qkv[0].shape[1] + mixed[0].shape[1]

    def spec(k):
        return pl.BlockSpec(
            (rows, slice_rows),
            lambda j, at: (0, j * n_part + lax.rem(at[0] - k + n_part, n_part)),
        )

    def whole(values):
        return pl.BlockSpec(values.shape, lambda j, at: (0, 0))

    specs = [spec(k) for k in range(n_part)] * 2
    out = pl.BlockSpec((1, slice_rows, columns), lambda j, at: (j, 0, 0))
    return pl.pallas_call(
        partial(head_gradients_kernel, n_part),
        grid_spec=pltpu.PrefetchScalarGridSpec(
            num_scalar_prefetch=1,
            grid=(n_shard,),
            in_specs=specs + specs + [whole(values) for values in d_qkv + mixed],
            out_specs=[out] * n_part,
        ),
        out_shape=[jax.ShapeDtypeStruct((n_shard, slice_rows, columns), jnp.bfloat16)] * n_part,
        compiler_params=pltpu.CompilerParams(vmem_limit_bytes=48 << 20),
        name="head_gradients",
    )(
        at,
        *[normed[0]] * n_part,
        *[normed[1]] * n_part,
        *[d_branch[0]] * n_part,
        *[d_branch[1]] * n_part,
        *d_qkv,
        *mixed,
    )


def reorder_kernel(z_ref, in_ref, out_ref):
    out_ref[...] = in_ref[0]


def ring_order(rank, gathered):
    count, rows, width = gathered.shape
    return pl.pallas_call(
        reorder_kernel,
        grid_spec=pltpu.PrefetchScalarGridSpec(
            num_scalar_prefetch=1,
            grid=(count,),
            in_specs=[
                pl.BlockSpec(
                    (1, rows, width), lambda k, z: (lax.rem(z[0] - k + count, count), 0, 0)
                )
            ],
            out_specs=pl.BlockSpec((rows, width), lambda k, z: (k, 0)),
        ),
        out_shape=jax.ShapeDtypeStruct((count * rows, width), gathered.dtype),
        name="ring_order",
    )(rank.reshape(1), gathered)


def inner_kernel(ffn_ref, gate_ref, up_ref, d_inner_ref, inner_ref, d_gate_ref, d_up_ref):
    ffn = ffn_ref[...]
    gate_pre = jnp.dot(ffn, gate_ref[...], preferred_element_type=jnp.float32)
    up_pre = jnp.dot(ffn, up_ref[...], preferred_element_type=jnp.float32)
    d_inner = d_inner_ref[...]
    sigma = jax.nn.sigmoid(gate_pre)
    act_gate = gate_pre * sigma
    inner_ref[...] = (act_gate * up_pre).astype(jnp.bfloat16)
    d_gate = d_inner * up_pre * sigma * (1.0 + gate_pre * (1.0 - sigma))
    d_gate_ref[...] = d_gate.astype(jnp.bfloat16)
    d_up_ref[...] = (d_inner * act_gate).astype(jnp.bfloat16)


def inner_parts(ffn_in, w_in, d_inner):
    rows, width = ffn_in.shape
    ff = w_in.shape[1] // 2
    block = 256 if ff % 256 == 0 else 128
    steps = ff // block
    out = pl.BlockSpec((rows, block), lambda j: (0, j))
    shape = jax.ShapeDtypeStruct((rows, ff), jnp.bfloat16)
    return pl.pallas_call(
        inner_kernel,
        grid=(steps,),
        in_specs=[
            pl.BlockSpec((rows, width), lambda j: (0, 0)),
            pl.BlockSpec((width, block), lambda j: (0, j)),
            pl.BlockSpec((width, block), lambda j: (0, steps + j)),
            out,
        ],
        out_specs=[out, out, out],
        out_shape=[shape, shape, shape],
        compiler_params=pltpu.CompilerParams(vmem_limit_bytes=48 << 20),
        name="inner_parts",
    )(ffn_in, w_in, w_in, d_inner)


def grouped_shards(
    n_hi,
    n_shard,
    n_ctx,
    tokens,
    span_starts,
    cotangent,
    w_query,
    key_weight,
    value_weight,
    w_out,
    attn_gain,
    query_gain,
    key_gain,
    w_gate,
    w_up,
    w_down,
    ffn_gain,
):
    bf16 = jnp.bfloat16
    f32 = jnp.float32
    z = lax.axis_index("shard")
    x = lax.axis_index("ctx")
    c = lax.axis_index("core")
    part = lax.axis_index(("hi", "ctx"))
    n_part = n_hi * n_ctx
    micro, _, rows, width = tokens.shape
    own = micro * rows
    group = n_shard * own
    n_tp = 2 * n_shard
    kv_local = KEY_VALUE_HEADS // n_tp
    q_local = QUERY_HEADS // n_tp
    group_width = QUERY_HEADS // KEY_VALUE_HEADS
    q_cols = q_local * HEAD_SIZE
    kv_cols = kv_local * HEAD_SIZE
    ff = w_down.shape[0] // 2

    slice_rows = w_query.shape[0] // n_part
    plain = (((1,), (0,)), ((), ()))
    turned = (((1,), (1,)), ((), ()))

    def product(left, right, dims):
        return lax.dot_general(left, right, dims, preferred_element_type=f32)

    def exchange(pieces):
        return lax.all_to_all(pieces, "shard", 0, 0, tiled=True)

    def gather_plane(values):
        full = lax.all_gather(values, ("hi", "core", "ctx"), axis=0)
        return full.reshape((n_hi, 2, n_ctx) + values.shape)

    def send_blocks(mine):
        return [mine[k * own : (k + 1) * own] for k in range(n_shard)]

    own_tokens = tokens.reshape(own, width)
    own_cot = cotangent.reshape(own, width)
    at = jnp.stack([part, c, z])
    gathered = lax.all_gather(own_tokens, "shard", axis=0)
    pieces_qkv = take_columns(at, n_part, n_shard, (w_query, key_weight, value_weight))
    pieces_in = take_columns(at, n_part, n_shard, (w_gate, w_up))
    got_qkv = after(exchange(pieces_qkv), pieces_in)
    w_out_rows = lax.dynamic_slice_in_dim(w_out, c * q_cols, q_cols, axis=0)
    w_down_rows = lax.dynamic_slice_in_dim(w_down, c * ff, ff, axis=0)
    gain_sizes = (attn_gain.shape[0], query_gain.shape[0], key_gain.shape[0], ffn_gain.shape[0])
    gains = after(jnp.concatenate([attn_gain, query_gain, key_gain, ffn_gain]), got_qkv)
    gains = in_order(from_ring(gains, "shard", n_shard), z).astype(f32)
    starts = after(span_starts.reshape(micro), got_qkv)
    starts = jnp.stack([starts, swap(starts, "core")])
    ring_qkv = from_ring(got_qkv, ("hi", "ctx"), n_part)
    gathered = after(gathered, ring_qkv, gains, starts)
    ends = [0]
    for size in gain_sizes:
        ends.append(ends[-1] + size)
    gain_attn, gain_query, gain_key, gain_ffn = [
        gains[:, ends[i] : ends[i + 1]].reshape(-1) for i in range(4)
    ]

    blocks = jnp.arange(n_shard, dtype=jnp.int32)
    owners = (z - blocks) % n_shard

    def positions(ctx_rank):
        start = (owners * n_ctx + ctx_rank) * rows
        return (start[:, None] + jnp.arange(rows, dtype=jnp.int32)[None, :]).reshape(-1)

    query_pos = positions(x)
    key_pos = jnp.concatenate([positions((x - k) % n_ctx) for k in range(n_ctx)])
    cosine, sine = (table[:, 0, :] for table in spin_tables(query_pos))
    sine = jnp.where(jnp.arange(HEAD_SIZE) < HEAD_SIZE // 2, -1.0, 1.0) * sine

    def by_row(table):
        table = table.reshape(n_shard, 1, rows, HEAD_SIZE)
        return jnp.broadcast_to(table, (n_shard, micro, rows, HEAD_SIZE)).reshape(group, HEAD_SIZE)

    cosine, sine = by_row(cosine), by_row(sine)
    query_pos = query_pos[:, None]
    key_pos = key_pos[None, :]
    order = (n_shard, micro, rows)

    normed_mine = norm_group(z, gathered, gain_attn)
    normed_theirs = swap(normed_mine, "core")
    got_in = exchange_ring(after(pieces_in, gathered), z, n_shard)
    cot_all = lax.all_gather(after(own_cot, gathered), "shard", axis=0)
    turns = (cosine, sine, gain_query, gain_key)
    q_mine, kv_mine, pre_mine = project(at, q_cols, normed_mine, ring_qkv, *turns)
    kv_mine_parts = from_ring(kv_mine, "ctx", n_ctx)
    q_theirs, kv_theirs, pre_theirs = project(
        at, q_cols, after(normed_theirs, kv_mine), ring_qkv, *turns
    )
    kv_theirs_parts = from_ring(kv_theirs, "ctx", n_ctx)
    w_qkv = lay_order(at, after(ring_qkv, kv_theirs))
    mixed_mine = attend(
        0, starts, *order, after(q_mine, w_qkv), kv_mine_parts, query_pos, key_pos
    )
    mixed_theirs = attend(
        1, starts, *order, after(q_theirs, mixed_mine), kv_theirs_parts, query_pos, key_pos
    )
    got_in = in_order(after(got_in, mixed_theirs), z)
    w_in = lax.all_gather(after(got_in, cot_all), ("hi", "ctx"), axis=1, tiled=True)
    w_in = w_in.reshape(width, -1)

    def core_sum(mine, theirs, right, dims):
        sent = product(theirs, right, dims).astype(bf16)
        kept = product(after(mine, sent), right, dims)
        return kept + after(swap(sent, "core"), kept).astype(f32)

    branch = core_sum(mixed_mine, mixed_theirs, w_out_rows, plain)
    hidden_in = own_tokens.astype(f32)
    branch_sent = send_blocks(branch)
    cot_mine = ring_order(z, after(cot_all, branch))
    cot_theirs = swap(cot_mine, "core")
    branch_terms = send_terms(branch_sent, "shard", n_shard)
    middle = hidden_in + sum_terms(after(branch_terms, w_in, cot_mine))

    recip_m = recip_rms(middle)
    unit_m = middle * recip_m
    ffn_own = (unit_m * gain_ffn).astype(bf16)
    ffn_ring = from_ring(ffn_own, "shard", n_shard)
    d_inner_mine = product(after(cot_mine, ffn_own), w_down_rows, turned)
    d_inner_theirs = product(after(cot_theirs, d_inner_mine), w_down_rows, turned)
    ffn_mine = jnp.concatenate(after(ffn_ring, d_inner_theirs), axis=0)
    ffn_theirs = swap(ffn_mine, "core")
    inner_mine, d_gate_mine, d_up_mine = inner_parts(ffn_mine, w_in, d_inner_mine)
    inner_theirs, d_gate_theirs, d_up_theirs = inner_parts(
        after(ffn_theirs, inner_mine), w_in, d_inner_theirs
    )
    d_pre_mine = jnp.concatenate([d_gate_mine, d_up_mine], axis=1)
    d_pre_theirs = jnp.concatenate([d_gate_theirs, d_up_theirs], axis=1)
    d_ffn = core_sum(d_pre_mine, d_pre_theirs, w_in, turned)
    d_ffn_sent = send_blocks(d_ffn)
    inner_act = jnp.concatenate([after(inner_mine, d_ffn), inner_theirs], axis=0)
    cot_rows = jnp.concatenate([cot_mine, cot_theirs], axis=0)
    grad_rows = over_rows(inner_act, cot_rows).astype(bf16)
    part_down = lax.psum_scatter(grad_rows, ("hi", "ctx"), scatter_dimension=0, tiled=True)
    ffn_in = jnp.concatenate([after(ffn_mine, grad_rows), ffn_theirs], axis=0)
    d_pre = jnp.concatenate([after(d_pre_mine, grad_rows), d_pre_theirs], axis=0)
    grad_in = over_rows(ffn_in, d_pre).astype(bf16).reshape(n_shard, n_part * slice_rows, -1)
    d_ffn_in = sum_terms(after(send_terms(d_ffn_sent, "shard", n_shard), grad_in))
    d_middle = own_cot.astype(f32) + norm_back(unit_m, recip_m, gain_ffn, d_ffn_in)

    d_branch_own = d_middle.astype(bf16)
    branch_ring = from_ring(d_branch_own, "shard", n_shard)
    part_in = lax.psum_scatter(
        after(grad_in, part_down, d_branch_own), ("hi", "ctx"), scatter_dimension=1, tiled=True
    )
    branch_mine = jnp.concatenate(after(branch_ring, part_down), axis=0)
    branch_theirs = swap(branch_mine, "core")
    d_mixed_mine = product(branch_mine, w_out_rows, turned).astype(bf16)
    tables = (query_pos, key_pos, cosine, sine, gain_query)
    d_q_mine, gain_q_mine, d_kv_mine = attend_back(
        0, starts, *order, q_mine, pre_mine, kv_mine_parts, d_mixed_mine, *tables
    )
    d_mixed_theirs = product(after(branch_theirs, d_q_mine), w_out_rows, turned).astype(bf16)
    d_q_theirs, gain_q_theirs, d_kv_theirs = attend_back(
        1, starts, *order, q_theirs, pre_theirs, kv_theirs_parts, d_mixed_theirs, *tables
    )
    part_in = after(part_in, d_q_theirs)

    def keys_gradient(d_queries, d_kv, pre, *others):
        got = [
            lax.ppermute(d_kv[n_ctx - k], "ctx", [(i, (i + k) % n_ctx) for i in range(n_ctx)])
            for k in range(1, n_ctx)
        ]
        got = [after(values, *others) for values in got]
        return keys_back(d_queries, d_kv[0], got, pre, cosine, sine, gain_key)

    d_qkv_mine, gain_k_mine = keys_gradient(d_q_mine, d_kv_mine, pre_mine, d_q_theirs)
    d_qkv_theirs, gain_k_theirs = keys_gradient(
        d_q_theirs, d_kv_theirs, pre_theirs, d_qkv_mine
    )
    sent_in = exchange_ring(part_in, z, n_shard)
    full_rows = gather_plane(after(part_down, part_in))
    d_in = core_sum(d_qkv_mine, after(d_qkv_theirs, part_in), w_qkv, turned)
    sent_in = jnp.stack(after(sent_in, d_in))
    sent = head_gradients(
        at,
        n_part,
        n_shard,
        (normed_mine, normed_theirs),
        (branch_mine, branch_theirs),
        (after(d_qkv_mine, d_in, sent_in), d_qkv_theirs),
        (mixed_mine, mixed_theirs),
    )
    part_heads = send_terms(sent, ("hi", "ctx"), n_part)
    full_in = gather_plane(after(sent_in, full_rows))
    head_gains = jnp.stack([gain_q_mine + gain_q_theirs, gain_k_mine + gain_k_theirs])
    head_gains = sum(after(from_ring(head_gains, "core", 2), sent))
    part_heads = sum_terms(after(part_heads, head_gains)).astype(bf16)
    qkv_cols = q_cols + 2 * kv_cols
    ring_heads = exchange_ring(part_heads[..., :qkv_cols], z, n_shard)
    head_gains = sum(after(from_ring(head_gains, "hi", n_hi), part_heads))
    d_normed = send_terms(send_blocks(after(d_in, ring_heads)), "shard", n_shard)
    ring_heads = after(ring_heads, head_gains)
    part_heads = jnp.concatenate([jnp.stack(ring_heads), part_heads[..., qkv_cols:]], axis=-1)
    mine_heads = from_ring(part_heads, ("hi", "ctx"), n_part)
    result = core_sum(after(inner_mine, part_heads), inner_theirs, w_down_rows, plain)
    grad_down = lay_rows(after(full_rows, result))
    head_gains = sum(after(from_ring(head_gains, "ctx", n_ctx), grad_down))
    d_normed = sum_terms(after(d_normed, grad_down))
    recip_h = recip_rms(hidden_in)
    unit_h = hidden_in * recip_h
    input_grad = d_middle + norm_back(unit_h, recip_h, gain_attn, d_normed)
    result = send_terms(send_blocks(after(result, input_grad)), "shard", n_shard)
    mine_heads = after(mine_heads, head_gains, input_grad)
    theirs_heads = [swap(values, "core") for values in mine_heads]
    head_gains = sum(from_ring(after(head_gains, mine_heads), "shard", n_shard))
    head_size = query_gain.shape[0]
    head_gains = lax.dynamic_slice_in_dim(head_gains, z * head_size, head_size, axis=1)
    grad_query, grad_key, grad_value, grad_out, attn_sums = lay_heads(
        at, mine_heads, theirs_heads, w_query, key_weight, value_weight
    )
    grad_gate, grad_up, ffn_sums = lay_in(z, after(full_in, grad_query), w_gate, w_up)
    result = (middle + sum_terms(after(result, grad_gate))).astype(bf16)
    grad_ffn_gain = jnp.sum(ffn_sums, axis=1) / ffn_gain.astype(f32)
    grad_attn_gain = jnp.sum(attn_sums, axis=1) / attn_gain.astype(f32)

    return (
        result.reshape(tokens.shape),
        input_grad.reshape(tokens.shape),
        grad_query,
        grad_key,
        grad_value,
        grad_out,
        grad_attn_gain,
        head_gains[0],
        head_gains[1],
        grad_gate,
        grad_up,
        grad_down,
        grad_ffn_gain,
    )


def solution(mesh):
    n_rep, n_shard, n_ctx = (mesh.shape[name] for name in ("rep", "shard", "ctx"))
    if n_rep % 2 == 0 and KEY_VALUE_HEADS % (2 * n_shard) == 0:
        mesh = Mesh(
            mesh.devices.reshape(n_rep // 2, 2, n_shard, n_ctx), ("hi", "core", "shard", "ctx")
        )
        rep = ("hi", "core")
        body = partial(grouped_shards, n_rep // 2, n_shard, n_ctx)
    else:
        rep = "rep"
        body = shards_general
    in_specs = (
        P(None, rep, ("shard", "ctx"), None),
        P(None, rep),
        P(None, rep, ("shard", "ctx"), None),
        P("shard", None),
        P("shard", None),
        P("shard", None),
        P("shard", None),
        P("shard"),
        P("shard"),
        P("shard"),
        P("shard", None),
        P("shard", None),
        P("shard", None),
        P("shard"),
    )
    out_specs = (
        P(None, rep, ("shard", "ctx"), None),
        P(None, rep, ("shard", "ctx"), None),
        P("shard", None),
        P("shard", None),
        P("shard", None),
        P("shard", None),
        P("shard"),
        P("shard"),
        P("shard"),
        P("shard", None),
        P("shard", None),
        P("shard", None),
        P("shard"),
    )
    return jax.shard_map(body, mesh=mesh, in_specs=in_specs, out_specs=out_specs, check_vma=False)
```

```python
from functools import partial

import jax
import jax.numpy as jnp
from jax import lax
from jax.experimental import pallas as pl
from jax.experimental.pallas import tpu as pltpu
from jax.sharding import Mesh
from jax.sharding import PartitionSpec as P

QUERY_HEADS = 16
KEY_VALUE_HEADS = 8
HEAD_SIZE = 128
PIC = 256


EPSILON = 1e-06
THETA = 1000000.0


def apply_rotation(values):
    half_width = values.shape[-1] // 2
    return jnp.concatenate([-values[..., half_width:], values[..., :half_width]], axis=-1)


def rotate_back(values):
    half_width = values.shape[-1] // 2
    return jnp.concatenate([values[..., half_width:], -values[..., :half_width]], axis=-1)


def spin_tables(positions):
    inverse = THETA ** (-jnp.arange(HEAD_SIZE // 2, dtype=jnp.float32) * 2.0 / HEAD_SIZE)
    angles = positions.astype(jnp.float32)[:, None] * inverse[None, :]
    cosine_table = jnp.concatenate([jnp.cos(angles), jnp.cos(angles)], axis=-1)[:, None, :]
    sine_values = jnp.concatenate([jnp.sin(angles), jnp.sin(angles)], axis=-1)[:, None, :]
    return (cosine_table, sine_values)


def recip_rms(values):
    return lax.rsqrt(jnp.mean(values * values, axis=-1, keepdims=True) + EPSILON)


def norm_back(unit, recip, gain, d_normed):
    d_unit = d_normed * gain
    return recip * (d_unit - unit * jnp.mean(d_unit * unit, axis=-1, keepdims=True))


def over_rows(left, right):
    return lax.dot_general(
        left, right, (((0,), (0,)), ((), ())), preferred_element_type=jnp.float32
    )


def compared_to(left, right):
    return lax.dot_general(
        left, right, (((1,), (1,)), ((), ())), preferred_element_type=jnp.float32
    )


def attention_set(w_query, key_weight, value_weight, w_out, attn_gain, query_gain, key_gain):
    return (
        lax.all_gather(w_query, "shard", axis=0, tiled=True),
        lax.all_gather(key_weight, "shard", axis=0, tiled=True),
        lax.all_gather(value_weight, "shard", axis=0, tiled=True),
        lax.all_gather(w_out, "shard", axis=0, tiled=True),
        lax.all_gather(attn_gain, "shard", axis=0, tiled=True),
        lax.all_gather(query_gain, "shard", axis=0, tiled=True),
        lax.all_gather(key_gain, "shard", axis=0, tiled=True),
    )


def feedforward_set(w_gate, w_up, w_down, ffn_gain):
    return (
        lax.all_gather(w_gate, "shard", axis=0, tiled=True),
        lax.all_gather(w_up, "shard", axis=0, tiled=True),
        lax.all_gather(w_down, "shard", axis=0, tiled=True),
        lax.all_gather(ffn_gain, "shard", axis=0, tiled=True),
    )


def masked_scores(allowed, q_head, k_head):
    scores = jnp.einsum(
        "tgd,sd->gts", q_head, k_head, preferred_element_type=jnp.float32
    ) * HEAD_SIZE ** (-0.5)
    return jnp.where(allowed, scores, -1e30)


def head_forward(allowed, pieces):
    q_head, k_head, v_head = pieces
    scores = masked_scores(allowed, q_head, k_head)
    highest = jnp.max(scores, axis=-1, keepdims=True)
    log_total = highest + jnp.log(jnp.sum(jnp.exp(scores - highest), axis=-1, keepdims=True))
    probs_low = jnp.exp(scores - log_total).astype(jnp.bfloat16)
    mixed = jnp.einsum("gts,sd->tgd", probs_low, v_head, preferred_element_type=jnp.float32)
    return (mixed, log_total)


def head_backward(allowed, pieces):
    q_head, k_head, v_head, d_mix_head, log_total = pieces
    probs = jnp.exp(masked_scores(allowed, q_head, k_head) - log_total)
    probs_low = probs.astype(jnp.bfloat16)
    d_probs = jnp.einsum("tgd,sd->gts", d_mix_head, v_head, preferred_element_type=jnp.float32)
    d_values = jnp.einsum("gts,tgd->sd", probs_low, d_mix_head, preferred_element_type=jnp.float32)
    row_dot = jnp.sum(probs * d_probs, axis=-1, keepdims=True)
    d_scores = (probs * (d_probs - row_dot)).astype(jnp.bfloat16)
    d_queries = jnp.einsum(
        "gts,sd->tgd", d_scores, k_head, preferred_element_type=jnp.float32
    ) * HEAD_SIZE ** (-0.5)
    d_keys = jnp.einsum(
        "gts,tgd->sd", d_scores, q_head, preferred_element_type=jnp.float32
    ) * HEAD_SIZE ** (-0.5)
    return (d_queries, d_keys, d_values)


def shards_general(
    tokens,
    span_starts,
    cotangent,
    w_query,
    key_weight,
    value_weight,
    w_out,
    attn_gain,
    query_gain,
    key_gain,
    w_gate,
    w_up,
    w_down,
    ffn_gain,
):
    seq_count = lax.axis_size(("shard", "ctx"))
    seq_rank = lax.axis_index(("shard", "ctx"))
    token_rows = tokens.shape[2]
    token_length = token_rows * seq_count
    group_width = QUERY_HEADS // KEY_VALUE_HEADS
    local_pos = seq_rank * token_rows + jnp.arange(token_rows, dtype=jnp.int32)
    key_pos = jnp.arange(token_length, dtype=jnp.int32)
    cosine_table, sine_values = spin_tables(local_pos)
    cos_keys = cosine_table[:, 0, :][None]
    sin_keys = sine_values[:, 0, :][None]
    out_list = []
    grad_list = []
    stored = []
    totals = None
    for micro_index in range(tokens.shape[0]):
        span_start = span_starts[micro_index, 0]
        inside_q = (local_pos >= span_start) & (local_pos < span_start + PIC)
        inside_k = (key_pos >= span_start) & (key_pos < span_start + PIC)
        allowed = (key_pos[None, :] <= local_pos[:, None]) | inside_q[:, None] & inside_k[None, :]
        hidden_in = tokens[micro_index, 0].astype(jnp.float32)
        full_query, full_key, full_value, complete_output, gain_attn, gain_query, gain_key = (
            attention_set(w_query, key_weight, value_weight, w_out, attn_gain, query_gain, key_gain)
        )
        gain_attn = gain_attn.astype(jnp.float32)
        gain_query = gain_query.astype(jnp.float32)
        gain_key = gain_key.astype(jnp.float32)
        recip_h = recip_rms(hidden_in)
        unit_h = hidden_in * recip_h
        normalized_rows = (unit_h * gain_attn).astype(jnp.bfloat16)
        q_pre = jnp.dot(normalized_rows, full_query, preferred_element_type=jnp.float32).reshape(
            token_rows, QUERY_HEADS, HEAD_SIZE
        )
        key_before_rotation = jnp.transpose(
            jnp.dot(normalized_rows, full_key, preferred_element_type=jnp.float32).reshape(
                token_rows, KEY_VALUE_HEADS, HEAD_SIZE
            ),
            (1, 0, 2),
        )
        value_local = jnp.transpose(
            jnp.dot(normalized_rows, full_value, preferred_element_type=jnp.float32)
            .astype(jnp.bfloat16)
            .reshape(token_rows, KEY_VALUE_HEADS, HEAD_SIZE),
            (1, 0, 2),
        )
        recip_q = recip_rms(q_pre)
        unit_query = q_pre * recip_q
        recip_k = recip_rms(key_before_rotation)
        unit_k = key_before_rotation * recip_k
        scaled_q = unit_query * gain_query
        scaled_k = unit_k * gain_key
        query_rows = jnp.transpose(
            (scaled_q * cosine_table + apply_rotation(scaled_q) * sine_values)
            .astype(jnp.bfloat16)
            .reshape(token_rows, KEY_VALUE_HEADS, group_width, HEAD_SIZE),
            (1, 0, 2, 3),
        )
        key_local = (scaled_k * cos_keys + apply_rotation(scaled_k) * sin_keys).astype(jnp.bfloat16)
        key_rows, value_matrix = (
            lax.all_gather(key_local, ("shard", "ctx"), axis=1, tiled=True),
            lax.all_gather(value_local, ("shard", "ctx"), axis=1, tiled=True),
        )
        mixed_split, log_total = lax.map(
            partial(head_forward, allowed), (query_rows, key_rows, value_matrix)
        )
        mixed_heads = (
            jnp.transpose(mixed_split, (1, 0, 2, 3))
            .reshape(token_rows, QUERY_HEADS * HEAD_SIZE)
            .astype(jnp.bfloat16)
        )
        middle = hidden_in + jnp.dot(
            mixed_heads, complete_output, preferred_element_type=jnp.float32
        )
        full_gate, full_up, full_down, gain_ffn = feedforward_set(w_gate, w_up, w_down, ffn_gain)
        gain_ffn = gain_ffn.astype(jnp.float32)
        recip_m = recip_rms(middle)
        unit_m = middle * recip_m
        ffn_in = (unit_m * gain_ffn).astype(jnp.bfloat16)
        gate_pre = jnp.dot(ffn_in, full_gate, preferred_element_type=jnp.float32)
        up_pre = jnp.dot(ffn_in, full_up, preferred_element_type=jnp.float32)
        sigma = jax.nn.sigmoid(gate_pre)
        act_gate = gate_pre * sigma
        inner_act = (act_gate * up_pre).astype(jnp.bfloat16)
        result = middle + jnp.dot(inner_act, full_down, preferred_element_type=jnp.float32)
        out_list.append(result.astype(jnp.bfloat16))
        cot_rows = cotangent[micro_index, 0]
        cot_float = cot_rows.astype(jnp.float32)
        d_inner = compared_to(cot_rows, full_down)
        d_gate = (d_inner * up_pre * sigma * (1.0 + gate_pre * (1.0 - sigma))).astype(jnp.bfloat16)
        d_up = (d_inner * act_gate).astype(jnp.bfloat16)
        d_ffn_in = compared_to(d_gate, full_gate) + compared_to(d_up, full_up)
        ffn_gain_part = jnp.sum(d_ffn_in * unit_m, axis=0)
        d_middle = cot_float + norm_back(unit_m, recip_m, gain_ffn, d_ffn_in)
        branch_gradient = d_middle.astype(jnp.bfloat16)
        d_mixed = jnp.transpose(
            compared_to(branch_gradient, complete_output)
            .astype(jnp.bfloat16)
            .reshape(token_rows, KEY_VALUE_HEADS, group_width, HEAD_SIZE),
            (1, 0, 2, 3),
        )
        d_split_q, d_keys, d_values = lax.map(
            partial(head_backward, allowed),
            (query_rows, key_rows, value_matrix, d_mixed, log_total),
        )
        d_queries = jnp.transpose(d_split_q, (1, 0, 2, 3)).reshape(
            token_rows, QUERY_HEADS, HEAD_SIZE
        )
        d_key_local, d_value_local = (
            lax.psum_scatter(
                d_keys.astype(jnp.bfloat16), ("shard", "ctx"), scatter_dimension=1, tiled=True
            ).astype(jnp.float32),
            lax.psum_scatter(
                d_values.astype(jnp.bfloat16), ("shard", "ctx"), scatter_dimension=1, tiled=True
            ).astype(jnp.float32),
        )
        d_unit_q = d_queries * cosine_table + rotate_back(d_queries * sine_values)
        d_unit_k = d_key_local * cos_keys + rotate_back(d_key_local * sin_keys)
        query_gain_part = jnp.sum(d_unit_q * unit_query, axis=(0, 1))
        key_gain_part = jnp.sum(d_unit_k * unit_k, axis=(0, 1))
        d_q_pre = (
            norm_back(unit_query, recip_q, gain_query, d_unit_q)
            .astype(jnp.bfloat16)
            .reshape(token_rows, QUERY_HEADS * HEAD_SIZE)
        )
        d_k_pre = jnp.transpose(
            norm_back(unit_k, recip_k, gain_key, d_unit_k).astype(jnp.bfloat16), (1, 0, 2)
        ).reshape(token_rows, KEY_VALUE_HEADS * HEAD_SIZE)
        d_v_pre = jnp.transpose(d_value_local.astype(jnp.bfloat16), (1, 0, 2)).reshape(
            token_rows, KEY_VALUE_HEADS * HEAD_SIZE
        )
        d_normed = (
            compared_to(d_q_pre, full_query)
            + compared_to(d_k_pre, full_key)
            + compared_to(d_v_pre, full_value)
        )
        attn_gain_part = jnp.sum(d_normed * unit_h, axis=0)
        grad_list.append(d_middle + norm_back(unit_h, recip_h, gain_attn, d_normed))
        stored.append(
            (
                normalized_rows,
                d_q_pre,
                d_k_pre,
                d_v_pre,
                mixed_heads,
                branch_gradient,
                ffn_in,
                d_gate,
                d_up,
                inner_act,
                cot_rows,
            )
        )
        parts = (attn_gain_part, query_gain_part, key_gain_part, ffn_gain_part)
        if totals is None:
            totals = parts
        else:
            totals = tuple((older + newer for older, newer in zip(totals, parts)))
    joined = [
        jnp.concatenate([saved_set[member] for saved_set in stored], axis=0) for member in range(11)
    ]
    (
        normed_all,
        dq_all,
        dk_all,
        dv_all,
        mixed_all,
        branch_all,
        ffn_all,
        gate_all,
        up_all,
        inner_all,
        cot_all,
    ) = joined
    totals = (
        lax.psum_scatter(
            over_rows(normed_all, dq_all).astype(jnp.bfloat16),
            "shard",
            scatter_dimension=0,
            tiled=True,
        ).astype(jnp.float32),
        lax.psum_scatter(
            over_rows(normed_all, dk_all).astype(jnp.bfloat16),
            "shard",
            scatter_dimension=0,
            tiled=True,
        ).astype(jnp.float32),
        lax.psum_scatter(
            over_rows(normed_all, dv_all).astype(jnp.bfloat16),
            "shard",
            scatter_dimension=0,
            tiled=True,
        ).astype(jnp.float32),
        lax.psum_scatter(
            over_rows(mixed_all, branch_all).astype(jnp.bfloat16),
            "shard",
            scatter_dimension=0,
            tiled=True,
        ).astype(jnp.float32),
        lax.psum_scatter(
            totals[0].astype(jnp.bfloat16), "shard", scatter_dimension=0, tiled=True
        ).astype(jnp.float32),
        lax.psum_scatter(
            totals[1].astype(jnp.bfloat16), "shard", scatter_dimension=0, tiled=True
        ).astype(jnp.float32),
        lax.psum_scatter(
            totals[2].astype(jnp.bfloat16), "shard", scatter_dimension=0, tiled=True
        ).astype(jnp.float32),
        lax.psum_scatter(
            over_rows(ffn_all, gate_all).astype(jnp.bfloat16),
            "shard",
            scatter_dimension=0,
            tiled=True,
        ).astype(jnp.float32),
        lax.psum_scatter(
            over_rows(ffn_all, up_all).astype(jnp.bfloat16),
            "shard",
            scatter_dimension=0,
            tiled=True,
        ).astype(jnp.float32),
        lax.psum_scatter(
            over_rows(inner_all, cot_all).astype(jnp.bfloat16),
            "shard",
            scatter_dimension=0,
            tiled=True,
        ).astype(jnp.float32),
        lax.psum_scatter(
            totals[3].astype(jnp.bfloat16), "shard", scatter_dimension=0, tiled=True
        ).astype(jnp.float32),
    )
    summed = (
        lax.psum(totals[0].astype(jnp.bfloat16), ("rep", "ctx")).astype(jnp.float32),
        lax.psum(totals[1].astype(jnp.bfloat16), ("rep", "ctx")).astype(jnp.float32),
        lax.psum(totals[2].astype(jnp.bfloat16), ("rep", "ctx")).astype(jnp.float32),
        lax.psum(totals[3].astype(jnp.bfloat16), ("rep", "ctx")).astype(jnp.float32),
        lax.psum(totals[4].astype(jnp.bfloat16), ("rep", "ctx")).astype(jnp.float32),
        lax.psum(totals[5].astype(jnp.bfloat16), ("rep", "ctx")).astype(jnp.float32),
        lax.psum(totals[6].astype(jnp.bfloat16), ("rep", "ctx")).astype(jnp.float32),
        lax.psum(totals[7].astype(jnp.bfloat16), ("rep", "ctx")).astype(jnp.float32),
        lax.psum(totals[8].astype(jnp.bfloat16), ("rep", "ctx")).astype(jnp.float32),
        lax.psum(totals[9].astype(jnp.bfloat16), ("rep", "ctx")).astype(jnp.float32),
        lax.psum(totals[10].astype(jnp.bfloat16), ("rep", "ctx")).astype(jnp.float32),
    )
    output = jnp.stack(out_list)[:, None]
    input_grad = jnp.stack(grad_list)[:, None]
    return (
        output,
        input_grad,
        summed[0],
        summed[1],
        summed[2],
        summed[3],
        summed[4],
        summed[5],
        summed[6],
        summed[7],
        summed[8],
        summed[9],
        summed[10],
    )


def from_ring(block, axis, count):
    return [block] + [
        lax.ppermute(block, axis, [(i, (i + k) % count) for i in range(count)])
        for k in range(1, count)
    ]


def send_terms(pieces, axis, count):
    return [pieces[0]] + [
        lax.ppermute(
            pieces[count - k].astype(jnp.bfloat16),
            axis,
            [(i, (i + k) % count) for i in range(count)],
        )
        for k in range(1, count)
    ]


def sum_terms(terms):
    return sum(term.astype(jnp.float32) for term in terms)


def swap(values, axis):
    return lax.ppermute(values, axis, [(0, 1), (1, 0)])


def after(value, *others):
    return lax.optimization_barrier((value,) + others)[0] if others else value


def in_order(blocks, rank):
    count = len(blocks)
    twice = jnp.stack(blocks[::-1] + blocks[:0:-1])
    return lax.dynamic_slice_in_dim(twice, count - 1 - rank, count, axis=0)


def lane_sums(values):
    return sum(
        values[:, start : start + 128] for start in range(0, values.shape[1], 128)
    )


def add_sums(step, sums_ref, values):
    @pl.when(step == 0)
    def _():
        sums_ref[...] = values

    @pl.when(step > 0)
    def _():
        sums_ref[...] += values


def lay_in_kernel(full_ref, gate_ref, up_ref, d_gate_ref, d_up_ref, sums_ref):
    columns = gate_ref.shape[1] // 2
    total = None
    for core in range(2):
        full = full_ref[0, core, 0, 0].astype(jnp.float32)
        span = slice(core * columns, (core + 1) * columns)
        d_gate = full[:, :columns]
        d_up = full[:, columns:]
        d_gate_ref[:, span] = d_gate
        d_up_ref[:, span] = d_up
        both = d_gate * gate_ref[:, span].astype(jnp.float32)
        both = lane_sums(both + d_up * up_ref[:, span].astype(jnp.float32))
        total = both if total is None else total + both
    add_sums(pl.program_id(1), sums_ref, total)


def lay_in(full, w_gate, w_up):
    n_hi, _, n_ctx, n_shard, rows, both = full.shape
    shape = jax.ShapeDtypeStruct(w_gate.shape, jnp.float32)
    block = pl.BlockSpec((rows, both), lambda i, j: (i, j))
    return pl.pallas_call(
        lay_in_kernel,
        grid=(n_hi * n_ctx, n_shard),
        in_specs=[
            pl.BlockSpec(
                (1, 2, 1, 1, rows, both), lambda i, j: (i // n_ctx, 0, i % n_ctx, j, 0, 0)
            ),
            block,
            block,
        ],
        out_specs=[block, block, pl.BlockSpec((rows, 128), lambda i, j: (i, 0))],
        out_shape=[shape, shape, jax.ShapeDtypeStruct((w_gate.shape[0], 128), jnp.float32)],
        compiler_params=pltpu.CompilerParams(vmem_limit_bytes=60 << 20),
        name="lay_in",
    )(full, w_gate, w_up)


def lay_rows_kernel(full_ref, out_ref):
    n_hi, _, n_ctx, _, rows, columns = full_ref.shape
    for hi in range(n_hi):
        for core in range(2):
            for ctx in range(n_ctx):
                start = (hi * n_ctx + ctx) * rows
                out_ref[core * columns : (core + 1) * columns, start : start + rows] = full_ref[
                    hi, core, ctx, 0
                ].astype(jnp.float32).T


def lay_rows(full):
    n_hi, _, n_ctx, n_shard, rows, columns = full.shape
    n_part = n_hi * n_ctx
    return pl.pallas_call(
        lay_rows_kernel,
        grid=(n_shard,),
        in_specs=[
            pl.BlockSpec((n_hi, 2, n_ctx, 1, rows, columns), lambda j: (0, 0, 0, j, 0, 0))
        ],
        out_specs=pl.BlockSpec((2 * columns, n_part * rows), lambda j: (0, j)),
        out_shape=jax.ShapeDtypeStruct((2 * columns, n_shard * n_part * rows), jnp.float32),
        compiler_params=pltpu.CompilerParams(vmem_limit_bytes=48 << 20),
        name="lay_rows",
    )(full)


def lay_heads_kernel(count, at_ref, *refs):
    mine, theirs = refs[:count], refs[count : 2 * count]
    wq_ref, wk_ref, wv_ref, dq_ref, dk_ref, dv_ref, d_out_ref, sums_ref, gains_ref = refs[
        2 * count :
    ]
    q_cols, kv_cols = wq_ref.shape[1] // 2, wk_ref.shape[1] // 2
    out_rows = d_out_ref.shape[0] // 2
    rows = wq_ref.shape[0] // count
    gains = mine[0][0, rows:, :].astype(jnp.float32) + theirs[0][0, rows:, :].astype(jnp.float32)
    add_sums(pl.program_id(0), gains_ref, gains)

    @pl.when(pl.program_id(0) == 0)
    def _():
        sums_ref[...] = jnp.zeros_like(sums_ref)

    for k in range(count):
        part = lax.rem(at_ref[0] - k + count, count)
        here = pl.ds(pl.multiple_of(part * rows, rows), rows)
        total = sums_ref[here, :]
        for core, full_ref in ((at_ref[1], mine[k]), (1 - at_ref[1], theirs[k])):
            full = full_ref[0, :rows].astype(jnp.float32)
            start = 0
            for weight_ref, grad_ref, columns in (
                (wq_ref, dq_ref, q_cols),
                (wk_ref, dk_ref, kv_cols),
                (wv_ref, dv_ref, kv_cols),
            ):
                grad = full[:, start : start + columns]
                span = pl.ds(pl.multiple_of(core * columns, 128), columns)
                grad_ref[here, span] = grad
                total += lane_sums(grad * weight_ref[here, span].astype(jnp.float32))
                start += columns
            d_out_ref[pl.ds(pl.multiple_of(core * out_rows, 128), out_rows), here] = full[
                :, start:
            ].T
        sums_ref[here, :] = total


def lay_heads(at, mine, theirs, w_query, key_weight, value_weight):
    n_part = len(mine)
    n_shard, all_rows, columns = mine[0].shape
    rows = w_query.shape[0] // n_part
    q_cols = w_query.shape[1] // n_shard
    kv_cols = key_weight.shape[1] // n_shard
    out_rows = 2 * columns - q_cols - 2 * kv_cols
    block = pl.BlockSpec((1, all_rows, columns), lambda j, at: (j, 0, 0))

    def spec(width):
        return pl.BlockSpec(
            (n_part * rows, width), lambda j, at: (0, j)
        )

    return pl.pallas_call(
        partial(lay_heads_kernel, n_part),
        grid_spec=pltpu.PrefetchScalarGridSpec(
            num_scalar_prefetch=1,
            grid=(n_shard,),
            in_specs=[block] * (2 * n_part) + [spec(q_cols), spec(kv_cols), spec(kv_cols)],
            out_specs=[
                spec(q_cols),
                spec(kv_cols),
                spec(kv_cols),
                pl.BlockSpec((out_rows, n_part * rows), lambda j, at: (0, j)),
                pl.BlockSpec((n_part * rows, 128), lambda j, at: (0, 0)),
                pl.BlockSpec((all_rows - rows, columns), lambda j, at: (0, 0)),
            ],
        ),
        out_shape=[
            jax.ShapeDtypeStruct(w_query.shape, jnp.float32),
            jax.ShapeDtypeStruct(key_weight.shape, jnp.float32),
            jax.ShapeDtypeStruct(value_weight.shape, jnp.float32),
            jax.ShapeDtypeStruct((out_rows, n_shard * n_part * rows), jnp.float32),
            jax.ShapeDtypeStruct((n_part * rows, 128), jnp.float32),
            jax.ShapeDtypeStruct((all_rows - rows, columns), jnp.float32),
        ],
        compiler_params=pltpu.CompilerParams(vmem_limit_bytes=48 << 20),
        name="lay_heads",
    )(at, *mine, *theirs, w_query, key_weight, value_weight)


def exchange_ring(pieces, rank, count):
    def piece_for(k):
        return lax.dynamic_index_in_dim(pieces, (rank + k) % count, axis=0, keepdims=False)

    return [piece_for(0)] + [
        lax.ppermute(piece_for(k), "shard", [(i, (i + k) % count) for i in range(count)])
        for k in range(1, count)
    ]


def take_columns_kernel(at_ref, *refs):
    out_ref = refs[-1]
    start = 0
    for ref in refs[:-1]:
        columns = ref.shape[1]
        out_ref[0, :, start : start + columns] = ref[...]
        start += columns


def take_columns(at, n_part, n_shard, weights):
    rows = weights[0].shape[0] // n_part
    widths = [weight.shape[1] // (2 * n_shard) for weight in weights]
    return pl.pallas_call(
        take_columns_kernel,
        grid_spec=pltpu.PrefetchScalarGridSpec(
            num_scalar_prefetch=1,
            grid=(n_shard,),
            in_specs=[
                pl.BlockSpec((rows, width), lambda j, at: (at[0], 2 * j + at[1]))
                for width in widths
            ],
            out_specs=pl.BlockSpec((1, rows, sum(widths)), lambda j, at: (j, 0, 0)),
        ),
        out_shape=jax.ShapeDtypeStruct((n_shard, rows, sum(widths)), weights[0].dtype),
        name="take_columns",
    )(at, *weights)


def lay_order_kernel(at_ref, *refs):
    out_ref = refs[-1]
    count = len(refs) - 1
    rows = refs[0].shape[1]
    for k, ref in enumerate(refs[:-1]):
        owner = lax.rem(at_ref[0] - k + count, count)
        out_ref[pl.ds(pl.multiple_of(owner * rows, rows), rows), :] = ref[0]


def lay_order(at, pieces):
    n_shard, rows, columns = pieces[0].shape
    block = len(pieces) * rows
    return pl.pallas_call(
        lay_order_kernel,
        grid_spec=pltpu.PrefetchScalarGridSpec(
            num_scalar_prefetch=1,
            grid=(n_shard,),
            in_specs=[pl.BlockSpec((1, rows, columns), lambda j, at: (j, 0, 0))] * len(pieces),
            out_specs=pl.BlockSpec((block, columns), lambda j, at: (j, 0)),
        ),
        out_shape=jax.ShapeDtypeStruct((n_shard * block, columns), pieces[0].dtype),
        name="lay_order",
    )(at, *pieces)


def place_kernel(z_ref, *refs):
    out_ref = refs[-1]
    count = len(refs) - 1
    for k, ref in enumerate(refs[:-1]):
        out_ref[lax.rem(z_ref[0] - k + count, count)] = ref[...]


def place(rank, pieces):
    return pl.pallas_call(
        place_kernel,
        grid_spec=pltpu.PrefetchScalarGridSpec(
            num_scalar_prefetch=1,
            grid=(1,),
            in_specs=[pl.BlockSpec(pieces[0].shape, lambda i, z: (0, 0))] * len(pieces),
            out_specs=pl.BlockSpec((len(pieces),) + pieces[0].shape, lambda i, z: (0, 0, 0)),
        ),
        out_shape=jax.ShapeDtypeStruct((len(pieces),) + pieces[0].shape, pieces[0].dtype),
        compiler_params=pltpu.CompilerParams(vmem_limit_bytes=48 << 20),
        name="place",
    )(rank.reshape(1), *pieces)


def norm_kernel(z_ref, tokens_ref, gain_ref, out_ref):
    values = tokens_ref[0].astype(jnp.float32)
    out_ref[...] = (values * recip_rms(values) * gain_ref[...]).astype(jnp.bfloat16)


def norm_group(rank, gathered, gain):
    count, rows, width = gathered.shape
    return pl.pallas_call(
        norm_kernel,
        grid_spec=pltpu.PrefetchScalarGridSpec(
            num_scalar_prefetch=1,
            grid=(count,),
            in_specs=[
                pl.BlockSpec(
                    (1, rows, width), lambda k, z: (lax.rem(z[0] - k + count, count), 0, 0)
                ),
                pl.BlockSpec((1, width), lambda k, z: (0, 0)),
            ],
            out_specs=pl.BlockSpec((rows, width), lambda k, z: (k, 0)),
        ),
        out_shape=jax.ShapeDtypeStruct((count * rows, width), jnp.bfloat16),
        name="norm_group",
    )(rank.reshape(1), gathered, gain.reshape(1, width))


def turn(values, table):
    return pltpu.roll(values, HEAD_SIZE // 2, 1) * table


def project_kernel(n_part, q_cols, at_ref, *refs):
    tokens = refs[:n_part]
    pieces = refs[n_part : 2 * n_part]
    cos_ref, sin_ref, gain_q_ref, gain_k_ref, queries_ref, kv_ref, pre_ref, acc_ref = refs[
        2 * n_part :
    ]
    step = pl.program_id(0)
    columns = acc_ref.shape[1]
    kv_cols = (columns - q_cols) // 2
    total = sum(
        jnp.dot(block[...], piece[0], preferred_element_type=jnp.float32)
        for block, piece in zip(tokens, pieces)
    )
    add_sums(step, acc_ref, total)

    @pl.when(step == pl.num_programs(0) - 1)
    def _():
        rows = 64

        def body(chunk, carry):
            span = pl.ds(pl.multiple_of(chunk * rows, rows), rows)
            cosine, sine = cos_ref[span, :], sin_ref[span, :]
            for start in range(0, q_cols + kv_cols, HEAD_SIZE):
                values = acc_ref[span, start : start + HEAD_SIZE]
                pre_ref[span, start : start + HEAD_SIZE] = values
                gain = gain_q_ref[...] if start < q_cols else gain_k_ref[...]
                scaled = values * recip_rms(values) * gain
                turned = (scaled * cosine + turn(scaled, sine)).astype(jnp.bfloat16)
                if start < q_cols:
                    queries_ref[span, start : start + HEAD_SIZE] = turned
                else:
                    kv_ref[span, start - q_cols : start - q_cols + HEAD_SIZE] = turned
            kv_ref[span, kv_cols:] = acc_ref[span, q_cols + kv_cols :].astype(jnp.bfloat16)
            return carry

        lax.fori_loop(0, acc_ref.shape[0] // rows, body, 0)


def project(at, q_cols, tokens, pieces, cosine, sine, gain_q, gain_k):
    n_part = len(pieces)
    n_shard, slice_rows, columns = pieces[0].shape
    group, width = tokens.shape
    kv_cols = (columns - q_cols) // 2

    def token_spec(k):
        return pl.BlockSpec(
            (group, slice_rows),
            lambda j, at: (0, j * n_part + lax.rem(at[0] - k + n_part, n_part)),
        )

    def whole(shape):
        return pl.BlockSpec(shape, lambda j, at: (0, 0))

    head = (1, HEAD_SIZE)
    return pl.pallas_call(
        partial(project_kernel, n_part, q_cols),
        grid_spec=pltpu.PrefetchScalarGridSpec(
            num_scalar_prefetch=1,
            grid=(n_shard,),
            in_specs=[token_spec(k) for k in range(n_part)]
            + [pl.BlockSpec((1, slice_rows, columns), lambda j, at: (j, 0, 0))] * n_part
            + [whole(cosine.shape), whole(sine.shape), whole(head), whole(head)],
            out_specs=[
                whole((group, q_cols)),
                whole((group, 2 * kv_cols)),
                whole((group, q_cols + kv_cols)),
            ],
            scratch_shapes=[pltpu.VMEM((group, columns), jnp.float32)],
        ),
        out_shape=[
            jax.ShapeDtypeStruct((group, q_cols), jnp.bfloat16),
            jax.ShapeDtypeStruct((group, 2 * kv_cols), jnp.bfloat16),
            jax.ShapeDtypeStruct((group, q_cols + kv_cols), jnp.float32),
        ],
        compiler_params=pltpu.CompilerParams(vmem_limit_bytes=48 << 20),
        name="project",
    )(
        at,
        *([tokens] * n_part),
        *pieces,
        cosine,
        sine,
        gain_q.reshape(head),
        gain_k.reshape(head),
    )


def head_probs(start, q_pos_ref, k_pos_ref, query, keys):
    scores = [
        lax.dot_general(
            query, key, (((1,), (1,)), ((), ())), preferred_element_type=jnp.float32
        )
        for key in keys
    ]
    scores = jnp.concatenate(scores, axis=1) * HEAD_SIZE ** (-0.5)
    q_pos, k_pos = q_pos_ref[...], k_pos_ref[...]
    inside_q = (q_pos >= start) & (q_pos < start + PIC)
    inside_k = (k_pos >= start) & (k_pos < start + PIC)
    allowed = (k_pos <= q_pos) | (inside_q & inside_k)
    scores = jnp.where(allowed, scores, -1e30)
    powers = jnp.exp(scores - jnp.max(scores, axis=1, keepdims=True))
    return powers / jnp.sum(powers, axis=1, keepdims=True)


def attend_kernel(n_ctx, core, starts_ref, *refs):
    kv_refs = refs[:n_ctx]
    queries_ref, q_pos_ref, k_pos_ref, mixed_ref = refs[n_ctx:]
    block = queries_ref.shape
    tokens = block[1] * block[3]
    start = starts_ref[core, pl.program_id(0)]
    queries = queries_ref[...].reshape(tokens, block[4])
    kv = [ref[...].reshape(tokens, ref.shape[4]) for ref in kv_refs]
    kv_cols = kv[0].shape[1] // 2
    group_width = block[4] // kv_cols
    out = []
    for head in range(block[4] // HEAD_SIZE):
        key_start = head // group_width * HEAD_SIZE
        query = queries[:, head * HEAD_SIZE : (head + 1) * HEAD_SIZE]
        keys = [part[:, key_start : key_start + HEAD_SIZE] for part in kv]
        values = [
            part[:, kv_cols + key_start : kv_cols + key_start + HEAD_SIZE] for part in kv
        ]
        probs = head_probs(start, q_pos_ref, k_pos_ref, query, keys).astype(jnp.bfloat16)
        mixed = sum(
            jnp.dot(
                probs[:, i * tokens : (i + 1) * tokens], part, preferred_element_type=jnp.float32
            )
            for i, part in enumerate(values)
        )
        out.append(mixed.astype(jnp.bfloat16))
    mixed_ref[...] = jnp.concatenate(out, axis=1).reshape(mixed_ref.shape)


def sequence_view(values, count, micro, rows):
    return values.reshape(1, count, micro, rows, values.shape[-1])


def attend(core, starts, count, micro, rows, queries, kv_parts, q_pos, k_pos):
    n_ctx = len(kv_parts)

    def spec(columns):
        return pl.BlockSpec((1, count, 1, rows, columns), lambda m, s: (0, 0, m, 0, 0))

    view = partial(sequence_view, count=count, micro=micro, rows=rows)
    columns = queries.shape[1]
    mixed = pl.pallas_call(
        partial(attend_kernel, n_ctx, core),
        grid_spec=pltpu.PrefetchScalarGridSpec(
            num_scalar_prefetch=1,
            grid=(micro,),
            in_specs=[spec(kv_parts[0].shape[1])] * n_ctx
            + [
                spec(columns),
                pl.BlockSpec(q_pos.shape, lambda m, s: (0, 0)),
                pl.BlockSpec(k_pos.shape, lambda m, s: (0, 0)),
            ],
            out_specs=spec(columns),
        ),
        out_shape=jax.ShapeDtypeStruct(view(queries).shape, jnp.bfloat16),
        compiler_params=pltpu.CompilerParams(vmem_limit_bytes=48 << 20),
        name="attend",
    )(starts, *[view(part) for part in kv_parts], view(queries), q_pos, k_pos)
    return mixed.reshape(queries.shape)


def norm_turn_back(pre, d_turned, cosine, sine, gain):
    recip = recip_rms(pre)
    unit = pre * recip
    d_unit = d_turned * cosine + pltpu.roll(d_turned * sine, HEAD_SIZE // 2, 1)
    d_gain = jnp.sum(d_unit * unit, axis=0, keepdims=True)
    return norm_back(unit, recip, gain, d_unit), d_gain


def attend_back_kernel(n_ctx, core, starts_ref, *refs):
    kv_refs = refs[:n_ctx]
    queries_ref, pre_ref, d_mixed_ref, q_pos_ref, k_pos_ref, cos_ref, sin_ref, gain_ref = refs[
        n_ctx : n_ctx + 8
    ]
    d_queries_ref, sums_ref = refs[n_ctx + 8 : n_ctx + 10]
    d_kv_refs = refs[n_ctx + 10 :]
    block = queries_ref.shape
    tokens = block[1] * block[3]
    start = starts_ref[core, pl.program_id(0)]
    queries = queries_ref[...].reshape(tokens, block[4])
    d_mixed = d_mixed_ref[...].reshape(tokens, block[4])
    pre = pre_ref[...].reshape(tokens, pre_ref.shape[4])
    kv = [ref[...].reshape(tokens, ref.shape[4]) for ref in kv_refs]
    kv_cols = kv[0].shape[1] // 2
    group_width = block[4] // kv_cols
    scale = HEAD_SIZE ** (-0.5)
    down = (((0,), (0,)), ((), ()))
    across = (((1,), (1,)), ((), ()))
    f32 = jnp.float32
    d_queries, sums = [], 0.0
    d_keys, d_values = {}, {}
    for head in range(block[4] // HEAD_SIZE):
        key_start = head // group_width * HEAD_SIZE
        span = slice(head * HEAD_SIZE, (head + 1) * HEAD_SIZE)
        query, d_mix = queries[:, span], d_mixed[:, span]
        keys = [part[:, key_start : key_start + HEAD_SIZE] for part in kv]
        values = [
            part[:, kv_cols + key_start : kv_cols + key_start + HEAD_SIZE] for part in kv
        ]
        probs = head_probs(start, q_pos_ref, k_pos_ref, query, keys)
        d_probs = jnp.concatenate(
            [lax.dot_general(d_mix, part, across, preferred_element_type=f32) for part in values],
            axis=1,
        )
        row_dot = jnp.sum(probs * d_probs, axis=1, keepdims=True)
        d_scores = (probs * (d_probs - row_dot)).astype(jnp.bfloat16)
        probs_low = probs.astype(jnp.bfloat16)
        d_query = 0.0
        for i, key in enumerate(keys):
            piece = slice(i * tokens, (i + 1) * tokens)
            d_query += jnp.dot(d_scores[:, piece], key, preferred_element_type=f32)
            d_key = lax.dot_general(d_scores[:, piece], query, down, preferred_element_type=f32)
            d_value = lax.dot_general(
                probs_low[:, piece], d_mix, down, preferred_element_type=f32
            )
            at = (i, key_start)
            d_keys[at] = d_keys.get(at, 0.0) + d_key * scale
            d_values[at] = d_values.get(at, 0.0) + d_value
        d_pre, d_gain = norm_turn_back(
            pre[:, span],
            d_query * scale,
            cos_ref[...].reshape(tokens, HEAD_SIZE),
            sin_ref[...].reshape(tokens, HEAD_SIZE),
            gain_ref[...],
        )
        d_queries.append(d_pre.astype(jnp.bfloat16))
        sums += d_gain
    d_queries_ref[...] = jnp.concatenate(d_queries, axis=1).reshape(d_queries_ref.shape)
    for i, ref in enumerate(d_kv_refs):
        parts = [d_keys[at] for at in sorted(d_keys) if at[0] == i]
        parts += [d_values[at] for at in sorted(d_values) if at[0] == i]
        ref[...] = jnp.concatenate(parts, axis=1).astype(ref.dtype).reshape(ref.shape)
    add_sums(pl.program_id(0), sums_ref, jnp.broadcast_to(sums, sums_ref.shape))


def attend_back(
    core, starts, count, micro, rows, queries, pre, kv_parts, d_mixed, q_pos, k_pos, cosine, sine, gain
):
    n_ctx = len(kv_parts)
    view = partial(sequence_view, count=count, micro=micro, rows=rows)

    def spec(columns):
        return pl.BlockSpec((1, count, 1, rows, columns), lambda m, s: (0, 0, m, 0, 0))

    def whole(values):
        return pl.BlockSpec(values.shape, lambda m, s: (0, 0))

    columns, kv_columns = queries.shape[1], kv_parts[0].shape[1]
    gain = gain.reshape(1, HEAD_SIZE)
    view_shape = view(d_mixed).shape
    outs = pl.pallas_call(
        partial(attend_back_kernel, n_ctx, core),
        grid_spec=pltpu.PrefetchScalarGridSpec(
            num_scalar_prefetch=1,
            grid=(micro,),
            in_specs=[spec(kv_columns)] * n_ctx
            + [spec(columns), spec(pre.shape[1]), spec(columns)]
            + [whole(q_pos), whole(k_pos), spec(HEAD_SIZE), spec(HEAD_SIZE), whole(gain)],
            out_specs=[spec(columns), pl.BlockSpec((8, HEAD_SIZE), lambda m, s: (0, 0))]
            + [spec(kv_columns)] * n_ctx,
        ),
        out_shape=[
            jax.ShapeDtypeStruct(view_shape, jnp.bfloat16),
            jax.ShapeDtypeStruct((8, HEAD_SIZE), jnp.float32),
        ]
        + [
            jax.ShapeDtypeStruct(
                view_shape[:-1] + (kv_columns,), jnp.float32 if i == 0 else jnp.bfloat16
            )
            for i in range(n_ctx)
        ],
        compiler_params=pltpu.CompilerParams(vmem_limit_bytes=48 << 20),
        name="attend_back",
    )(
        starts,
        *[view(part) for part in kv_parts],
        view(queries),
        view(pre),
        view(d_mixed),
        q_pos,
        k_pos,
        view(cosine),
        view(sine),
        gain,
    )
    flat = [values.reshape(d_mixed.shape[0], -1) for values in outs[:1] + outs[2:]]
    return flat[0], outs[1][0], flat[1:]


def keys_back_kernel(n_got, q_cols, *refs):
    d_q_ref, own_ref = refs[:2]
    got_refs = refs[2 : 2 + n_got]
    pre_ref, cos_ref, sin_ref, gain_ref, out_ref, sums_ref = refs[2 + n_got :]
    total = own_ref[...]
    for ref in got_refs:
        total += ref[...].astype(jnp.float32)
    kv_cols = total.shape[1] // 2
    out_ref[:, :q_cols] = d_q_ref[...]
    out_ref[:, q_cols + kv_cols :] = total[:, kv_cols:].astype(jnp.bfloat16)
    sums = 0.0
    for start in range(0, kv_cols, HEAD_SIZE):
        span = slice(start, start + HEAD_SIZE)
        at = slice(q_cols + start, q_cols + start + HEAD_SIZE)
        d_pre, d_gain = norm_turn_back(
            pre_ref[:, at], total[:, span], cos_ref[...], sin_ref[...], gain_ref[...]
        )
        out_ref[:, at] = d_pre.astype(jnp.bfloat16)
        sums += d_gain
    sums_ref[...] = jnp.broadcast_to(sums, sums_ref.shape)


def keys_back(d_queries, own, got, pre, cosine, sine, gain):
    rows, q_cols = d_queries.shape
    out, sums = pl.pallas_call(
        partial(keys_back_kernel, len(got), q_cols),
        out_shape=[
            jax.ShapeDtypeStruct((rows, q_cols + own.shape[1]), jnp.bfloat16),
            jax.ShapeDtypeStruct((8, HEAD_SIZE), jnp.float32),
        ],
        name="keys_back",
    )(d_queries, own, *got, pre, cosine, sine, gain.reshape(1, HEAD_SIZE))
    return out, sums[0]


def head_gradients_kernel(count, at_ref, *refs):
    normed, branch = refs[: 2 * count], refs[2 * count : 4 * count]
    d_qkv, mixed = refs[4 * count : 4 * count + 2], refs[4 * count + 2 : 4 * count + 4]
    gains_ref = refs[4 * count + 4]
    down = (((0,), (0,)), ((), ()))
    slice_rows = normed[0].shape[1]
    for k, out_ref in enumerate(refs[4 * count + 5 :]):
        split = d_qkv[0].shape[1]
        out_ref[0, slice_rows:, :] = gains_ref[...]
        for columns, left, right in (
            (slice(0, split), normed, d_qkv),
            (slice(split, out_ref.shape[2]), branch, mixed),
        ):
            out_ref[0, :slice_rows, columns] = sum(
                lax.dot_general(
                    left[core * count + k][...],
                    right[core][...],
                    down,
                    preferred_element_type=jnp.float32,
                )
                for core in range(2)
            ).astype(jnp.bfloat16)


def head_gradients(at, n_part, n_shard, normed, d_branch, d_qkv, mixed, gains):
    rows, width = normed[0].shape
    slice_rows = width // (n_part * n_shard)
    columns = d_qkv[0].shape[1] + mixed[0].shape[1]

    def spec(k):
        return pl.BlockSpec(
            (rows, slice_rows),
            lambda j, at: (0, j * n_part + lax.rem(at[0] - k + n_part, n_part)),
        )

    def whole(values):
        return pl.BlockSpec(values.shape, lambda j, at: (0, 0))

    specs = [spec(k) for k in range(n_part)] * 2
    out_rows = slice_rows + gains.shape[0]
    out = pl.BlockSpec((1, out_rows, columns), lambda j, at: (j, 0, 0))
    return pl.pallas_call(
        partial(head_gradients_kernel, n_part),
        grid_spec=pltpu.PrefetchScalarGridSpec(
            num_scalar_prefetch=1,
            grid=(n_shard,),
            in_specs=specs + specs + [whole(values) for values in d_qkv + mixed + (gains,)],
            out_specs=[out] * n_part,
        ),
        out_shape=[jax.ShapeDtypeStruct((n_shard, out_rows, columns), jnp.bfloat16)] * n_part,
        compiler_params=pltpu.CompilerParams(vmem_limit_bytes=48 << 20),
        name="head_gradients",
    )(
        at,
        *[normed[0]] * n_part,
        *[normed[1]] * n_part,
        *[d_branch[0]] * n_part,
        *[d_branch[1]] * n_part,
        *d_qkv,
        *mixed,
        gains,
    )


def product_kernel(groups, has_got, *refs):
    count = sum(n for n, _ in groups)
    lefts, rights, rest = refs[:count], refs[count : 2 * count], refs[2 * count :]
    if has_got:
        got_ref, rest = rest[0], rest[1:]
    rows = rest[0].shape[1]
    at = 0
    for group, (n, contract) in enumerate(groups):
        total = sum(
            lax.dot_general(
                left[...],
                right[...],
                (((1,), (contract,)), ((), ())),
                preferred_element_type=jnp.float32,
            )
            for left, right in zip(lefts[at : at + n], rights[at : at + n])
        )
        at += n
        if has_got:
            total = total + got_ref[group].astype(jnp.float32)
        for k, ref in enumerate(rest):
            ref[group] = total[k * rows : (k + 1) * rows].astype(ref.dtype)


def product(groups, dtype=jnp.bfloat16, got=None, split=1):
    rows = groups[0][0][0].shape[0]
    columns = groups[0][1].shape[1 - groups[0][2]]
    block = 512 if columns % 512 == 0 else 256
    left_specs, right_specs, lefts, rights = [], [], [], []

    def right_spec(contract, depth, k):
        if contract:
            return pl.BlockSpec((block, depth), lambda j: (j, k))
        return pl.BlockSpec((depth, block), lambda j: (k, j))

    for terms, right, contract in groups:
        for k, term in enumerate(terms):
            depth = term.shape[1]
            left_specs.append(pl.BlockSpec((rows, depth), lambda j: (0, 0)))
            right_specs.append(right_spec(contract, depth, k))
            lefts.append(term)
            rights.append(right)
    n = len(groups)
    in_specs, args = left_specs + right_specs, lefts + rights
    if got is not None:
        in_specs = in_specs + [pl.BlockSpec((n, rows, block), lambda j: (0, 0, j))]
        args = args + [got]
    dtypes = [dtype] if got is None else [jnp.float32] + [jnp.bfloat16] * (split - 1)
    outs = pl.pallas_call(
        partial(
            product_kernel,
            [(len(terms), contract) for terms, _, contract in groups],
            got is not None,
        ),
        grid=(columns // block,),
        in_specs=in_specs,
        out_specs=[pl.BlockSpec((n, rows // split, block), lambda j: (0, 0, j))] * split,
        out_shape=[jax.ShapeDtypeStruct((n, rows // split, columns), kind) for kind in dtypes],
        compiler_params=pltpu.CompilerParams(vmem_limit_bytes=48 << 20),
        name="product",
    )(*args)
    return outs if got is not None else outs[0]


def ffn_gradients_kernel(*refs):
    ffn, cot, d_gate, d_up, inner = (refs[2 * i : 2 * i + 2] for i in range(5))
    out_ref = refs[10]
    down = (((0,), (0,)), ((), ()))
    start = 0
    for left, right in ((ffn, d_gate), (ffn, d_up), (cot, inner)):
        stop = start + right[0].shape[1]
        out_ref[0, :, start:stop] = sum(
            lax.dot_general(
                left[core][...], right[core][...], down, preferred_element_type=jnp.float32
            )
            for core in range(2)
        ).astype(jnp.bfloat16)
        start = stop


def ffn_gradients(n_shard, ffn_in, cot, d_gate, d_up, inner):
    rows, width = ffn_in[0].shape
    ff = inner[0].shape[1]
    block = 256
    per = width // (n_shard * block)
    left = pl.BlockSpec((rows, block), lambda j: (0, j))
    right = pl.BlockSpec((rows, ff), lambda j: (0, 0))
    return pl.pallas_call(
        ffn_gradients_kernel,
        grid=(width // block,),
        in_specs=[left] * 4 + [right] * 6,
        out_specs=pl.BlockSpec((1, block, 3 * ff), lambda j: (j // per, j % per, 0)),
        out_shape=jax.ShapeDtypeStruct((n_shard, width // n_shard, 3 * ff), jnp.bfloat16),
        compiler_params=pltpu.CompilerParams(vmem_limit_bytes=56 << 20),
        name="ffn_gradients",
    )(*ffn_in, *cot, *d_gate, *d_up, *inner)


def reorder_kernel(z_ref, in_ref, out_ref):
    out_ref[...] = in_ref[0]


def ring_order(rank, gathered):
    count, rows, width = gathered.shape
    return pl.pallas_call(
        reorder_kernel,
        grid_spec=pltpu.PrefetchScalarGridSpec(
            num_scalar_prefetch=1,
            grid=(count,),
            in_specs=[
                pl.BlockSpec(
                    (1, rows, width), lambda k, z: (lax.rem(z[0] - k + count, count), 0, 0)
                )
            ],
            out_specs=pl.BlockSpec((rows, width), lambda k, z: (k, 0)),
        ),
        out_shape=jax.ShapeDtypeStruct((count * rows, width), gathered.dtype),
        name="ring_order",
    )(rank.reshape(1), gathered)


def inner_kernel(ffn_ref, gate_ref, up_ref, d_inner_ref, inner_ref, d_gate_ref, d_up_ref):
    ffn = ffn_ref[...]
    gate_pre = jnp.dot(ffn, gate_ref[...], preferred_element_type=jnp.float32)
    up_pre = jnp.dot(ffn, up_ref[...], preferred_element_type=jnp.float32)
    d_inner = d_inner_ref[...]
    sigma = jax.nn.sigmoid(gate_pre)
    act_gate = gate_pre * sigma
    inner_ref[...] = (act_gate * up_pre).astype(jnp.bfloat16)
    d_gate = d_inner * up_pre * sigma * (1.0 + gate_pre * (1.0 - sigma))
    d_gate_ref[...] = d_gate.astype(jnp.bfloat16)
    d_up_ref[...] = (d_inner * act_gate).astype(jnp.bfloat16)


def inner_parts(ffn_in, w_in, d_inner):
    rows, width = ffn_in.shape
    ff = w_in.shape[1] // 2
    block = 256 if ff % 256 == 0 else 128
    steps = ff // block
    out = pl.BlockSpec((rows, block), lambda j: (0, j))
    shape = jax.ShapeDtypeStruct((rows, ff), jnp.bfloat16)
    return pl.pallas_call(
        inner_kernel,
        grid=(steps,),
        in_specs=[
            pl.BlockSpec((rows, width), lambda j: (0, 0)),
            pl.BlockSpec((width, block), lambda j: (0, j)),
            pl.BlockSpec((width, block), lambda j: (0, steps + j)),
            out,
        ],
        out_specs=[out, out, out],
        out_shape=[shape, shape, shape],
        compiler_params=pltpu.CompilerParams(vmem_limit_bytes=48 << 20),
        name="inner_parts",
    )(ffn_in, w_in, w_in, d_inner)


def grouped_shards(
    n_hi,
    n_shard,
    n_ctx,
    tokens,
    span_starts,
    cotangent,
    w_query,
    key_weight,
    value_weight,
    w_out,
    attn_gain,
    query_gain,
    key_gain,
    w_gate,
    w_up,
    w_down,
    ffn_gain,
):
    bf16 = jnp.bfloat16
    f32 = jnp.float32
    z = lax.axis_index("shard")
    x = lax.axis_index("ctx")
    c = lax.axis_index("core")
    part = lax.axis_index(("hi", "ctx"))
    n_part = n_hi * n_ctx
    micro, _, rows, width = tokens.shape
    own = micro * rows
    group = n_shard * own
    n_tp = 2 * n_shard
    kv_local = KEY_VALUE_HEADS // n_tp
    q_local = QUERY_HEADS // n_tp
    group_width = QUERY_HEADS // KEY_VALUE_HEADS
    q_cols = q_local * HEAD_SIZE
    kv_cols = kv_local * HEAD_SIZE
    ff = w_down.shape[0] // 2

    slice_rows = w_query.shape[0] // n_part
    def exchange(pieces):
        return lax.all_to_all(pieces, "shard", 0, 0, tiled=True)

    def gather_plane(values):
        full = lax.all_gather(values, ("hi", "core", "ctx"), axis=0)
        return full.reshape((n_hi, 2, n_ctx) + values.shape)

    own_tokens = tokens.reshape(own, width)
    own_cot = cotangent.reshape(own, width)
    at = jnp.stack([part, c, z])
    gathered = lax.all_gather(own_tokens, "shard", axis=0)
    pieces_qkv = take_columns(at, n_part, n_shard, (w_query, key_weight, value_weight))
    pieces_in = take_columns(at, n_part, n_shard, (w_gate, w_up))
    gain_sizes = (attn_gain.shape[0], query_gain.shape[0], key_gain.shape[0], ffn_gain.shape[0])
    gains = after(jnp.concatenate([attn_gain, query_gain, key_gain, ffn_gain]), pieces_qkv)
    gains = from_ring(gains, "shard", n_shard)
    starts = after(span_starts.reshape(micro), pieces_qkv)
    starts = jnp.stack([starts, swap(starts, "core")])
    got_qkv = after(exchange(pieces_qkv), pieces_in, gains, starts)
    gains = in_order(gains, z).astype(f32)
    w_out_rows = lax.dynamic_slice_in_dim(w_out, c * q_cols, q_cols, axis=0)
    w_down_rows = lax.dynamic_slice_in_dim(w_down, c * ff, ff, axis=0)
    ring_qkv = from_ring(got_qkv, ("hi", "ctx"), n_part)
    gathered = after(gathered, ring_qkv, gains, starts)
    ends = [0]
    for size in gain_sizes:
        ends.append(ends[-1] + size)
    gain_attn, gain_query, gain_key, gain_ffn = [
        gains[:, ends[i] : ends[i + 1]].reshape(-1) for i in range(4)
    ]

    blocks = jnp.arange(n_shard, dtype=jnp.int32)
    owners = (z - blocks) % n_shard

    def positions(ctx_rank):
        start = (owners * n_ctx + ctx_rank) * rows
        return (start[:, None] + jnp.arange(rows, dtype=jnp.int32)[None, :]).reshape(-1)

    query_pos = positions(x)
    key_pos = jnp.concatenate([positions((x - k) % n_ctx) for k in range(n_ctx)])
    cosine, sine = (table[:, 0, :] for table in spin_tables(query_pos))
    sine = jnp.where(jnp.arange(HEAD_SIZE) < HEAD_SIZE // 2, -1.0, 1.0) * sine

    def by_row(table):
        table = table.reshape(n_shard, 1, rows, HEAD_SIZE)
        return jnp.broadcast_to(table, (n_shard, micro, rows, HEAD_SIZE)).reshape(group, HEAD_SIZE)

    cosine, sine = by_row(cosine), by_row(sine)
    query_pos = query_pos[:, None]
    key_pos = key_pos[None, :]
    order = (n_shard, micro, rows)

    normed_mine = norm_group(z, gathered, gain_attn)
    normed_theirs = swap(normed_mine, "core")
    got_in = exchange_ring(after(pieces_in, gathered), z, n_shard)
    cot_all = lax.all_gather(after(own_cot, gathered), "shard", axis=0)
    turns = (cosine, sine, gain_query, gain_key)
    q_mine, kv_mine, pre_mine = project(at, q_cols, normed_mine, ring_qkv, *turns)
    q_theirs, kv_theirs, pre_theirs = project(
        at, q_cols, after(normed_theirs, kv_mine), ring_qkv, *turns
    )
    kv_parts = from_ring(jnp.concatenate([kv_mine, kv_theirs], axis=0), "ctx", n_ctx)
    kv_mine_parts = [values[:group] for values in kv_parts]
    kv_theirs_parts = [values[group:] for values in kv_parts]
    w_qkv = lay_order(at, after(ring_qkv, kv_theirs))
    mixed_mine = attend(
        0, starts, *order, after(q_mine, w_qkv), kv_mine_parts, query_pos, key_pos
    )
    mixed_theirs = attend(
        1, starts, *order, after(q_theirs, mixed_mine), kv_theirs_parts, query_pos, key_pos
    )
    def core_sum(mine, theirs, right, contract):
        got = swap(product([(theirs, right, contract)]), "core")
        pieces = product([(mine, right, contract)], got=got, split=n_shard)
        return [piece[0] for piece in pieces]

    branch_sent = core_sum([mixed_mine], [mixed_theirs], w_out_rows, 0)
    hidden_in = own_tokens.astype(f32)
    got_in = place(z, after(got_in, branch_sent))
    cot_all = after(cot_all, got_in)
    w_in = lax.all_gather(after(got_in, cot_all), ("hi", "ctx"), axis=1, tiled=True)
    w_in = w_in.reshape(width, -1)
    cot_mine = ring_order(z, cot_all)
    cot_theirs = swap(cot_mine, "core")
    branch_terms = send_terms(branch_sent, "shard", n_shard)
    middle = hidden_in + sum_terms(after(branch_terms, cot_mine))

    recip_m = recip_rms(middle)
    unit_m = middle * recip_m
    ffn_own = (unit_m * gain_ffn).astype(bf16)
    ffn_ring = from_ring(ffn_own, "shard", n_shard)
    d_inner_mine = product([([after(cot_mine, ffn_own)], w_down_rows, 1)], f32)[0]
    d_inner_theirs = product([([after(cot_theirs, d_inner_mine)], w_down_rows, 1)], f32)[0]
    ffn_mine = jnp.concatenate(after(ffn_ring, d_inner_theirs, w_in), axis=0)
    ffn_theirs = swap(ffn_mine, "core")
    inner_mine, d_gate_mine, d_up_mine = inner_parts(ffn_mine, w_in, d_inner_mine)
    inner_theirs, d_gate_theirs, d_up_theirs = inner_parts(
        after(ffn_theirs, inner_mine), w_in, d_inner_theirs
    )
    grad_in = ffn_gradients(
        n_shard,
        (ffn_mine, ffn_theirs),
        (cot_mine, cot_theirs),
        (d_gate_mine, d_gate_theirs),
        (d_up_mine, d_up_theirs),
        (inner_mine, inner_theirs),
    )
    part_in = lax.psum_scatter(grad_in, ("hi", "ctx"), scatter_dimension=1, tiled=True)
    d_ffn_sent = core_sum(
        [d_gate_mine, d_up_mine], [after(d_gate_theirs, grad_in), d_up_theirs], w_in, 1
    )
    d_ffn_in = sum_terms(send_terms(d_ffn_sent, "shard", n_shard))
    d_middle = own_cot.astype(f32) + norm_back(unit_m, recip_m, gain_ffn, d_ffn_in)

    d_branch_own = d_middle.astype(bf16)
    branch_ring = from_ring(d_branch_own, "shard", n_shard)
    branch_mine, part_in = lax.optimization_barrier((jnp.concatenate(branch_ring, axis=0), part_in))
    branch_theirs = swap(branch_mine, "core")
    d_mixed_mine = product([([branch_mine], w_out_rows, 1)])[0]
    tables = (query_pos, key_pos, cosine, sine, gain_query)
    d_q_mine, gain_q_mine, d_kv_mine = attend_back(
        0, starts, *order, q_mine, pre_mine, kv_mine_parts, d_mixed_mine, *tables
    )
    d_mixed_theirs = product([([after(branch_theirs, d_q_mine)], w_out_rows, 1)])[0]
    d_q_theirs, gain_q_theirs, d_kv_theirs = attend_back(
        1, starts, *order, q_theirs, pre_theirs, kv_theirs_parts, d_mixed_theirs, *tables
    )

    sent_in = exchange_ring(part_in[..., : 2 * ff], z, n_shard)
    full_down = gather_plane(part_in[..., 2 * ff :])

    def keys_gradient(d_queries, d_kv, pre, *others):
        got = [
            lax.ppermute(d_kv[n_ctx - k], "ctx", [(i, (i + k) % n_ctx) for i in range(n_ctx)])
            for k in range(1, n_ctx)
        ]
        got = [after(values, *others) for values in got]
        return keys_back(d_queries, d_kv[0], got, pre, cosine, sine, gain_key)

    d_qkv_mine, gain_k_mine = keys_gradient(d_q_mine, d_kv_mine, pre_mine, d_q_theirs)
    d_qkv_theirs, gain_k_theirs = keys_gradient(
        d_q_theirs, d_kv_theirs, pre_theirs, d_qkv_mine
    )
    sent_in = place(z, after(sent_in, d_qkv_theirs))
    qkv_cols = q_cols + 2 * kv_cols
    head_columns = qkv_cols + q_cols
    full_in = gather_plane(after(sent_in, full_down))
    head_gains = jnp.concatenate([gain_q_mine + gain_q_theirs, gain_k_mine + gain_k_theirs])
    head_gains = jnp.zeros((16, head_columns), f32).at[0, : 2 * HEAD_SIZE].set(head_gains)
    sent = head_gradients(
        at,
        n_part,
        n_shard,
        (normed_mine, normed_theirs),
        (branch_mine, branch_theirs),
        (after(d_qkv_mine, sent_in), d_qkv_theirs),
        (mixed_mine, mixed_theirs),
        head_gains.astype(bf16),
    )
    part_heads = send_terms(sent, ("hi", "ctx"), n_part)
    got = product([([after(d_qkv_theirs, sent)], w_qkv, 1), ([inner_theirs], w_down_rows, 0)])
    part_heads = sum_terms(after(part_heads, got)).astype(bf16)
    last = product(
        [([after(d_qkv_mine, part_heads)], w_qkv, 1), ([inner_mine], w_down_rows, 0)],
        got=swap(got, "core"),
        split=n_shard,
    )
    ring_heads = exchange(part_heads[..., :qkv_cols])
    ring_heads = after(ring_heads, last)
    last = send_terms(last, "shard", n_shard)
    part_heads = jnp.concatenate([ring_heads, part_heads[..., qkv_cols:]], axis=-1)
    mine_heads = from_ring(part_heads, ("hi", "ctx"), n_part)
    grad_down = lay_rows(after(full_down, part_heads))
    grad_gate, grad_up, ffn_sums = lay_in(after(full_in, grad_down), w_gate, w_up)
    mine_heads = after(mine_heads, grad_gate)
    theirs_heads = [swap(values, "core") for values in mine_heads]
    last = sum_terms(after(last, mine_heads))
    recip_h = recip_rms(hidden_in)
    unit_h = hidden_in * recip_h
    input_grad = d_middle + norm_back(unit_h, recip_h, gain_attn, last[0])
    result = (middle + last[1]).astype(bf16)
    grad_query, grad_key, grad_value, grad_out, attn_sums, gain_sums = lay_heads(
        at, mine_heads, theirs_heads, w_query, key_weight, value_weight
    )
    head_gains = gain_sums[0, : 2 * HEAD_SIZE].reshape(2, HEAD_SIZE)
    head_size = query_gain.shape[0]
    head_gains = lax.dynamic_slice_in_dim(head_gains, z * head_size, head_size, axis=1)
    grad_ffn_gain = jnp.sum(ffn_sums, axis=1) / ffn_gain.astype(f32)
    grad_attn_gain = jnp.sum(attn_sums, axis=1) / attn_gain.astype(f32)

    return (
        result.reshape(tokens.shape),
        input_grad.reshape(tokens.shape),
        grad_query,
        grad_key,
        grad_value,
        grad_out,
        grad_attn_gain,
        head_gains[0],
        head_gains[1],
        grad_gate,
        grad_up,
        grad_down,
        grad_ffn_gain,
    )


def solution(mesh):
    n_rep, n_shard, n_ctx = (mesh.shape[name] for name in ("rep", "shard", "ctx"))
    if n_rep % 2 == 0 and KEY_VALUE_HEADS % (2 * n_shard) == 0:
        mesh = Mesh(
            mesh.devices.reshape(n_rep // 2, 2, n_shard, n_ctx), ("hi", "core", "shard", "ctx")
        )
        rep = ("hi", "core")
        body = partial(grouped_shards, n_rep // 2, n_shard, n_ctx)
    else:
        rep = "rep"
        body = shards_general
    in_specs = (
        P(None, rep, ("shard", "ctx"), None),
        P(None, rep),
        P(None, rep, ("shard", "ctx"), None),
        P("shard", None),
        P("shard", None),
        P("shard", None),
        P("shard", None),
        P("shard"),
        P("shard"),
        P("shard"),
        P("shard", None),
        P("shard", None),
        P("shard", None),
        P("shard"),
    )
    out_specs = (
        P(None, rep, ("shard", "ctx"), None),
        P(None, rep, ("shard", "ctx"), None),
        P("shard", None),
        P("shard", None),
        P("shard", None),
        P("shard", None),
        P("shard"),
        P("shard"),
        P("shard"),
        P("shard", None),
        P("shard", None),
        P("shard", None),
        P("shard"),
    )
    return jax.shard_map(body, mesh=mesh, in_specs=in_specs, out_specs=out_specs, check_vma=False)
```

```python
from functools import partial

import jax
import jax.numpy as jnp
from jax import lax
from jax.experimental import pallas as pl
from jax.experimental.pallas import tpu as pltpu
from jax.sharding import Mesh
from jax.sharding import PartitionSpec as P

QUERY_HEADS = 16
KEY_VALUE_HEADS = 8
HEAD_SIZE = 128
PIC = 256


EPSILON = 1e-06
THETA = 1000000.0
FF_BLOCK = 256


def apply_rotation(values):
    half_width = values.shape[-1] // 2
    return jnp.concatenate([-values[..., half_width:], values[..., :half_width]], axis=-1)


def rotate_back(values):
    half_width = values.shape[-1] // 2
    return jnp.concatenate([values[..., half_width:], -values[..., :half_width]], axis=-1)


def spin_tables(positions):
    inverse = THETA ** (-jnp.arange(HEAD_SIZE // 2, dtype=jnp.float32) * 2.0 / HEAD_SIZE)
    angles = positions.astype(jnp.float32)[:, None] * inverse[None, :]
    cosine_table = jnp.concatenate([jnp.cos(angles), jnp.cos(angles)], axis=-1)[:, None, :]
    sine_values = jnp.concatenate([jnp.sin(angles), jnp.sin(angles)], axis=-1)[:, None, :]
    return (cosine_table, sine_values)


def recip_rms(values):
    return lax.rsqrt(jnp.mean(values * values, axis=-1, keepdims=True) + EPSILON)


def norm_back(unit, recip, gain, d_normed):
    d_unit = d_normed * gain
    return recip * (d_unit - unit * jnp.mean(d_unit * unit, axis=-1, keepdims=True))


def over_rows(left, right):
    return lax.dot_general(
        left, right, (((0,), (0,)), ((), ())), preferred_element_type=jnp.float32
    )


def compared_to(left, right):
    return lax.dot_general(
        left, right, (((1,), (1,)), ((), ())), preferred_element_type=jnp.float32
    )


def attention_set(w_query, key_weight, value_weight, w_out, attn_gain, query_gain, key_gain):
    return (
        lax.all_gather(w_query, "shard", axis=0, tiled=True),
        lax.all_gather(key_weight, "shard", axis=0, tiled=True),
        lax.all_gather(value_weight, "shard", axis=0, tiled=True),
        lax.all_gather(w_out, "shard", axis=0, tiled=True),
        lax.all_gather(attn_gain, "shard", axis=0, tiled=True),
        lax.all_gather(query_gain, "shard", axis=0, tiled=True),
        lax.all_gather(key_gain, "shard", axis=0, tiled=True),
    )


def feedforward_set(w_gate, w_up, w_down, ffn_gain):
    return (
        lax.all_gather(w_gate, "shard", axis=0, tiled=True),
        lax.all_gather(w_up, "shard", axis=0, tiled=True),
        lax.all_gather(w_down, "shard", axis=0, tiled=True),
        lax.all_gather(ffn_gain, "shard", axis=0, tiled=True),
    )


def masked_scores(allowed, q_head, k_head):
    scores = jnp.einsum(
        "tgd,sd->gts", q_head, k_head, preferred_element_type=jnp.float32
    ) * HEAD_SIZE ** (-0.5)
    return jnp.where(allowed, scores, -1e30)


def head_forward(allowed, pieces):
    q_head, k_head, v_head = pieces
    scores = masked_scores(allowed, q_head, k_head)
    highest = jnp.max(scores, axis=-1, keepdims=True)
    log_total = highest + jnp.log(jnp.sum(jnp.exp(scores - highest), axis=-1, keepdims=True))
    probs_low = jnp.exp(scores - log_total).astype(jnp.bfloat16)
    mixed = jnp.einsum("gts,sd->tgd", probs_low, v_head, preferred_element_type=jnp.float32)
    return (mixed, log_total)


def head_backward(allowed, pieces):
    q_head, k_head, v_head, d_mix_head, log_total = pieces
    probs = jnp.exp(masked_scores(allowed, q_head, k_head) - log_total)
    probs_low = probs.astype(jnp.bfloat16)
    d_probs = jnp.einsum("tgd,sd->gts", d_mix_head, v_head, preferred_element_type=jnp.float32)
    d_values = jnp.einsum("gts,tgd->sd", probs_low, d_mix_head, preferred_element_type=jnp.float32)
    row_dot = jnp.sum(probs * d_probs, axis=-1, keepdims=True)
    d_scores = (probs * (d_probs - row_dot)).astype(jnp.bfloat16)
    d_queries = jnp.einsum(
        "gts,sd->tgd", d_scores, k_head, preferred_element_type=jnp.float32
    ) * HEAD_SIZE ** (-0.5)
    d_keys = jnp.einsum(
        "gts,tgd->sd", d_scores, q_head, preferred_element_type=jnp.float32
    ) * HEAD_SIZE ** (-0.5)
    return (d_queries, d_keys, d_values)


def shards_general(
    tokens,
    span_starts,
    cotangent,
    w_query,
    key_weight,
    value_weight,
    w_out,
    attn_gain,
    query_gain,
    key_gain,
    w_gate,
    w_up,
    w_down,
    ffn_gain,
):
    seq_count = lax.axis_size(("shard", "ctx"))
    seq_rank = lax.axis_index(("shard", "ctx"))
    token_rows = tokens.shape[2]
    token_length = token_rows * seq_count
    group_width = QUERY_HEADS // KEY_VALUE_HEADS
    local_pos = seq_rank * token_rows + jnp.arange(token_rows, dtype=jnp.int32)
    key_pos = jnp.arange(token_length, dtype=jnp.int32)
    cosine_table, sine_values = spin_tables(local_pos)
    cos_keys = cosine_table[:, 0, :][None]
    sin_keys = sine_values[:, 0, :][None]
    out_list = []
    grad_list = []
    stored = []
    totals = None
    for micro_index in range(tokens.shape[0]):
        span_start = span_starts[micro_index, 0]
        inside_q = (local_pos >= span_start) & (local_pos < span_start + PIC)
        inside_k = (key_pos >= span_start) & (key_pos < span_start + PIC)
        allowed = (key_pos[None, :] <= local_pos[:, None]) | inside_q[:, None] & inside_k[None, :]
        hidden_in = tokens[micro_index, 0].astype(jnp.float32)
        full_query, full_key, full_value, complete_output, gain_attn, gain_query, gain_key = (
            attention_set(w_query, key_weight, value_weight, w_out, attn_gain, query_gain, key_gain)
        )
        gain_attn = gain_attn.astype(jnp.float32)
        gain_query = gain_query.astype(jnp.float32)
        gain_key = gain_key.astype(jnp.float32)
        recip_h = recip_rms(hidden_in)
        unit_h = hidden_in * recip_h
        normalized_rows = (unit_h * gain_attn).astype(jnp.bfloat16)
        q_pre = jnp.dot(normalized_rows, full_query, preferred_element_type=jnp.float32).reshape(
            token_rows, QUERY_HEADS, HEAD_SIZE
        )
        key_before_rotation = jnp.transpose(
            jnp.dot(normalized_rows, full_key, preferred_element_type=jnp.float32).reshape(
                token_rows, KEY_VALUE_HEADS, HEAD_SIZE
            ),
            (1, 0, 2),
        )
        value_local = jnp.transpose(
            jnp.dot(normalized_rows, full_value, preferred_element_type=jnp.float32)
            .astype(jnp.bfloat16)
            .reshape(token_rows, KEY_VALUE_HEADS, HEAD_SIZE),
            (1, 0, 2),
        )
        recip_q = recip_rms(q_pre)
        unit_query = q_pre * recip_q
        recip_k = recip_rms(key_before_rotation)
        unit_k = key_before_rotation * recip_k
        scaled_q = unit_query * gain_query
        scaled_k = unit_k * gain_key
        query_rows = jnp.transpose(
            (scaled_q * cosine_table + apply_rotation(scaled_q) * sine_values)
            .astype(jnp.bfloat16)
            .reshape(token_rows, KEY_VALUE_HEADS, group_width, HEAD_SIZE),
            (1, 0, 2, 3),
        )
        key_local = (scaled_k * cos_keys + apply_rotation(scaled_k) * sin_keys).astype(jnp.bfloat16)
        key_rows, value_matrix = (
            lax.all_gather(key_local, ("shard", "ctx"), axis=1, tiled=True),
            lax.all_gather(value_local, ("shard", "ctx"), axis=1, tiled=True),
        )
        mixed_split, log_total = lax.map(
            partial(head_forward, allowed), (query_rows, key_rows, value_matrix)
        )
        mixed_heads = (
            jnp.transpose(mixed_split, (1, 0, 2, 3))
            .reshape(token_rows, QUERY_HEADS * HEAD_SIZE)
            .astype(jnp.bfloat16)
        )
        middle = hidden_in + jnp.dot(
            mixed_heads, complete_output, preferred_element_type=jnp.float32
        )
        full_gate, full_up, full_down, gain_ffn = feedforward_set(w_gate, w_up, w_down, ffn_gain)
        gain_ffn = gain_ffn.astype(jnp.float32)
        recip_m = recip_rms(middle)
        unit_m = middle * recip_m
        ffn_in = (unit_m * gain_ffn).astype(jnp.bfloat16)
        gate_pre = jnp.dot(ffn_in, full_gate, preferred_element_type=jnp.float32)
        up_pre = jnp.dot(ffn_in, full_up, preferred_element_type=jnp.float32)
        sigma = jax.nn.sigmoid(gate_pre)
        act_gate = gate_pre * sigma
        inner_act = (act_gate * up_pre).astype(jnp.bfloat16)
        result = middle + jnp.dot(inner_act, full_down, preferred_element_type=jnp.float32)
        out_list.append(result.astype(jnp.bfloat16))
        cot_rows = cotangent[micro_index, 0]
        cot_float = cot_rows.astype(jnp.float32)
        d_inner = compared_to(cot_rows, full_down)
        d_gate = (d_inner * up_pre * sigma * (1.0 + gate_pre * (1.0 - sigma))).astype(jnp.bfloat16)
        d_up = (d_inner * act_gate).astype(jnp.bfloat16)
        d_ffn_in = compared_to(d_gate, full_gate) + compared_to(d_up, full_up)
        ffn_gain_part = jnp.sum(d_ffn_in * unit_m, axis=0)
        d_middle = cot_float + norm_back(unit_m, recip_m, gain_ffn, d_ffn_in)
        branch_gradient = d_middle.astype(jnp.bfloat16)
        d_mixed = jnp.transpose(
            compared_to(branch_gradient, complete_output)
            .astype(jnp.bfloat16)
            .reshape(token_rows, KEY_VALUE_HEADS, group_width, HEAD_SIZE),
            (1, 0, 2, 3),
        )
        d_split_q, d_keys, d_values = lax.map(
            partial(head_backward, allowed),
            (query_rows, key_rows, value_matrix, d_mixed, log_total),
        )
        d_queries = jnp.transpose(d_split_q, (1, 0, 2, 3)).reshape(
            token_rows, QUERY_HEADS, HEAD_SIZE
        )
        d_key_local, d_value_local = (
            lax.psum_scatter(
                d_keys.astype(jnp.bfloat16), ("shard", "ctx"), scatter_dimension=1, tiled=True
            ).astype(jnp.float32),
            lax.psum_scatter(
                d_values.astype(jnp.bfloat16), ("shard", "ctx"), scatter_dimension=1, tiled=True
            ).astype(jnp.float32),
        )
        d_unit_q = d_queries * cosine_table + rotate_back(d_queries * sine_values)
        d_unit_k = d_key_local * cos_keys + rotate_back(d_key_local * sin_keys)
        query_gain_part = jnp.sum(d_unit_q * unit_query, axis=(0, 1))
        key_gain_part = jnp.sum(d_unit_k * unit_k, axis=(0, 1))
        d_q_pre = (
            norm_back(unit_query, recip_q, gain_query, d_unit_q)
            .astype(jnp.bfloat16)
            .reshape(token_rows, QUERY_HEADS * HEAD_SIZE)
        )
        d_k_pre = jnp.transpose(
            norm_back(unit_k, recip_k, gain_key, d_unit_k).astype(jnp.bfloat16), (1, 0, 2)
        ).reshape(token_rows, KEY_VALUE_HEADS * HEAD_SIZE)
        d_v_pre = jnp.transpose(d_value_local.astype(jnp.bfloat16), (1, 0, 2)).reshape(
            token_rows, KEY_VALUE_HEADS * HEAD_SIZE
        )
        d_normed = (
            compared_to(d_q_pre, full_query)
            + compared_to(d_k_pre, full_key)
            + compared_to(d_v_pre, full_value)
        )
        attn_gain_part = jnp.sum(d_normed * unit_h, axis=0)
        grad_list.append(d_middle + norm_back(unit_h, recip_h, gain_attn, d_normed))
        stored.append(
            (
                normalized_rows,
                d_q_pre,
                d_k_pre,
                d_v_pre,
                mixed_heads,
                branch_gradient,
                ffn_in,
                d_gate,
                d_up,
                inner_act,
                cot_rows,
            )
        )
        parts = (attn_gain_part, query_gain_part, key_gain_part, ffn_gain_part)
        if totals is None:
            totals = parts
        else:
            totals = tuple((older + newer for older, newer in zip(totals, parts)))
    joined = [
        jnp.concatenate([saved_set[member] for saved_set in stored], axis=0) for member in range(11)
    ]
    (
        normed_all,
        dq_all,
        dk_all,
        dv_all,
        mixed_all,
        branch_all,
        ffn_all,
        gate_all,
        up_all,
        inner_all,
        cot_all,
    ) = joined
    totals = (
        lax.psum_scatter(
            over_rows(normed_all, dq_all).astype(jnp.bfloat16),
            "shard",
            scatter_dimension=0,
            tiled=True,
        ).astype(jnp.float32),
        lax.psum_scatter(
            over_rows(normed_all, dk_all).astype(jnp.bfloat16),
            "shard",
            scatter_dimension=0,
            tiled=True,
        ).astype(jnp.float32),
        lax.psum_scatter(
            over_rows(normed_all, dv_all).astype(jnp.bfloat16),
            "shard",
            scatter_dimension=0,
            tiled=True,
        ).astype(jnp.float32),
        lax.psum_scatter(
            over_rows(mixed_all, branch_all).astype(jnp.bfloat16),
            "shard",
            scatter_dimension=0,
            tiled=True,
        ).astype(jnp.float32),
        lax.psum_scatter(
            totals[0].astype(jnp.bfloat16), "shard", scatter_dimension=0, tiled=True
        ).astype(jnp.float32),
        lax.psum_scatter(
            totals[1].astype(jnp.bfloat16), "shard", scatter_dimension=0, tiled=True
        ).astype(jnp.float32),
        lax.psum_scatter(
            totals[2].astype(jnp.bfloat16), "shard", scatter_dimension=0, tiled=True
        ).astype(jnp.float32),
        lax.psum_scatter(
            over_rows(ffn_all, gate_all).astype(jnp.bfloat16),
            "shard",
            scatter_dimension=0,
            tiled=True,
        ).astype(jnp.float32),
        lax.psum_scatter(
            over_rows(ffn_all, up_all).astype(jnp.bfloat16),
            "shard",
            scatter_dimension=0,
            tiled=True,
        ).astype(jnp.float32),
        lax.psum_scatter(
            over_rows(inner_all, cot_all).astype(jnp.bfloat16),
            "shard",
            scatter_dimension=0,
            tiled=True,
        ).astype(jnp.float32),
        lax.psum_scatter(
            totals[3].astype(jnp.bfloat16), "shard", scatter_dimension=0, tiled=True
        ).astype(jnp.float32),
    )
    summed = (
        lax.psum(totals[0].astype(jnp.bfloat16), ("rep", "ctx")).astype(jnp.float32),
        lax.psum(totals[1].astype(jnp.bfloat16), ("rep", "ctx")).astype(jnp.float32),
        lax.psum(totals[2].astype(jnp.bfloat16), ("rep", "ctx")).astype(jnp.float32),
        lax.psum(totals[3].astype(jnp.bfloat16), ("rep", "ctx")).astype(jnp.float32),
        lax.psum(totals[4].astype(jnp.bfloat16), ("rep", "ctx")).astype(jnp.float32),
        lax.psum(totals[5].astype(jnp.bfloat16), ("rep", "ctx")).astype(jnp.float32),
        lax.psum(totals[6].astype(jnp.bfloat16), ("rep", "ctx")).astype(jnp.float32),
        lax.psum(totals[7].astype(jnp.bfloat16), ("rep", "ctx")).astype(jnp.float32),
        lax.psum(totals[8].astype(jnp.bfloat16), ("rep", "ctx")).astype(jnp.float32),
        lax.psum(totals[9].astype(jnp.bfloat16), ("rep", "ctx")).astype(jnp.float32),
        lax.psum(totals[10].astype(jnp.bfloat16), ("rep", "ctx")).astype(jnp.float32),
    )
    output = jnp.stack(out_list)[:, None]
    input_grad = jnp.stack(grad_list)[:, None]
    return (
        output,
        input_grad,
        summed[0],
        summed[1],
        summed[2],
        summed[3],
        summed[4],
        summed[5],
        summed[6],
        summed[7],
        summed[8],
        summed[9],
        summed[10],
    )


def from_ring(block, axis, count):
    return [block] + [
        lax.ppermute(block, axis, [(i, (i + k) % count) for i in range(count)])
        for k in range(1, count)
    ]


def send_terms(pieces, axis, count):
    return [pieces[0]] + [
        lax.ppermute(
            pieces[count - k].astype(jnp.bfloat16),
            axis,
            [(i, (i + k) % count) for i in range(count)],
        )
        for k in range(1, count)
    ]


def sum_terms(terms):
    return sum(term.astype(jnp.float32) for term in terms)


def swap(values, axis):
    return lax.ppermute(values, axis, [(0, 1), (1, 0)])


def after(value, *others):
    return lax.optimization_barrier((value,) + others)[0] if others else value


def in_order(blocks, rank):
    count = len(blocks)
    twice = jnp.stack(blocks[::-1] + blocks[:0:-1])
    return lax.dynamic_slice_in_dim(twice, count - 1 - rank, count, axis=0)


def lane_sums(values):
    return sum(
        values[:, start : start + 128] for start in range(0, values.shape[1], 128)
    )


def add_sums(step, sums_ref, values):
    @pl.when(step == 0)
    def _():
        sums_ref[...] = values

    @pl.when(step > 0)
    def _():
        sums_ref[...] += values


def lay_in_kernel(full_ref, gate_ref, up_ref, d_gate_ref, d_up_ref, sums_ref):
    columns = gate_ref.shape[1] // 2
    total = None
    for core in range(2):
        for at in range(0, columns, FF_BLOCK):
            full = full_ref[0, core, 0, 0, :, 2 * at : 2 * (at + FF_BLOCK)].astype(jnp.float32)
            span = slice(core * columns + at, core * columns + at + FF_BLOCK)
            d_gate = full[:, :FF_BLOCK]
            d_up = full[:, FF_BLOCK:]
            d_gate_ref[:, span] = d_gate
            d_up_ref[:, span] = d_up
            both = d_gate * gate_ref[:, span].astype(jnp.float32)
            both = lane_sums(both + d_up * up_ref[:, span].astype(jnp.float32))
            total = both if total is None else total + both
    add_sums(pl.program_id(1), sums_ref, total)


def lay_in(full, w_gate, w_up):
    n_hi, _, n_ctx, n_shard, rows, both = full.shape
    shape = jax.ShapeDtypeStruct(w_gate.shape, jnp.float32)
    block = pl.BlockSpec((rows, both), lambda i, j: (i, j))
    return pl.pallas_call(
        lay_in_kernel,
        grid=(n_hi * n_ctx, n_shard),
        in_specs=[
            pl.BlockSpec(
                (1, 2, 1, 1, rows, both), lambda i, j: (i // n_ctx, 0, i % n_ctx, j, 0, 0)
            ),
            block,
            block,
        ],
        out_specs=[block, block, pl.BlockSpec((rows, 128), lambda i, j: (i, 0))],
        out_shape=[shape, shape, jax.ShapeDtypeStruct((w_gate.shape[0], 128), jnp.float32)],
        compiler_params=pltpu.CompilerParams(vmem_limit_bytes=60 << 20),
        name="lay_in",
    )(full, w_gate, w_up)


def lay_rows_kernel(full_ref, out_ref):
    n_hi, _, n_ctx, _, rows, columns = full_ref.shape
    for hi in range(n_hi):
        for core in range(2):
            for ctx in range(n_ctx):
                start = (hi * n_ctx + ctx) * rows
                out_ref[core * columns : (core + 1) * columns, start : start + rows] = full_ref[
                    hi, core, ctx, 0
                ].astype(jnp.float32).T


def lay_rows(full):
    n_hi, _, n_ctx, n_shard, rows, columns = full.shape
    n_part = n_hi * n_ctx
    return pl.pallas_call(
        lay_rows_kernel,
        grid=(n_shard,),
        in_specs=[
            pl.BlockSpec((n_hi, 2, n_ctx, 1, rows, columns), lambda j: (0, 0, 0, j, 0, 0))
        ],
        out_specs=pl.BlockSpec((2 * columns, n_part * rows), lambda j: (0, j)),
        out_shape=jax.ShapeDtypeStruct((2 * columns, n_shard * n_part * rows), jnp.float32),
        compiler_params=pltpu.CompilerParams(vmem_limit_bytes=60 << 20),
        name="lay_rows",
    )(full)


def lay_heads_kernel(count, at_ref, *refs):
    mine, theirs = refs[:count], refs[count : 2 * count]
    wq_ref, wk_ref, wv_ref, dq_ref, dk_ref, dv_ref, d_out_ref, sums_ref, gains_ref = refs[
        2 * count :
    ]
    q_cols, kv_cols = wq_ref.shape[1] // 2, wk_ref.shape[1] // 2
    out_rows = d_out_ref.shape[0] // 2
    rows = wq_ref.shape[0] // count
    gains = mine[0][0, rows:, :].astype(jnp.float32) + theirs[0][0, rows:, :].astype(jnp.float32)
    add_sums(pl.program_id(0), gains_ref, gains)

    @pl.when(pl.program_id(0) == 0)
    def _():
        sums_ref[...] = jnp.zeros_like(sums_ref)

    for k in range(count):
        part = lax.rem(at_ref[0] - k + count, count)
        here = pl.ds(pl.multiple_of(part * rows, rows), rows)
        total = sums_ref[here, :]
        for core, full_ref in ((at_ref[1], mine[k]), (1 - at_ref[1], theirs[k])):
            full = full_ref[0, :rows].astype(jnp.float32)
            start = 0
            for weight_ref, grad_ref, columns in (
                (wq_ref, dq_ref, q_cols),
                (wk_ref, dk_ref, kv_cols),
                (wv_ref, dv_ref, kv_cols),
            ):
                grad = full[:, start : start + columns]
                span = pl.ds(pl.multiple_of(core * columns, 128), columns)
                grad_ref[here, span] = grad
                total += lane_sums(grad * weight_ref[here, span].astype(jnp.float32))
                start += columns
            d_out_ref[pl.ds(pl.multiple_of(core * out_rows, 128), out_rows), here] = full[
                :, start:
            ].T
        sums_ref[here, :] = total


def lay_heads(at, mine, theirs, w_query, key_weight, value_weight):
    n_part = len(mine)
    n_shard, all_rows, columns = mine[0].shape
    rows = w_query.shape[0] // n_part
    q_cols = w_query.shape[1] // n_shard
    kv_cols = key_weight.shape[1] // n_shard
    out_rows = 2 * columns - q_cols - 2 * kv_cols
    block = pl.BlockSpec((1, all_rows, columns), lambda j, at: (j, 0, 0))

    def spec(width):
        return pl.BlockSpec(
            (n_part * rows, width), lambda j, at: (0, j)
        )

    return pl.pallas_call(
        partial(lay_heads_kernel, n_part),
        grid_spec=pltpu.PrefetchScalarGridSpec(
            num_scalar_prefetch=1,
            grid=(n_shard,),
            in_specs=[block] * (2 * n_part) + [spec(q_cols), spec(kv_cols), spec(kv_cols)],
            out_specs=[
                spec(q_cols),
                spec(kv_cols),
                spec(kv_cols),
                pl.BlockSpec((out_rows, n_part * rows), lambda j, at: (0, j)),
                pl.BlockSpec((n_part * rows, 128), lambda j, at: (0, 0)),
                pl.BlockSpec((all_rows - rows, columns), lambda j, at: (0, 0)),
            ],
        ),
        out_shape=[
            jax.ShapeDtypeStruct(w_query.shape, jnp.float32),
            jax.ShapeDtypeStruct(key_weight.shape, jnp.float32),
            jax.ShapeDtypeStruct(value_weight.shape, jnp.float32),
            jax.ShapeDtypeStruct((out_rows, n_shard * n_part * rows), jnp.float32),
            jax.ShapeDtypeStruct((n_part * rows, 128), jnp.float32),
            jax.ShapeDtypeStruct((all_rows - rows, columns), jnp.float32),
        ],
        compiler_params=pltpu.CompilerParams(vmem_limit_bytes=48 << 20),
        name="lay_heads",
    )(at, *mine, *theirs, w_query, key_weight, value_weight)


def exchange_ring(pieces, rank, count):
    def piece_for(k):
        return lax.dynamic_index_in_dim(pieces, (rank + k) % count, axis=0, keepdims=False)

    return [piece_for(0)] + [
        lax.ppermute(piece_for(k), "shard", [(i, (i + k) % count) for i in range(count)])
        for k in range(1, count)
    ]


def take_columns_kernel(block, at_ref, *refs):
    out_ref = refs[-1]
    at = 0
    for first in range(0, refs[0].shape[1], block or refs[0].shape[1]):
        for ref in refs[:-1]:
            columns = block or ref.shape[1]
            out_ref[0, :, at : at + columns] = ref[:, first : first + columns]
            at += columns


def take_columns(at, n_part, n_shard, weights, block=0):
    rows = weights[0].shape[0] // n_part
    widths = [weight.shape[1] // (2 * n_shard) for weight in weights]
    return pl.pallas_call(
        partial(take_columns_kernel, block),
        grid_spec=pltpu.PrefetchScalarGridSpec(
            num_scalar_prefetch=1,
            grid=(n_shard,),
            in_specs=[
                pl.BlockSpec((rows, width), lambda j, at: (at[0], 2 * j + at[1]))
                for width in widths
            ],
            out_specs=pl.BlockSpec((1, rows, sum(widths)), lambda j, at: (j, 0, 0)),
        ),
        out_shape=jax.ShapeDtypeStruct((n_shard, rows, sum(widths)), weights[0].dtype),
        name="take_columns",
    )(at, *weights)


def lay_order_kernel(at_ref, *refs):
    out_ref = refs[-1]
    count = len(refs) - 1
    rows = refs[0].shape[1]
    for k, ref in enumerate(refs[:-1]):
        owner = lax.rem(at_ref[0] - k + count, count)
        out_ref[pl.ds(pl.multiple_of(owner * rows, rows), rows), :] = ref[0]


def lay_order(at, pieces):
    n_shard, rows, columns = pieces[0].shape
    block = len(pieces) * rows
    return pl.pallas_call(
        lay_order_kernel,
        grid_spec=pltpu.PrefetchScalarGridSpec(
            num_scalar_prefetch=1,
            grid=(n_shard,),
            in_specs=[pl.BlockSpec((1, rows, columns), lambda j, at: (j, 0, 0))] * len(pieces),
            out_specs=pl.BlockSpec((block, columns), lambda j, at: (j, 0)),
        ),
        out_shape=jax.ShapeDtypeStruct((n_shard * block, columns), pieces[0].dtype),
        name="lay_order",
    )(at, *pieces)


def place_kernel(z_ref, *refs):
    out_ref = refs[-1]
    count = len(refs) - 1
    for k, ref in enumerate(refs[:-1]):
        out_ref[lax.rem(z_ref[0] - k + count, count)] = ref[...]


def place(rank, pieces):
    return pl.pallas_call(
        place_kernel,
        grid_spec=pltpu.PrefetchScalarGridSpec(
            num_scalar_prefetch=1,
            grid=(1,),
            in_specs=[pl.BlockSpec(pieces[0].shape, lambda i, z: (0, 0))] * len(pieces),
            out_specs=pl.BlockSpec((len(pieces),) + pieces[0].shape, lambda i, z: (0, 0, 0)),
        ),
        out_shape=jax.ShapeDtypeStruct((len(pieces),) + pieces[0].shape, pieces[0].dtype),
        compiler_params=pltpu.CompilerParams(vmem_limit_bytes=8 << 20),
        name="place",
    )(rank.reshape(1), *pieces)


def norm_kernel(z_ref, tokens_ref, gain_ref, out_ref):
    values = tokens_ref[0].astype(jnp.float32)
    out_ref[...] = (values * recip_rms(values) * gain_ref[...]).astype(jnp.bfloat16)


def norm_group(rank, gathered, gain):
    count, rows, width = gathered.shape
    return pl.pallas_call(
        norm_kernel,
        grid_spec=pltpu.PrefetchScalarGridSpec(
            num_scalar_prefetch=1,
            grid=(count,),
            in_specs=[
                pl.BlockSpec(
                    (1, rows, width), lambda k, z: (lax.rem(z[0] - k + count, count), 0, 0)
                ),
                pl.BlockSpec((1, width), lambda k, z: (0, 0)),
            ],
            out_specs=pl.BlockSpec((rows, width), lambda k, z: (k, 0)),
        ),
        out_shape=jax.ShapeDtypeStruct((count * rows, width), jnp.bfloat16),
        name="norm_group",
    )(rank.reshape(1), gathered, gain.reshape(1, width))


def turn(values, table):
    return pltpu.roll(values, HEAD_SIZE // 2, 1) * table


def project_kernel(n_part, q_cols, at_ref, *refs):
    tokens = refs[:n_part]
    pieces = refs[n_part : 2 * n_part]
    cos_ref, sin_ref, gain_q_ref, gain_k_ref, queries_ref, kv_ref, pre_ref, acc_ref = refs[
        2 * n_part :
    ]
    step = pl.program_id(0)
    columns = acc_ref.shape[1]
    kv_cols = (columns - q_cols) // 2
    total = sum(
        jnp.dot(block[...], piece[0], preferred_element_type=jnp.float32)
        for block, piece in zip(tokens, pieces)
    )
    add_sums(step, acc_ref, total)

    @pl.when(step == pl.num_programs(0) - 1)
    def _():
        rows = 64

        def body(chunk, carry):
            span = pl.ds(pl.multiple_of(chunk * rows, rows), rows)
            cosine, sine = cos_ref[span, :], sin_ref[span, :]
            for start in range(0, q_cols + kv_cols, HEAD_SIZE):
                values = acc_ref[span, start : start + HEAD_SIZE]
                pre_ref[span, start : start + HEAD_SIZE] = values
                gain = gain_q_ref[...] if start < q_cols else gain_k_ref[...]
                scaled = values * recip_rms(values) * gain
                turned = (scaled * cosine + turn(scaled, sine)).astype(jnp.bfloat16)
                if start < q_cols:
                    queries_ref[span, start : start + HEAD_SIZE] = turned
                else:
                    kv_ref[span, start - q_cols : start - q_cols + HEAD_SIZE] = turned
            kv_ref[span, kv_cols:] = acc_ref[span, q_cols + kv_cols :].astype(jnp.bfloat16)
            return carry

        lax.fori_loop(0, acc_ref.shape[0] // rows, body, 0)


def project(at, q_cols, tokens, pieces, cosine, sine, gain_q, gain_k):
    n_part = len(pieces)
    n_shard, slice_rows, columns = pieces[0].shape
    group, width = tokens.shape
    kv_cols = (columns - q_cols) // 2

    def token_spec(k):
        return pl.BlockSpec(
            (group, slice_rows),
            lambda j, at: (0, j * n_part + lax.rem(at[0] - k + n_part, n_part)),
        )

    def whole(shape):
        return pl.BlockSpec(shape, lambda j, at: (0, 0))

    head = (1, HEAD_SIZE)
    return pl.pallas_call(
        partial(project_kernel, n_part, q_cols),
        grid_spec=pltpu.PrefetchScalarGridSpec(
            num_scalar_prefetch=1,
            grid=(n_shard,),
            in_specs=[token_spec(k) for k in range(n_part)]
            + [pl.BlockSpec((1, slice_rows, columns), lambda j, at: (j, 0, 0))] * n_part
            + [whole(cosine.shape), whole(sine.shape), whole(head), whole(head)],
            out_specs=[
                whole((group, q_cols)),
                whole((group, 2 * kv_cols)),
                whole((group, q_cols + kv_cols)),
            ],
            scratch_shapes=[pltpu.VMEM((group, columns), jnp.float32)],
        ),
        out_shape=[
            jax.ShapeDtypeStruct((group, q_cols), jnp.bfloat16),
            jax.ShapeDtypeStruct((group, 2 * kv_cols), jnp.bfloat16),
            jax.ShapeDtypeStruct((group, q_cols + kv_cols), jnp.float32),
        ],
        compiler_params=pltpu.CompilerParams(vmem_limit_bytes=20 << 20),
        name="project",
    )(
        at,
        *([tokens] * n_part),
        *pieces,
        cosine,
        sine,
        gain_q.reshape(head),
        gain_k.reshape(head),
    )


def head_probs(start, q_pos_ref, k_pos_ref, query, keys):
    scores = [
        lax.dot_general(
            query, key, (((1,), (1,)), ((), ())), preferred_element_type=jnp.float32
        )
        for key in keys
    ]
    scores = jnp.concatenate(scores, axis=1) * HEAD_SIZE ** (-0.5)
    q_pos, k_pos = q_pos_ref[...], k_pos_ref[...]
    inside_q = (q_pos >= start) & (q_pos < start + PIC)
    inside_k = (k_pos >= start) & (k_pos < start + PIC)
    allowed = (k_pos <= q_pos) | (inside_q & inside_k)
    scores = jnp.where(allowed, scores, -1e30)
    powers = jnp.exp(scores - jnp.max(scores, axis=1, keepdims=True))
    return powers / jnp.sum(powers, axis=1, keepdims=True)


def attend_kernel(n_ctx, core, starts_ref, *refs):
    kv_refs = refs[:n_ctx]
    queries_ref, q_pos_ref, k_pos_ref, mixed_ref = refs[n_ctx:]
    block = queries_ref.shape
    tokens = block[1] * block[3]
    start = starts_ref[core, pl.program_id(0)]
    queries = queries_ref[...].reshape(tokens, block[4])
    kv = [ref[...].reshape(tokens, ref.shape[4]) for ref in kv_refs]
    kv_cols = kv[0].shape[1] // 2
    group_width = block[4] // kv_cols
    out = []
    for head in range(block[4] // HEAD_SIZE):
        key_start = head // group_width * HEAD_SIZE
        query = queries[:, head * HEAD_SIZE : (head + 1) * HEAD_SIZE]
        keys = [part[:, key_start : key_start + HEAD_SIZE] for part in kv]
        values = [
            part[:, kv_cols + key_start : kv_cols + key_start + HEAD_SIZE] for part in kv
        ]
        probs = head_probs(start, q_pos_ref, k_pos_ref, query, keys).astype(jnp.bfloat16)
        mixed = sum(
            jnp.dot(
                probs[:, i * tokens : (i + 1) * tokens], part, preferred_element_type=jnp.float32
            )
            for i, part in enumerate(values)
        )
        out.append(mixed.astype(jnp.bfloat16))
    mixed_ref[...] = jnp.concatenate(out, axis=1).reshape(mixed_ref.shape)


def sequence_view(values, count, micro, rows):
    return values.reshape(1, count, micro, rows, values.shape[-1])


def attend(core, starts, count, micro, rows, queries, kv_parts, q_pos, k_pos):
    n_ctx = len(kv_parts)

    def spec(columns):
        return pl.BlockSpec((1, count, 1, rows, columns), lambda m, s: (0, 0, m, 0, 0))

    view = partial(sequence_view, count=count, micro=micro, rows=rows)
    columns = queries.shape[1]
    mixed = pl.pallas_call(
        partial(attend_kernel, n_ctx, core),
        grid_spec=pltpu.PrefetchScalarGridSpec(
            num_scalar_prefetch=1,
            grid=(micro,),
            in_specs=[spec(kv_parts[0].shape[1])] * n_ctx
            + [
                spec(columns),
                pl.BlockSpec(q_pos.shape, lambda m, s: (0, 0)),
                pl.BlockSpec(k_pos.shape, lambda m, s: (0, 0)),
            ],
            out_specs=spec(columns),
        ),
        out_shape=jax.ShapeDtypeStruct(view(queries).shape, jnp.bfloat16),
        compiler_params=pltpu.CompilerParams(vmem_limit_bytes=16 << 20),
        name="attend",
    )(starts, *[view(part) for part in kv_parts], view(queries), q_pos, k_pos)
    return mixed.reshape(queries.shape)


def norm_turn_back(pre, d_turned, cosine, sine, gain):
    recip = recip_rms(pre)
    unit = pre * recip
    d_unit = d_turned * cosine + pltpu.roll(d_turned * sine, HEAD_SIZE // 2, 1)
    d_gain = jnp.sum(d_unit * unit, axis=0, keepdims=True)
    return norm_back(unit, recip, gain, d_unit), d_gain


def attend_back_kernel(n_ctx, core, starts_ref, *refs):
    kv_refs = refs[:n_ctx]
    queries_ref, pre_ref, d_mixed_ref, q_pos_ref, k_pos_ref, cos_ref, sin_ref, gain_ref = refs[
        n_ctx : n_ctx + 8
    ]
    d_queries_ref, sums_ref = refs[n_ctx + 8 : n_ctx + 10]
    d_kv_refs = refs[n_ctx + 10 :]
    block = queries_ref.shape
    tokens = block[1] * block[3]
    start = starts_ref[core, pl.program_id(0)]
    queries = queries_ref[...].reshape(tokens, block[4])
    d_mixed = d_mixed_ref[...].reshape(tokens, block[4])
    pre = pre_ref[...].reshape(tokens, pre_ref.shape[4])
    kv = [ref[...].reshape(tokens, ref.shape[4]) for ref in kv_refs]
    kv_cols = kv[0].shape[1] // 2
    group_width = block[4] // kv_cols
    scale = HEAD_SIZE ** (-0.5)
    down = (((0,), (0,)), ((), ()))
    across = (((1,), (1,)), ((), ()))
    f32 = jnp.float32
    d_queries, sums = [], 0.0
    d_keys, d_values = {}, {}
    for head in range(block[4] // HEAD_SIZE):
        key_start = head // group_width * HEAD_SIZE
        span = slice(head * HEAD_SIZE, (head + 1) * HEAD_SIZE)
        query, d_mix = queries[:, span], d_mixed[:, span]
        keys = [part[:, key_start : key_start + HEAD_SIZE] for part in kv]
        values = [
            part[:, kv_cols + key_start : kv_cols + key_start + HEAD_SIZE] for part in kv
        ]
        probs = head_probs(start, q_pos_ref, k_pos_ref, query, keys)
        d_probs = jnp.concatenate(
            [lax.dot_general(d_mix, part, across, preferred_element_type=f32) for part in values],
            axis=1,
        )
        row_dot = jnp.sum(probs * d_probs, axis=1, keepdims=True)
        d_scores = (probs * (d_probs - row_dot)).astype(jnp.bfloat16)
        probs_low = probs.astype(jnp.bfloat16)
        d_query = 0.0
        for i, key in enumerate(keys):
            piece = slice(i * tokens, (i + 1) * tokens)
            d_query += jnp.dot(d_scores[:, piece], key, preferred_element_type=f32)
            d_key = lax.dot_general(d_scores[:, piece], query, down, preferred_element_type=f32)
            d_value = lax.dot_general(
                probs_low[:, piece], d_mix, down, preferred_element_type=f32
            )
            at = (i, key_start)
            d_keys[at] = d_keys.get(at, 0.0) + d_key * scale
            d_values[at] = d_values.get(at, 0.0) + d_value
        d_pre, d_gain = norm_turn_back(
            pre[:, span],
            d_query * scale,
            cos_ref[...].reshape(tokens, HEAD_SIZE),
            sin_ref[...].reshape(tokens, HEAD_SIZE),
            gain_ref[...],
        )
        d_queries.append(d_pre.astype(jnp.bfloat16))
        sums += d_gain
    d_queries_ref[...] = jnp.concatenate(d_queries, axis=1).reshape(d_queries_ref.shape)
    for i, ref in enumerate(d_kv_refs):
        parts = [d_keys[at] for at in sorted(d_keys) if at[0] == i]
        parts += [d_values[at] for at in sorted(d_values) if at[0] == i]
        ref[...] = jnp.concatenate(parts, axis=1).astype(ref.dtype).reshape(ref.shape)
    add_sums(pl.program_id(0), sums_ref, jnp.broadcast_to(sums, sums_ref.shape))


def attend_back(
    core, starts, count, micro, rows, queries, pre, kv_parts, d_mixed, q_pos, k_pos, cosine, sine, gain
):
    n_ctx = len(kv_parts)
    view = partial(sequence_view, count=count, micro=micro, rows=rows)

    def spec(columns):
        return pl.BlockSpec((1, count, 1, rows, columns), lambda m, s: (0, 0, m, 0, 0))

    def whole(values):
        return pl.BlockSpec(values.shape, lambda m, s: (0, 0))

    columns, kv_columns = queries.shape[1], kv_parts[0].shape[1]
    gain = gain.reshape(1, HEAD_SIZE)
    view_shape = view(d_mixed).shape
    outs = pl.pallas_call(
        partial(attend_back_kernel, n_ctx, core),
        grid_spec=pltpu.PrefetchScalarGridSpec(
            num_scalar_prefetch=1,
            grid=(micro,),
            in_specs=[spec(kv_columns)] * n_ctx
            + [spec(columns), spec(pre.shape[1]), spec(columns)]
            + [whole(q_pos), whole(k_pos), spec(HEAD_SIZE), spec(HEAD_SIZE), whole(gain)],
            out_specs=[spec(columns), pl.BlockSpec((8, HEAD_SIZE), lambda m, s: (0, 0))]
            + [spec(kv_columns)] * n_ctx,
        ),
        out_shape=[
            jax.ShapeDtypeStruct(view_shape, jnp.bfloat16),
            jax.ShapeDtypeStruct((8, HEAD_SIZE), jnp.float32),
        ]
        + [
            jax.ShapeDtypeStruct(
                view_shape[:-1] + (kv_columns,), jnp.float32 if i == 0 else jnp.bfloat16
            )
            for i in range(n_ctx)
        ],
        compiler_params=pltpu.CompilerParams(vmem_limit_bytes=24 << 20),
        name="attend_back",
    )(
        starts,
        *[view(part) for part in kv_parts],
        view(queries),
        view(pre),
        view(d_mixed),
        q_pos,
        k_pos,
        view(cosine),
        view(sine),
        gain,
    )
    flat = [values.reshape(d_mixed.shape[0], -1) for values in outs[:1] + outs[2:]]
    return flat[0], outs[1][0], flat[1:]


def keys_back_kernel(n_got, q_cols, *refs):
    d_q_ref, own_ref = refs[:2]
    got_refs = refs[2 : 2 + n_got]
    pre_ref, cos_ref, sin_ref, gain_ref, out_ref, sums_ref = refs[2 + n_got :]
    total = own_ref[...]
    for ref in got_refs:
        total += ref[...].astype(jnp.float32)
    kv_cols = total.shape[1] // 2
    out_ref[:, :q_cols] = d_q_ref[...]
    out_ref[:, q_cols + kv_cols :] = total[:, kv_cols:].astype(jnp.bfloat16)
    sums = 0.0
    for start in range(0, kv_cols, HEAD_SIZE):
        span = slice(start, start + HEAD_SIZE)
        at = slice(q_cols + start, q_cols + start + HEAD_SIZE)
        d_pre, d_gain = norm_turn_back(
            pre_ref[:, at], total[:, span], cos_ref[...], sin_ref[...], gain_ref[...]
        )
        out_ref[:, at] = d_pre.astype(jnp.bfloat16)
        sums += d_gain
    sums_ref[...] = jnp.broadcast_to(sums, sums_ref.shape)


def keys_back(d_queries, own, got, pre, cosine, sine, gain):
    rows, q_cols = d_queries.shape
    out, sums = pl.pallas_call(
        partial(keys_back_kernel, len(got), q_cols),
        out_shape=[
            jax.ShapeDtypeStruct((rows, q_cols + own.shape[1]), jnp.bfloat16),
            jax.ShapeDtypeStruct((8, HEAD_SIZE), jnp.float32),
        ],
        name="keys_back",
    )(d_queries, own, *got, pre, cosine, sine, gain.reshape(1, HEAD_SIZE))
    return out, sums[0]


def head_gradients_kernel(count, at_ref, *refs):
    normed, branch = refs[: 2 * count], refs[2 * count : 4 * count]
    d_qkv, mixed = refs[4 * count : 4 * count + 2], refs[4 * count + 2 : 4 * count + 4]
    gains_ref = refs[4 * count + 4]
    down = (((0,), (0,)), ((), ()))
    slice_rows = normed[0].shape[1]
    for k, out_ref in enumerate(refs[4 * count + 5 :]):
        split = d_qkv[0].shape[1]
        out_ref[0, slice_rows:, :] = gains_ref[...]
        for columns, left, right in (
            (slice(0, split), normed, d_qkv),
            (slice(split, out_ref.shape[2]), branch, mixed),
        ):
            out_ref[0, :slice_rows, columns] = sum(
                lax.dot_general(
                    left[core * count + k][...],
                    right[core][...],
                    down,
                    preferred_element_type=jnp.float32,
                )
                for core in range(2)
            ).astype(jnp.bfloat16)


def head_gradients(at, n_part, n_shard, normed, d_branch, d_qkv, mixed, gains):
    rows, width = normed[0].shape
    slice_rows = width // (n_part * n_shard)
    columns = d_qkv[0].shape[1] + mixed[0].shape[1]

    def spec(k):
        return pl.BlockSpec(
            (rows, slice_rows),
            lambda j, at: (0, j * n_part + lax.rem(at[0] - k + n_part, n_part)),
        )

    def whole(values):
        return pl.BlockSpec(values.shape, lambda j, at: (0, 0))

    specs = [spec(k) for k in range(n_part)] * 2
    out_rows = slice_rows + gains.shape[0]
    out = pl.BlockSpec((1, out_rows, columns), lambda j, at: (j, 0, 0))
    return pl.pallas_call(
        partial(head_gradients_kernel, n_part),
        grid_spec=pltpu.PrefetchScalarGridSpec(
            num_scalar_prefetch=1,
            grid=(n_shard,),
            in_specs=specs + specs + [whole(values) for values in d_qkv + mixed + (gains,)],
            out_specs=[out] * n_part,
        ),
        out_shape=[jax.ShapeDtypeStruct((n_shard, out_rows, columns), jnp.bfloat16)] * n_part,
        compiler_params=pltpu.CompilerParams(vmem_limit_bytes=24 << 20),
        name="head_gradients",
    )(
        at,
        *[normed[0]] * n_part,
        *[normed[1]] * n_part,
        *[d_branch[0]] * n_part,
        *[d_branch[1]] * n_part,
        *d_qkv,
        *mixed,
        gains,
    )


def product_kernel(groups, has_got, *refs):
    count = sum(n for n, _ in groups)
    lefts, rights, rest = refs[:count], refs[count : 2 * count], refs[2 * count :]
    if has_got:
        got_ref, rest = rest[0], rest[1:]
    rows = rest[0].shape[1]
    at = 0
    for group, (n, contract) in enumerate(groups):
        total = sum(
            lax.dot_general(
                left[...],
                right[...],
                (((1,), (contract,)), ((), ())),
                preferred_element_type=jnp.float32,
            )
            for left, right in zip(lefts[at : at + n], rights[at : at + n])
        )
        at += n
        if has_got:
            total = total + got_ref[group].astype(jnp.float32)
        for k, ref in enumerate(rest):
            ref[group] = total[k * rows : (k + 1) * rows].astype(ref.dtype)


def product(groups, dtype=jnp.bfloat16, got=None, split=1):
    rows = groups[0][0][0].shape[0]
    columns = groups[0][1].shape[1 - groups[0][2]]
    block = 512 if columns % 512 == 0 else 256
    left_specs, right_specs, lefts, rights = [], [], [], []

    def right_spec(contract, depth, k):
        if contract:
            return pl.BlockSpec((block, depth), lambda j: (j, k))
        return pl.BlockSpec((depth, block), lambda j: (k, j))

    for terms, right, contract in groups:
        for k, term in enumerate(terms):
            depth = term.shape[1]
            left_specs.append(pl.BlockSpec((rows, depth), lambda j: (0, 0)))
            right_specs.append(right_spec(contract, depth, k))
            lefts.append(term)
            rights.append(right)
    n = len(groups)
    in_specs, args = left_specs + right_specs, lefts + rights
    if got is not None:
        in_specs = in_specs + [pl.BlockSpec((n, rows, block), lambda j: (0, 0, j))]
        args = args + [got]
    dtypes = [dtype] if got is None else [jnp.float32] + [jnp.bfloat16] * (split - 1)
    outs = pl.pallas_call(
        partial(
            product_kernel,
            [(len(terms), contract) for terms, _, contract in groups],
            got is not None,
        ),
        grid=(columns // block,),
        in_specs=in_specs,
        out_specs=[pl.BlockSpec((n, rows // split, block), lambda j: (0, 0, j))] * split,
        out_shape=[jax.ShapeDtypeStruct((n, rows // split, columns), kind) for kind in dtypes],
        compiler_params=pltpu.CompilerParams(vmem_limit_bytes=24 << 20),
        name="product",
    )(*args)
    return outs if got is not None else outs[0]


def ffn_gradients_kernel(*refs):
    ffn, cot, d_pre, inner = (refs[2 * i : 2 * i + 2] for i in range(4))
    out_ref = refs[8]
    down = (((0,), (0,)), ((), ()))
    start = 0
    for left, right in ((ffn, d_pre), (cot, inner)):
        stop = start + right[0].shape[1]
        out_ref[0, :, start:stop] = sum(
            lax.dot_general(
                left[core][...], right[core][...], down, preferred_element_type=jnp.float32
            )
            for core in range(2)
        ).astype(jnp.bfloat16)
        start = stop


def ffn_gradients(n_shard, ffn_in, cot, d_pre, inner):
    rows, width = ffn_in[0].shape
    ff = inner[0].shape[1]
    block = 256
    per = width // (n_shard * block)
    left = pl.BlockSpec((rows, block), lambda j: (0, j))
    wide = pl.BlockSpec((rows, 2 * ff), lambda j: (0, 0))
    narrow = pl.BlockSpec((rows, ff), lambda j: (0, 0))
    return pl.pallas_call(
        ffn_gradients_kernel,
        grid=(width // block,),
        in_specs=[left] * 4 + [wide] * 2 + [narrow] * 2,
        out_specs=pl.BlockSpec((1, block, 3 * ff), lambda j: (j // per, j % per, 0)),
        out_shape=jax.ShapeDtypeStruct((n_shard, width // n_shard, 3 * ff), jnp.bfloat16),
        compiler_params=pltpu.CompilerParams(vmem_limit_bytes=50 << 20),
        name="ffn_gradients",
    )(*ffn_in, *cot, *d_pre, *inner)


def reorder_kernel(z_ref, in_ref, out_ref):
    out_ref[...] = in_ref[0]


def ring_order(rank, gathered):
    count, rows, width = gathered.shape
    return pl.pallas_call(
        reorder_kernel,
        grid_spec=pltpu.PrefetchScalarGridSpec(
            num_scalar_prefetch=1,
            grid=(count,),
            in_specs=[
                pl.BlockSpec(
                    (1, rows, width), lambda k, z: (lax.rem(z[0] - k + count, count), 0, 0)
                )
            ],
            out_specs=pl.BlockSpec((rows, width), lambda k, z: (k, 0)),
        ),
        out_shape=jax.ShapeDtypeStruct((count * rows, width), gathered.dtype),
        name="ring_order",
    )(rank.reshape(1), gathered)


def inner_kernel(ffn_ref, weight_ref, d_inner_ref, inner_ref, d_pre_ref):
    pre = jnp.dot(ffn_ref[...], weight_ref[...], preferred_element_type=jnp.float32)
    gate_pre, up_pre = pre[:, :FF_BLOCK], pre[:, FF_BLOCK:]
    d_inner = d_inner_ref[...]
    sigma = jax.nn.sigmoid(gate_pre)
    act_gate = gate_pre * sigma
    inner_ref[...] = (act_gate * up_pre).astype(jnp.bfloat16)
    d_gate = d_inner * up_pre * sigma * (1.0 + gate_pre * (1.0 - sigma))
    d_pre_ref[:, :FF_BLOCK] = d_gate.astype(jnp.bfloat16)
    d_pre_ref[:, FF_BLOCK:] = (d_inner * act_gate).astype(jnp.bfloat16)


def inner_parts(ffn_in, w_in, d_inner):
    rows, width = ffn_in.shape
    ff = w_in.shape[1] // 2
    narrow = pl.BlockSpec((rows, FF_BLOCK), lambda j: (0, j))
    wide = pl.BlockSpec((rows, 2 * FF_BLOCK), lambda j: (0, j))
    return pl.pallas_call(
        inner_kernel,
        grid=(ff // FF_BLOCK,),
        in_specs=[
            pl.BlockSpec((rows, width), lambda j: (0, 0)),
            pl.BlockSpec((width, 2 * FF_BLOCK), lambda j: (0, j)),
            narrow,
        ],
        out_specs=[narrow, wide],
        out_shape=[
            jax.ShapeDtypeStruct((rows, ff), jnp.bfloat16),
            jax.ShapeDtypeStruct((rows, 2 * ff), jnp.bfloat16),
        ],
        compiler_params=pltpu.CompilerParams(vmem_limit_bytes=20 << 20),
        name="inner_parts",
    )(ffn_in, w_in, d_inner)


def grouped_shards(
    n_hi,
    n_shard,
    n_ctx,
    tokens,
    span_starts,
    cotangent,
    w_query,
    key_weight,
    value_weight,
    w_out,
    attn_gain,
    query_gain,
    key_gain,
    w_gate,
    w_up,
    w_down,
    ffn_gain,
):
    bf16 = jnp.bfloat16
    f32 = jnp.float32
    z = lax.axis_index("shard")
    x = lax.axis_index("ctx")
    c = lax.axis_index("core")
    part = lax.axis_index(("hi", "ctx"))
    n_part = n_hi * n_ctx
    micro, _, rows, width = tokens.shape
    own = micro * rows
    group = n_shard * own
    n_tp = 2 * n_shard
    kv_local = KEY_VALUE_HEADS // n_tp
    q_local = QUERY_HEADS // n_tp
    group_width = QUERY_HEADS // KEY_VALUE_HEADS
    q_cols = q_local * HEAD_SIZE
    kv_cols = kv_local * HEAD_SIZE
    ff = w_down.shape[0] // 2

    slice_rows = w_query.shape[0] // n_part
    def exchange(pieces):
        return lax.all_to_all(pieces, "shard", 0, 0, tiled=True)

    def gather_plane(values):
        full = lax.all_gather(values, ("hi", "core", "ctx"), axis=0)
        return full.reshape((n_hi, 2, n_ctx) + values.shape)

    own_tokens = tokens.reshape(own, width)
    own_cot = cotangent.reshape(own, width)
    at = jnp.stack([part, c, z])
    gathered = lax.all_gather(own_tokens, "shard", axis=0)
    pieces_qkv = take_columns(at, n_part, n_shard, (w_query, key_weight, value_weight))
    pieces_in = take_columns(at, n_part, n_shard, (w_gate, w_up), FF_BLOCK)
    gain_sizes = (attn_gain.shape[0], query_gain.shape[0], key_gain.shape[0], ffn_gain.shape[0])
    gains = after(jnp.concatenate([attn_gain, query_gain, key_gain, ffn_gain]), pieces_qkv)
    gains = from_ring(gains, "shard", n_shard)
    starts = after(span_starts.reshape(micro), pieces_qkv)
    starts = jnp.stack([starts, swap(starts, "core")])
    got_qkv = after(exchange(pieces_qkv), pieces_in, gains, starts)
    gains = in_order(gains, z).astype(f32)
    w_out_rows = lax.dynamic_slice_in_dim(w_out, c * q_cols, q_cols, axis=0)
    w_down_rows = lax.dynamic_slice_in_dim(w_down, c * ff, ff, axis=0)
    ring_qkv = from_ring(got_qkv, ("hi", "ctx"), n_part)
    gathered = after(gathered, ring_qkv, gains, starts)
    ends = [0]
    for size in gain_sizes:
        ends.append(ends[-1] + size)
    gain_attn, gain_query, gain_key, gain_ffn = [
        gains[:, ends[i] : ends[i + 1]].reshape(-1) for i in range(4)
    ]

    blocks = jnp.arange(n_shard, dtype=jnp.int32)
    owners = (z - blocks) % n_shard

    def positions(ctx_rank):
        start = (owners * n_ctx + ctx_rank) * rows
        return (start[:, None] + jnp.arange(rows, dtype=jnp.int32)[None, :]).reshape(-1)

    query_pos = positions(x)
    key_pos = jnp.concatenate([positions((x - k) % n_ctx) for k in range(n_ctx)])
    cosine, sine = (table[:, 0, :] for table in spin_tables(query_pos))
    sine = jnp.where(jnp.arange(HEAD_SIZE) < HEAD_SIZE // 2, -1.0, 1.0) * sine

    def by_row(table):
        table = table.reshape(n_shard, 1, rows, HEAD_SIZE)
        return jnp.broadcast_to(table, (n_shard, micro, rows, HEAD_SIZE)).reshape(group, HEAD_SIZE)

    cosine, sine = by_row(cosine), by_row(sine)
    query_pos = query_pos[:, None]
    key_pos = key_pos[None, :]
    order = (n_shard, micro, rows)

    normed_mine = norm_group(z, gathered, gain_attn)
    normed_theirs = swap(normed_mine, "core")
    got_in = exchange_ring(after(pieces_in, gathered), z, n_shard)
    cot_all = lax.all_gather(after(own_cot, gathered), "shard", axis=0)
    turns = (cosine, sine, gain_query, gain_key)
    q_mine, kv_mine, pre_mine = project(at, q_cols, normed_mine, ring_qkv, *turns)
    q_theirs, kv_theirs, pre_theirs = project(
        at, q_cols, after(normed_theirs, kv_mine), ring_qkv, *turns
    )
    kv_parts = from_ring(jnp.concatenate([kv_mine, kv_theirs], axis=0), "ctx", n_ctx)
    kv_mine_parts = [values[:group] for values in kv_parts]
    kv_theirs_parts = [values[group:] for values in kv_parts]
    w_qkv = lay_order(at, after(ring_qkv, kv_theirs))
    mixed_mine = attend(
        0, starts, *order, after(q_mine, w_qkv), kv_mine_parts, query_pos, key_pos
    )
    mixed_theirs = attend(
        1, starts, *order, after(q_theirs, mixed_mine), kv_theirs_parts, query_pos, key_pos
    )
    def core_sum(mine, theirs, right, contract):
        got = swap(product([(theirs, right, contract)]), "core")
        pieces = product([(mine, right, contract)], got=got, split=n_shard)
        return [piece[0] for piece in pieces]

    branch_sent = core_sum([mixed_mine], [mixed_theirs], w_out_rows, 0)
    hidden_in = own_tokens.astype(f32)
    got_in = place(z, after(got_in, branch_sent))
    cot_all = after(cot_all, got_in)
    w_in = lax.all_gather(after(got_in, cot_all), ("hi", "ctx"), axis=1, tiled=True)
    w_in = w_in.reshape(width, -1)
    cot_mine = ring_order(z, cot_all)
    cot_theirs = swap(cot_mine, "core")
    branch_terms = send_terms(branch_sent, "shard", n_shard)
    middle = hidden_in + sum_terms(after(branch_terms, cot_mine))

    recip_m = recip_rms(middle)
    unit_m = middle * recip_m
    ffn_own = (unit_m * gain_ffn).astype(bf16)
    ffn_ring = from_ring(ffn_own, "shard", n_shard)
    d_inner_mine = product([([after(cot_mine, ffn_own)], w_down_rows, 1)], f32)[0]
    d_inner_theirs = product([([after(cot_theirs, d_inner_mine)], w_down_rows, 1)], f32)[0]
    ffn_mine = jnp.concatenate(after(ffn_ring, d_inner_theirs, w_in), axis=0)
    ffn_theirs = swap(ffn_mine, "core")
    inner_mine, d_pre_mine = inner_parts(ffn_mine, w_in, d_inner_mine)
    inner_theirs, d_pre_theirs = inner_parts(
        after(ffn_theirs, inner_mine), w_in, d_inner_theirs
    )
    grad_in = ffn_gradients(
        n_shard,
        (ffn_mine, ffn_theirs),
        (cot_mine, cot_theirs),
        (d_pre_mine, d_pre_theirs),
        (inner_mine, inner_theirs),
    )
    part_in = lax.psum_scatter(grad_in, ("hi", "ctx"), scatter_dimension=1, tiled=True)
    d_ffn_sent = core_sum([d_pre_mine], [after(d_pre_theirs, grad_in)], w_in, 1)
    d_ffn_in = sum_terms(send_terms(d_ffn_sent, "shard", n_shard))
    d_middle = own_cot.astype(f32) + norm_back(unit_m, recip_m, gain_ffn, d_ffn_in)

    d_branch_own = d_middle.astype(bf16)
    branch_ring = from_ring(d_branch_own, "shard", n_shard)
    branch_mine, part_in = lax.optimization_barrier((jnp.concatenate(branch_ring, axis=0), part_in))
    branch_theirs = swap(branch_mine, "core")
    d_mixed_mine = product([([branch_mine], w_out_rows, 1)])[0]
    tables = (query_pos, key_pos, cosine, sine, gain_query)
    d_q_mine, gain_q_mine, d_kv_mine = attend_back(
        0, starts, *order, q_mine, pre_mine, kv_mine_parts, d_mixed_mine, *tables
    )
    d_mixed_theirs = product([([after(branch_theirs, d_q_mine)], w_out_rows, 1)])[0]
    d_q_theirs, gain_q_theirs, d_kv_theirs = attend_back(
        1, starts, *order, q_theirs, pre_theirs, kv_theirs_parts, d_mixed_theirs, *tables
    )

    sent_in = exchange_ring(part_in[..., : 2 * ff], z, n_shard)
    full_down = gather_plane(part_in[..., 2 * ff :])

    def keys_gradient(d_queries, d_kv, pre, *others):
        got = [
            lax.ppermute(d_kv[n_ctx - k], "ctx", [(i, (i + k) % n_ctx) for i in range(n_ctx)])
            for k in range(1, n_ctx)
        ]
        got = [after(values, *others) for values in got]
        return keys_back(d_queries, d_kv[0], got, pre, cosine, sine, gain_key)

    d_qkv_mine, gain_k_mine = keys_gradient(d_q_mine, d_kv_mine, pre_mine, d_q_theirs)
    d_qkv_theirs, gain_k_theirs = keys_gradient(
        d_q_theirs, d_kv_theirs, pre_theirs, d_qkv_mine
    )
    sent_in = place(z, after(sent_in, d_qkv_theirs))
    full_in = gather_plane(after(sent_in, full_down))
    qkv_cols = q_cols + 2 * kv_cols
    head_columns = qkv_cols + q_cols
    head_gains = jnp.concatenate([gain_q_mine + gain_q_theirs, gain_k_mine + gain_k_theirs])
    head_gains = jnp.zeros((16, head_columns), f32).at[0, : 2 * HEAD_SIZE].set(head_gains)
    sent = head_gradients(
        at,
        n_part,
        n_shard,
        (normed_mine, normed_theirs),
        (branch_mine, branch_theirs),
        (after(d_qkv_mine, sent_in), d_qkv_theirs),
        (mixed_mine, mixed_theirs),
        head_gains.astype(bf16),
    )
    part_heads = send_terms(sent, ("hi", "ctx"), n_part)
    got = product([([after(d_qkv_theirs, sent)], w_qkv, 1), ([inner_theirs], w_down_rows, 0)])
    last = product(
        [([after(d_qkv_mine, got)], w_qkv, 1), ([inner_mine], w_down_rows, 0)],
        got=swap(got, "core"),
        split=n_shard,
    )
    part_heads = sum_terms(after(part_heads, last)).astype(bf16)
    ring_heads = exchange(part_heads[..., :qkv_cols])
    last = send_terms(after(last, part_heads), "shard", n_shard)
    part_heads = jnp.concatenate([ring_heads, part_heads[..., qkv_cols:]], axis=-1)
    mine_heads = from_ring(part_heads, ("hi", "ctx"), n_part)
    grad_down = lay_rows(after(full_down, part_heads))
    grad_gate, grad_up, ffn_sums = lay_in(after(full_in, grad_down), w_gate, w_up)
    mine_heads = after(mine_heads, grad_gate)
    theirs_heads = [swap(values, "core") for values in mine_heads]
    grad_query, grad_key, grad_value, grad_out, attn_sums, gain_sums = lay_heads(
        at, mine_heads, theirs_heads, w_query, key_weight, value_weight
    )
    last = sum_terms(after(last, mine_heads))
    recip_h = recip_rms(hidden_in)
    unit_h = hidden_in * recip_h
    input_grad = d_middle + norm_back(unit_h, recip_h, gain_attn, last[0])
    result = (middle + last[1]).astype(bf16)
    head_gains = gain_sums[0, : 2 * HEAD_SIZE].reshape(2, HEAD_SIZE)
    head_size = query_gain.shape[0]
    head_gains = lax.dynamic_slice_in_dim(head_gains, z * head_size, head_size, axis=1)
    grad_ffn_gain = jnp.sum(ffn_sums, axis=1) / ffn_gain.astype(f32)
    grad_attn_gain = jnp.sum(attn_sums, axis=1) / attn_gain.astype(f32)

    return (
        result.reshape(tokens.shape),
        input_grad.reshape(tokens.shape),
        grad_query,
        grad_key,
        grad_value,
        grad_out,
        grad_attn_gain,
        head_gains[0],
        head_gains[1],
        grad_gate,
        grad_up,
        grad_down,
        grad_ffn_gain,
    )


def solution(mesh):
    n_rep, n_shard, n_ctx = (mesh.shape[name] for name in ("rep", "shard", "ctx"))
    if n_rep % 2 == 0 and KEY_VALUE_HEADS % (2 * n_shard) == 0:
        mesh = Mesh(
            mesh.devices.reshape(n_rep // 2, 2, n_shard, n_ctx), ("hi", "core", "shard", "ctx")
        )
        rep = ("hi", "core")
        body = partial(grouped_shards, n_rep // 2, n_shard, n_ctx)
    else:
        rep = "rep"
        body = shards_general
    in_specs = (
        P(None, rep, ("shard", "ctx"), None),
        P(None, rep),
        P(None, rep, ("shard", "ctx"), None),
        P("shard", None),
        P("shard", None),
        P("shard", None),
        P("shard", None),
        P("shard"),
        P("shard"),
        P("shard"),
        P("shard", None),
        P("shard", None),
        P("shard", None),
        P("shard"),
    )
    out_specs = (
        P(None, rep, ("shard", "ctx"), None),
        P(None, rep, ("shard", "ctx"), None),
        P("shard", None),
        P("shard", None),
        P("shard", None),
        P("shard", None),
        P("shard"),
        P("shard"),
        P("shard"),
        P("shard", None),
        P("shard", None),
        P("shard", None),
        P("shard"),
    )
    return jax.shard_map(body, mesh=mesh, in_specs=in_specs, out_specs=out_specs, check_vma=False)
```

```python
from functools import partial

import jax
import jax.numpy as jnp
from jax import lax
from jax.experimental import pallas as pl
from jax.experimental.pallas import tpu as pltpu
from jax.sharding import Mesh
from jax.sharding import PartitionSpec as P

QUERY_HEADS = 16
KEY_VALUE_HEADS = 8
HEAD_SIZE = 128
PIC = 256


EPSILON = 1e-06
THETA = 1000000.0
FF_BLOCK = 256


def apply_rotation(values):
    half_width = values.shape[-1] // 2
    return jnp.concatenate([-values[..., half_width:], values[..., :half_width]], axis=-1)


def rotate_back(values):
    half_width = values.shape[-1] // 2
    return jnp.concatenate([values[..., half_width:], -values[..., :half_width]], axis=-1)


def spin_tables(positions):
    inverse = THETA ** (-jnp.arange(HEAD_SIZE // 2, dtype=jnp.float32) * 2.0 / HEAD_SIZE)
    angles = positions.astype(jnp.float32)[:, None] * inverse[None, :]
    cosine_table = jnp.concatenate([jnp.cos(angles), jnp.cos(angles)], axis=-1)[:, None, :]
    sine_values = jnp.concatenate([jnp.sin(angles), jnp.sin(angles)], axis=-1)[:, None, :]
    return (cosine_table, sine_values)


def recip_rms(values):
    return lax.rsqrt(jnp.mean(values * values, axis=-1, keepdims=True) + EPSILON)


def norm_back(unit, recip, gain, d_normed):
    d_unit = d_normed * gain
    return recip * (d_unit - unit * jnp.mean(d_unit * unit, axis=-1, keepdims=True))


def over_rows(left, right):
    return lax.dot_general(
        left, right, (((0,), (0,)), ((), ())), preferred_element_type=jnp.float32
    )


def compared_to(left, right):
    return lax.dot_general(
        left, right, (((1,), (1,)), ((), ())), preferred_element_type=jnp.float32
    )


def attention_set(w_query, key_weight, value_weight, w_out, attn_gain, query_gain, key_gain):
    return (
        lax.all_gather(w_query, "shard", axis=0, tiled=True),
        lax.all_gather(key_weight, "shard", axis=0, tiled=True),
        lax.all_gather(value_weight, "shard", axis=0, tiled=True),
        lax.all_gather(w_out, "shard", axis=0, tiled=True),
        lax.all_gather(attn_gain, "shard", axis=0, tiled=True),
        lax.all_gather(query_gain, "shard", axis=0, tiled=True),
        lax.all_gather(key_gain, "shard", axis=0, tiled=True),
    )


def feedforward_set(w_gate, w_up, w_down, ffn_gain):
    return (
        lax.all_gather(w_gate, "shard", axis=0, tiled=True),
        lax.all_gather(w_up, "shard", axis=0, tiled=True),
        lax.all_gather(w_down, "shard", axis=0, tiled=True),
        lax.all_gather(ffn_gain, "shard", axis=0, tiled=True),
    )


def masked_scores(allowed, q_head, k_head):
    scores = jnp.einsum(
        "tgd,sd->gts", q_head, k_head, preferred_element_type=jnp.float32
    ) * HEAD_SIZE ** (-0.5)
    return jnp.where(allowed, scores, -1e30)


def head_forward(allowed, pieces):
    q_head, k_head, v_head = pieces
    scores = masked_scores(allowed, q_head, k_head)
    highest = jnp.max(scores, axis=-1, keepdims=True)
    log_total = highest + jnp.log(jnp.sum(jnp.exp(scores - highest), axis=-1, keepdims=True))
    probs_low = jnp.exp(scores - log_total).astype(jnp.bfloat16)
    mixed = jnp.einsum("gts,sd->tgd", probs_low, v_head, preferred_element_type=jnp.float32)
    return (mixed, log_total)


def head_backward(allowed, pieces):
    q_head, k_head, v_head, d_mix_head, log_total = pieces
    probs = jnp.exp(masked_scores(allowed, q_head, k_head) - log_total)
    probs_low = probs.astype(jnp.bfloat16)
    d_probs = jnp.einsum("tgd,sd->gts", d_mix_head, v_head, preferred_element_type=jnp.float32)
    d_values = jnp.einsum("gts,tgd->sd", probs_low, d_mix_head, preferred_element_type=jnp.float32)
    row_dot = jnp.sum(probs * d_probs, axis=-1, keepdims=True)
    d_scores = (probs * (d_probs - row_dot)).astype(jnp.bfloat16)
    d_queries = jnp.einsum(
        "gts,sd->tgd", d_scores, k_head, preferred_element_type=jnp.float32
    ) * HEAD_SIZE ** (-0.5)
    d_keys = jnp.einsum(
        "gts,tgd->sd", d_scores, q_head, preferred_element_type=jnp.float32
    ) * HEAD_SIZE ** (-0.5)
    return (d_queries, d_keys, d_values)


def shards_general(
    tokens,
    span_starts,
    cotangent,
    w_query,
    key_weight,
    value_weight,
    w_out,
    attn_gain,
    query_gain,
    key_gain,
    w_gate,
    w_up,
    w_down,
    ffn_gain,
):
    seq_count = lax.axis_size(("shard", "ctx"))
    seq_rank = lax.axis_index(("shard", "ctx"))
    token_rows = tokens.shape[2]
    token_length = token_rows * seq_count
    group_width = QUERY_HEADS // KEY_VALUE_HEADS
    local_pos = seq_rank * token_rows + jnp.arange(token_rows, dtype=jnp.int32)
    key_pos = jnp.arange(token_length, dtype=jnp.int32)
    cosine_table, sine_values = spin_tables(local_pos)
    cos_keys = cosine_table[:, 0, :][None]
    sin_keys = sine_values[:, 0, :][None]
    out_list = []
    grad_list = []
    stored = []
    totals = None
    for micro_index in range(tokens.shape[0]):
        span_start = span_starts[micro_index, 0]
        inside_q = (local_pos >= span_start) & (local_pos < span_start + PIC)
        inside_k = (key_pos >= span_start) & (key_pos < span_start + PIC)
        allowed = (key_pos[None, :] <= local_pos[:, None]) | inside_q[:, None] & inside_k[None, :]
        hidden_in = tokens[micro_index, 0].astype(jnp.float32)
        full_query, full_key, full_value, complete_output, gain_attn, gain_query, gain_key = (
            attention_set(w_query, key_weight, value_weight, w_out, attn_gain, query_gain, key_gain)
        )
        gain_attn = gain_attn.astype(jnp.float32)
        gain_query = gain_query.astype(jnp.float32)
        gain_key = gain_key.astype(jnp.float32)
        recip_h = recip_rms(hidden_in)
        unit_h = hidden_in * recip_h
        normalized_rows = (unit_h * gain_attn).astype(jnp.bfloat16)
        q_pre = jnp.dot(normalized_rows, full_query, preferred_element_type=jnp.float32).reshape(
            token_rows, QUERY_HEADS, HEAD_SIZE
        )
        key_before_rotation = jnp.transpose(
            jnp.dot(normalized_rows, full_key, preferred_element_type=jnp.float32).reshape(
                token_rows, KEY_VALUE_HEADS, HEAD_SIZE
            ),
            (1, 0, 2),
        )
        value_local = jnp.transpose(
            jnp.dot(normalized_rows, full_value, preferred_element_type=jnp.float32)
            .astype(jnp.bfloat16)
            .reshape(token_rows, KEY_VALUE_HEADS, HEAD_SIZE),
            (1, 0, 2),
        )
        recip_q = recip_rms(q_pre)
        unit_query = q_pre * recip_q
        recip_k = recip_rms(key_before_rotation)
        unit_k = key_before_rotation * recip_k
        scaled_q = unit_query * gain_query
        scaled_k = unit_k * gain_key
        query_rows = jnp.transpose(
            (scaled_q * cosine_table + apply_rotation(scaled_q) * sine_values)
            .astype(jnp.bfloat16)
            .reshape(token_rows, KEY_VALUE_HEADS, group_width, HEAD_SIZE),
            (1, 0, 2, 3),
        )
        key_local = (scaled_k * cos_keys + apply_rotation(scaled_k) * sin_keys).astype(jnp.bfloat16)
        key_rows, value_matrix = (
            lax.all_gather(key_local, ("shard", "ctx"), axis=1, tiled=True),
            lax.all_gather(value_local, ("shard", "ctx"), axis=1, tiled=True),
        )
        mixed_split, log_total = lax.map(
            partial(head_forward, allowed), (query_rows, key_rows, value_matrix)
        )
        mixed_heads = (
            jnp.transpose(mixed_split, (1, 0, 2, 3))
            .reshape(token_rows, QUERY_HEADS * HEAD_SIZE)
            .astype(jnp.bfloat16)
        )
        middle = hidden_in + jnp.dot(
            mixed_heads, complete_output, preferred_element_type=jnp.float32
        )
        full_gate, full_up, full_down, gain_ffn = feedforward_set(w_gate, w_up, w_down, ffn_gain)
        gain_ffn = gain_ffn.astype(jnp.float32)
        recip_m = recip_rms(middle)
        unit_m = middle * recip_m
        ffn_in = (unit_m * gain_ffn).astype(jnp.bfloat16)
        gate_pre = jnp.dot(ffn_in, full_gate, preferred_element_type=jnp.float32)
        up_pre = jnp.dot(ffn_in, full_up, preferred_element_type=jnp.float32)
        sigma = jax.nn.sigmoid(gate_pre)
        act_gate = gate_pre * sigma
        inner_act = (act_gate * up_pre).astype(jnp.bfloat16)
        result = middle + jnp.dot(inner_act, full_down, preferred_element_type=jnp.float32)
        out_list.append(result.astype(jnp.bfloat16))
        cot_rows = cotangent[micro_index, 0]
        cot_float = cot_rows.astype(jnp.float32)
        d_inner = compared_to(cot_rows, full_down)
        d_gate = (d_inner * up_pre * sigma * (1.0 + gate_pre * (1.0 - sigma))).astype(jnp.bfloat16)
        d_up = (d_inner * act_gate).astype(jnp.bfloat16)
        d_ffn_in = compared_to(d_gate, full_gate) + compared_to(d_up, full_up)
        ffn_gain_part = jnp.sum(d_ffn_in * unit_m, axis=0)
        d_middle = cot_float + norm_back(unit_m, recip_m, gain_ffn, d_ffn_in)
        branch_gradient = d_middle.astype(jnp.bfloat16)
        d_mixed = jnp.transpose(
            compared_to(branch_gradient, complete_output)
            .astype(jnp.bfloat16)
            .reshape(token_rows, KEY_VALUE_HEADS, group_width, HEAD_SIZE),
            (1, 0, 2, 3),
        )
        d_split_q, d_keys, d_values = lax.map(
            partial(head_backward, allowed),
            (query_rows, key_rows, value_matrix, d_mixed, log_total),
        )
        d_queries = jnp.transpose(d_split_q, (1, 0, 2, 3)).reshape(
            token_rows, QUERY_HEADS, HEAD_SIZE
        )
        d_key_local, d_value_local = (
            lax.psum_scatter(
                d_keys.astype(jnp.bfloat16), ("shard", "ctx"), scatter_dimension=1, tiled=True
            ).astype(jnp.float32),
            lax.psum_scatter(
                d_values.astype(jnp.bfloat16), ("shard", "ctx"), scatter_dimension=1, tiled=True
            ).astype(jnp.float32),
        )
        d_unit_q = d_queries * cosine_table + rotate_back(d_queries * sine_values)
        d_unit_k = d_key_local * cos_keys + rotate_back(d_key_local * sin_keys)
        query_gain_part = jnp.sum(d_unit_q * unit_query, axis=(0, 1))
        key_gain_part = jnp.sum(d_unit_k * unit_k, axis=(0, 1))
        d_q_pre = (
            norm_back(unit_query, recip_q, gain_query, d_unit_q)
            .astype(jnp.bfloat16)
            .reshape(token_rows, QUERY_HEADS * HEAD_SIZE)
        )
        d_k_pre = jnp.transpose(
            norm_back(unit_k, recip_k, gain_key, d_unit_k).astype(jnp.bfloat16), (1, 0, 2)
        ).reshape(token_rows, KEY_VALUE_HEADS * HEAD_SIZE)
        d_v_pre = jnp.transpose(d_value_local.astype(jnp.bfloat16), (1, 0, 2)).reshape(
            token_rows, KEY_VALUE_HEADS * HEAD_SIZE
        )
        d_normed = (
            compared_to(d_q_pre, full_query)
            + compared_to(d_k_pre, full_key)
            + compared_to(d_v_pre, full_value)
        )
        attn_gain_part = jnp.sum(d_normed * unit_h, axis=0)
        grad_list.append(d_middle + norm_back(unit_h, recip_h, gain_attn, d_normed))
        stored.append(
            (
                normalized_rows,
                d_q_pre,
                d_k_pre,
                d_v_pre,
                mixed_heads,
                branch_gradient,
                ffn_in,
                d_gate,
                d_up,
                inner_act,
                cot_rows,
            )
        )
        parts = (attn_gain_part, query_gain_part, key_gain_part, ffn_gain_part)
        if totals is None:
            totals = parts
        else:
            totals = tuple((older + newer for older, newer in zip(totals, parts)))
    joined = [
        jnp.concatenate([saved_set[member] for saved_set in stored], axis=0) for member in range(11)
    ]
    (
        normed_all,
        dq_all,
        dk_all,
        dv_all,
        mixed_all,
        branch_all,
        ffn_all,
        gate_all,
        up_all,
        inner_all,
        cot_all,
    ) = joined
    totals = (
        lax.psum_scatter(
            over_rows(normed_all, dq_all).astype(jnp.bfloat16),
            "shard",
            scatter_dimension=0,
            tiled=True,
        ).astype(jnp.float32),
        lax.psum_scatter(
            over_rows(normed_all, dk_all).astype(jnp.bfloat16),
            "shard",
            scatter_dimension=0,
            tiled=True,
        ).astype(jnp.float32),
        lax.psum_scatter(
            over_rows(normed_all, dv_all).astype(jnp.bfloat16),
            "shard",
            scatter_dimension=0,
            tiled=True,
        ).astype(jnp.float32),
        lax.psum_scatter(
            over_rows(mixed_all, branch_all).astype(jnp.bfloat16),
            "shard",
            scatter_dimension=0,
            tiled=True,
        ).astype(jnp.float32),
        lax.psum_scatter(
            totals[0].astype(jnp.bfloat16), "shard", scatter_dimension=0, tiled=True
        ).astype(jnp.float32),
        lax.psum_scatter(
            totals[1].astype(jnp.bfloat16), "shard", scatter_dimension=0, tiled=True
        ).astype(jnp.float32),
        lax.psum_scatter(
            totals[2].astype(jnp.bfloat16), "shard", scatter_dimension=0, tiled=True
        ).astype(jnp.float32),
        lax.psum_scatter(
            over_rows(ffn_all, gate_all).astype(jnp.bfloat16),
            "shard",
            scatter_dimension=0,
            tiled=True,
        ).astype(jnp.float32),
        lax.psum_scatter(
            over_rows(ffn_all, up_all).astype(jnp.bfloat16),
            "shard",
            scatter_dimension=0,
            tiled=True,
        ).astype(jnp.float32),
        lax.psum_scatter(
            over_rows(inner_all, cot_all).astype(jnp.bfloat16),
            "shard",
            scatter_dimension=0,
            tiled=True,
        ).astype(jnp.float32),
        lax.psum_scatter(
            totals[3].astype(jnp.bfloat16), "shard", scatter_dimension=0, tiled=True
        ).astype(jnp.float32),
    )
    summed = (
        lax.psum(totals[0].astype(jnp.bfloat16), ("rep", "ctx")).astype(jnp.float32),
        lax.psum(totals[1].astype(jnp.bfloat16), ("rep", "ctx")).astype(jnp.float32),
        lax.psum(totals[2].astype(jnp.bfloat16), ("rep", "ctx")).astype(jnp.float32),
        lax.psum(totals[3].astype(jnp.bfloat16), ("rep", "ctx")).astype(jnp.float32),
        lax.psum(totals[4].astype(jnp.bfloat16), ("rep", "ctx")).astype(jnp.float32),
        lax.psum(totals[5].astype(jnp.bfloat16), ("rep", "ctx")).astype(jnp.float32),
        lax.psum(totals[6].astype(jnp.bfloat16), ("rep", "ctx")).astype(jnp.float32),
        lax.psum(totals[7].astype(jnp.bfloat16), ("rep", "ctx")).astype(jnp.float32),
        lax.psum(totals[8].astype(jnp.bfloat16), ("rep", "ctx")).astype(jnp.float32),
        lax.psum(totals[9].astype(jnp.bfloat16), ("rep", "ctx")).astype(jnp.float32),
        lax.psum(totals[10].astype(jnp.bfloat16), ("rep", "ctx")).astype(jnp.float32),
    )
    output = jnp.stack(out_list)[:, None]
    input_grad = jnp.stack(grad_list)[:, None]
    return (
        output,
        input_grad,
        summed[0],
        summed[1],
        summed[2],
        summed[3],
        summed[4],
        summed[5],
        summed[6],
        summed[7],
        summed[8],
        summed[9],
        summed[10],
    )


def from_ring(block, axis, count):
    return [block] + [
        lax.ppermute(block, axis, [(i, (i + k) % count) for i in range(count)])
        for k in range(1, count)
    ]


def send_terms(pieces, axis, count):
    return [pieces[0]] + [
        lax.ppermute(
            pieces[count - k].astype(jnp.bfloat16),
            axis,
            [(i, (i + k) % count) for i in range(count)],
        )
        for k in range(1, count)
    ]


def sum_terms(terms):
    return sum(term.astype(jnp.float32) for term in terms)


def swap(values, axis):
    return lax.ppermute(values, axis, [(0, 1), (1, 0)])


def after(value, *others):
    return lax.optimization_barrier((value,) + others)[0] if others else value


def in_order(blocks, rank):
    count = len(blocks)
    twice = jnp.stack(blocks[::-1] + blocks[:0:-1])
    return lax.dynamic_slice_in_dim(twice, count - 1 - rank, count, axis=0)


def lane_sums(values):
    return sum(
        values[:, start : start + 128] for start in range(0, values.shape[1], 128)
    )


def add_sums(step, sums_ref, values):
    @pl.when(step == 0)
    def _():
        sums_ref[...] = values

    @pl.when(step > 0)
    def _():
        sums_ref[...] += values


def lay_in_kernel(full_ref, gate_ref, up_ref, d_gate_ref, d_up_ref, sums_ref):
    columns = gate_ref.shape[1] // 2
    total = None
    for core in range(2):
        for at in range(0, columns, FF_BLOCK):
            full = full_ref[0, core, 0, 0, :, 2 * at : 2 * (at + FF_BLOCK)].astype(jnp.float32)
            span = slice(core * columns + at, core * columns + at + FF_BLOCK)
            d_gate = full[:, :FF_BLOCK]
            d_up = full[:, FF_BLOCK:]
            d_gate_ref[:, span] = d_gate
            d_up_ref[:, span] = d_up
            both = d_gate * gate_ref[:, span].astype(jnp.float32)
            both = lane_sums(both + d_up * up_ref[:, span].astype(jnp.float32))
            total = both if total is None else total + both
    add_sums(pl.program_id(1), sums_ref, total)


def lay_in(full, w_gate, w_up):
    n_hi, _, n_ctx, n_shard, rows, both = full.shape
    shape = jax.ShapeDtypeStruct(w_gate.shape, jnp.float32)
    block = pl.BlockSpec((rows, both), lambda i, j: (i, j))
    return pl.pallas_call(
        lay_in_kernel,
        grid=(n_hi * n_ctx, n_shard),
        in_specs=[
            pl.BlockSpec(
                (1, 2, 1, 1, rows, both), lambda i, j: (i // n_ctx, 0, i % n_ctx, j, 0, 0)
            ),
            block,
            block,
        ],
        out_specs=[block, block, pl.BlockSpec((rows, 128), lambda i, j: (i, 0))],
        out_shape=[shape, shape, jax.ShapeDtypeStruct((w_gate.shape[0], 128), jnp.float32)],
        compiler_params=pltpu.CompilerParams(vmem_limit_bytes=60 << 20),
        name="lay_in",
    )(full, w_gate, w_up)


def lay_rows_kernel(full_ref, out_ref):
    n_hi, _, n_ctx, _, rows, columns = full_ref.shape
    for hi in range(n_hi):
        for core in range(2):
            for ctx in range(n_ctx):
                start = (hi * n_ctx + ctx) * rows
                out_ref[core * columns : (core + 1) * columns, start : start + rows] = full_ref[
                    hi, core, ctx, 0
                ].astype(jnp.float32).T


def lay_rows(full):
    n_hi, _, n_ctx, n_shard, rows, columns = full.shape
    n_part = n_hi * n_ctx
    return pl.pallas_call(
        lay_rows_kernel,
        grid=(n_shard,),
        in_specs=[
            pl.BlockSpec((n_hi, 2, n_ctx, 1, rows, columns), lambda j: (0, 0, 0, j, 0, 0))
        ],
        out_specs=pl.BlockSpec((2 * columns, n_part * rows), lambda j: (0, j)),
        out_shape=jax.ShapeDtypeStruct((2 * columns, n_shard * n_part * rows), jnp.float32),
        compiler_params=pltpu.CompilerParams(vmem_limit_bytes=60 << 20),
        name="lay_rows",
    )(full)


def lay_heads_kernel(count, at_ref, *refs):
    mine, theirs = refs[:count], refs[count : 2 * count]
    wq_ref, wk_ref, wv_ref, dq_ref, dk_ref, dv_ref, d_out_ref, sums_ref, gains_ref = refs[
        2 * count :
    ]
    q_cols, kv_cols = wq_ref.shape[1] // 2, wk_ref.shape[1] // 2
    out_rows = d_out_ref.shape[0] // 2
    rows = wq_ref.shape[0] // count
    gains = mine[0][0, rows:, :].astype(jnp.float32) + theirs[0][0, rows:, :].astype(jnp.float32)
    add_sums(pl.program_id(0), gains_ref, gains)

    @pl.when(pl.program_id(0) == 0)
    def _():
        sums_ref[...] = jnp.zeros_like(sums_ref)

    for k in range(count):
        part = lax.rem(at_ref[0] - k + count, count)
        here = pl.ds(pl.multiple_of(part * rows, rows), rows)
        total = sums_ref[here, :]
        for core, full_ref in ((at_ref[1], mine[k]), (1 - at_ref[1], theirs[k])):
            full = full_ref[0, :rows].astype(jnp.float32)
            start = 0
            for weight_ref, grad_ref, columns in (
                (wq_ref, dq_ref, q_cols),
                (wk_ref, dk_ref, kv_cols),
                (wv_ref, dv_ref, kv_cols),
            ):
                grad = full[:, start : start + columns]
                span = pl.ds(pl.multiple_of(core * columns, 128), columns)
                grad_ref[here, span] = grad
                total += lane_sums(grad * weight_ref[here, span].astype(jnp.float32))
                start += columns
            d_out_ref[pl.ds(pl.multiple_of(core * out_rows, 128), out_rows), here] = full[
                :, start:
            ].T
        sums_ref[here, :] = total


def lay_heads(at, mine, theirs, w_query, key_weight, value_weight):
    n_part = len(mine)
    n_shard, all_rows, columns = mine[0].shape
    rows = w_query.shape[0] // n_part
    q_cols = w_query.shape[1] // n_shard
    kv_cols = key_weight.shape[1] // n_shard
    out_rows = 2 * columns - q_cols - 2 * kv_cols
    block = pl.BlockSpec((1, all_rows, columns), lambda j, at: (j, 0, 0))

    def spec(width):
        return pl.BlockSpec(
            (n_part * rows, width), lambda j, at: (0, j)
        )

    return pl.pallas_call(
        partial(lay_heads_kernel, n_part),
        grid_spec=pltpu.PrefetchScalarGridSpec(
            num_scalar_prefetch=1,
            grid=(n_shard,),
            in_specs=[block] * (2 * n_part) + [spec(q_cols), spec(kv_cols), spec(kv_cols)],
            out_specs=[
                spec(q_cols),
                spec(kv_cols),
                spec(kv_cols),
                pl.BlockSpec((out_rows, n_part * rows), lambda j, at: (0, j)),
                pl.BlockSpec((n_part * rows, 128), lambda j, at: (0, 0)),
                pl.BlockSpec((all_rows - rows, columns), lambda j, at: (0, 0)),
            ],
        ),
        out_shape=[
            jax.ShapeDtypeStruct(w_query.shape, jnp.float32),
            jax.ShapeDtypeStruct(key_weight.shape, jnp.float32),
            jax.ShapeDtypeStruct(value_weight.shape, jnp.float32),
            jax.ShapeDtypeStruct((out_rows, n_shard * n_part * rows), jnp.float32),
            jax.ShapeDtypeStruct((n_part * rows, 128), jnp.float32),
            jax.ShapeDtypeStruct((all_rows - rows, columns), jnp.float32),
        ],
        compiler_params=pltpu.CompilerParams(vmem_limit_bytes=48 << 20),
        name="lay_heads",
    )(at, *mine, *theirs, w_query, key_weight, value_weight)


def exchange_ring(pieces, rank, count):
    def piece_for(k):
        return lax.dynamic_index_in_dim(pieces, (rank + k) % count, axis=0, keepdims=False)

    return [piece_for(0)] + [
        lax.ppermute(piece_for(k), "shard", [(i, (i + k) % count) for i in range(count)])
        for k in range(1, count)
    ]


def take_columns_kernel(block, at_ref, *refs):
    out_ref = refs[-1]
    at = 0
    for first in range(0, refs[0].shape[1], block or refs[0].shape[1]):
        for ref in refs[:-1]:
            columns = block or ref.shape[1]
            out_ref[0, :, at : at + columns] = ref[:, first : first + columns]
            at += columns


def take_columns(at, n_part, n_shard, weights, block=0):
    rows = weights[0].shape[0] // n_part
    widths = [weight.shape[1] // (2 * n_shard) for weight in weights]
    return pl.pallas_call(
        partial(take_columns_kernel, block),
        grid_spec=pltpu.PrefetchScalarGridSpec(
            num_scalar_prefetch=1,
            grid=(n_shard,),
            in_specs=[
                pl.BlockSpec((rows, width), lambda j, at: (at[0], 2 * j + at[1]))
                for width in widths
            ],
            out_specs=pl.BlockSpec((1, rows, sum(widths)), lambda j, at: (j, 0, 0)),
        ),
        out_shape=jax.ShapeDtypeStruct((n_shard, rows, sum(widths)), weights[0].dtype),
        name="take_columns",
    )(at, *weights)


def lay_order_kernel(at_ref, *refs):
    out_ref = refs[-1]
    count = len(refs) - 1
    rows = refs[0].shape[1]
    for k, ref in enumerate(refs[:-1]):
        owner = lax.rem(at_ref[0] - k + count, count)
        out_ref[pl.ds(pl.multiple_of(owner * rows, rows), rows), :] = ref[0]


def lay_order(at, pieces):
    n_shard, rows, columns = pieces[0].shape
    block = len(pieces) * rows
    return pl.pallas_call(
        lay_order_kernel,
        grid_spec=pltpu.PrefetchScalarGridSpec(
            num_scalar_prefetch=1,
            grid=(n_shard,),
            in_specs=[pl.BlockSpec((1, rows, columns), lambda j, at: (j, 0, 0))] * len(pieces),
            out_specs=pl.BlockSpec((block, columns), lambda j, at: (j, 0)),
        ),
        out_shape=jax.ShapeDtypeStruct((n_shard * block, columns), pieces[0].dtype),
        name="lay_order",
    )(at, *pieces)


def place_kernel(z_ref, *refs):
    out_ref = refs[-1]
    count = len(refs) - 1
    for k, ref in enumerate(refs[:-1]):
        out_ref[lax.rem(z_ref[0] - k + count, count)] = ref[...]


def place(rank, pieces):
    return pl.pallas_call(
        place_kernel,
        grid_spec=pltpu.PrefetchScalarGridSpec(
            num_scalar_prefetch=1,
            grid=(1,),
            in_specs=[pl.BlockSpec(pieces[0].shape, lambda i, z: (0, 0))] * len(pieces),
            out_specs=pl.BlockSpec((len(pieces),) + pieces[0].shape, lambda i, z: (0, 0, 0)),
        ),
        out_shape=jax.ShapeDtypeStruct((len(pieces),) + pieces[0].shape, pieces[0].dtype),
        compiler_params=pltpu.CompilerParams(vmem_limit_bytes=8 << 20),
        name="place",
    )(rank.reshape(1), *pieces)


def norm_kernel(z_ref, tokens_ref, gain_ref, out_ref):
    values = tokens_ref[0].astype(jnp.float32)
    out_ref[...] = (values * recip_rms(values) * gain_ref[...]).astype(jnp.bfloat16)


def norm_group(rank, gathered, gain):
    count, rows, width = gathered.shape
    return pl.pallas_call(
        norm_kernel,
        grid_spec=pltpu.PrefetchScalarGridSpec(
            num_scalar_prefetch=1,
            grid=(count,),
            in_specs=[
                pl.BlockSpec(
                    (1, rows, width), lambda k, z: (lax.rem(z[0] - k + count, count), 0, 0)
                ),
                pl.BlockSpec((1, width), lambda k, z: (0, 0)),
            ],
            out_specs=pl.BlockSpec((rows, width), lambda k, z: (k, 0)),
        ),
        out_shape=jax.ShapeDtypeStruct((count * rows, width), jnp.bfloat16),
        name="norm_group",
    )(rank.reshape(1), gathered, gain.reshape(1, width))


def turn(values, table):
    return pltpu.roll(values, HEAD_SIZE // 2, 1) * table


def project_kernel(n_part, q_cols, at_ref, *refs):
    tokens = refs[:n_part]
    pieces = refs[n_part : 2 * n_part]
    cos_ref, sin_ref, gain_q_ref, gain_k_ref, queries_ref, kv_ref, pre_ref, acc_ref = refs[
        2 * n_part :
    ]
    step = pl.program_id(0)
    columns = acc_ref.shape[1]
    kv_cols = (columns - q_cols) // 2
    total = sum(
        jnp.dot(block[...], piece[0], preferred_element_type=jnp.float32)
        for block, piece in zip(tokens, pieces)
    )
    add_sums(step, acc_ref, total)

    @pl.when(step == pl.num_programs(0) - 1)
    def _():
        rows = 64

        def body(chunk, carry):
            span = pl.ds(pl.multiple_of(chunk * rows, rows), rows)
            cosine, sine = cos_ref[span, :], sin_ref[span, :]
            for start in range(0, q_cols + kv_cols, HEAD_SIZE):
                values = acc_ref[span, start : start + HEAD_SIZE]
                pre_ref[span, start : start + HEAD_SIZE] = values
                gain = gain_q_ref[...] if start < q_cols else gain_k_ref[...]
                scaled = values * recip_rms(values) * gain
                turned = (scaled * cosine + turn(scaled, sine)).astype(jnp.bfloat16)
                if start < q_cols:
                    queries_ref[span, start : start + HEAD_SIZE] = turned
                else:
                    kv_ref[span, start - q_cols : start - q_cols + HEAD_SIZE] = turned
            kv_ref[span, kv_cols:] = acc_ref[span, q_cols + kv_cols :].astype(jnp.bfloat16)
            return carry

        lax.fori_loop(0, acc_ref.shape[0] // rows, body, 0)


def project(at, q_cols, tokens, pieces, cosine, sine, gain_q, gain_k):
    n_part = len(pieces)
    n_shard, slice_rows, columns = pieces[0].shape
    group, width = tokens.shape
    kv_cols = (columns - q_cols) // 2

    def token_spec(k):
        return pl.BlockSpec(
            (group, slice_rows),
            lambda j, at: (0, j * n_part + lax.rem(at[0] - k + n_part, n_part)),
        )

    def whole(shape):
        return pl.BlockSpec(shape, lambda j, at: (0, 0))

    head = (1, HEAD_SIZE)
    return pl.pallas_call(
        partial(project_kernel, n_part, q_cols),
        grid_spec=pltpu.PrefetchScalarGridSpec(
            num_scalar_prefetch=1,
            grid=(n_shard,),
            in_specs=[token_spec(k) for k in range(n_part)]
            + [pl.BlockSpec((1, slice_rows, columns), lambda j, at: (j, 0, 0))] * n_part
            + [whole(cosine.shape), whole(sine.shape), whole(head), whole(head)],
            out_specs=[
                whole((group, q_cols)),
                whole((group, 2 * kv_cols)),
                whole((group, q_cols + kv_cols)),
            ],
            scratch_shapes=[pltpu.VMEM((group, columns), jnp.float32)],
        ),
        out_shape=[
            jax.ShapeDtypeStruct((group, q_cols), jnp.bfloat16),
            jax.ShapeDtypeStruct((group, 2 * kv_cols), jnp.bfloat16),
            jax.ShapeDtypeStruct((group, q_cols + kv_cols), jnp.float32),
        ],
        compiler_params=pltpu.CompilerParams(vmem_limit_bytes=20 << 20),
        name="project",
    )(
        at,
        *([tokens] * n_part),
        *pieces,
        cosine,
        sine,
        gain_q.reshape(head),
        gain_k.reshape(head),
    )


def head_probs(start, q_pos_ref, k_pos_ref, query, keys):
    scores = [
        lax.dot_general(
            query, key, (((1,), (1,)), ((), ())), preferred_element_type=jnp.float32
        )
        for key in keys
    ]
    scores = jnp.concatenate(scores, axis=1) * HEAD_SIZE ** (-0.5)
    q_pos, k_pos = q_pos_ref[...], k_pos_ref[...]
    inside_q = (q_pos >= start) & (q_pos < start + PIC)
    inside_k = (k_pos >= start) & (k_pos < start + PIC)
    allowed = (k_pos <= q_pos) | (inside_q & inside_k)
    scores = jnp.where(allowed, scores, -1e30)
    powers = jnp.exp(scores - jnp.max(scores, axis=1, keepdims=True))
    return powers / jnp.sum(powers, axis=1, keepdims=True)


def attend_kernel(n_ctx, core, starts_ref, *refs):
    kv_refs = refs[:n_ctx]
    queries_ref, q_pos_ref, k_pos_ref, mixed_ref = refs[n_ctx:]
    block = queries_ref.shape
    tokens = block[1] * block[3]
    start = starts_ref[core, pl.program_id(0)]
    queries = queries_ref[...].reshape(tokens, block[4])
    kv = [ref[...].reshape(tokens, ref.shape[4]) for ref in kv_refs]
    kv_cols = kv[0].shape[1] // 2
    group_width = block[4] // kv_cols
    out = []
    for head in range(block[4] // HEAD_SIZE):
        key_start = head // group_width * HEAD_SIZE
        query = queries[:, head * HEAD_SIZE : (head + 1) * HEAD_SIZE]
        keys = [part[:, key_start : key_start + HEAD_SIZE] for part in kv]
        values = [
            part[:, kv_cols + key_start : kv_cols + key_start + HEAD_SIZE] for part in kv
        ]
        probs = head_probs(start, q_pos_ref, k_pos_ref, query, keys).astype(jnp.bfloat16)
        mixed = sum(
            jnp.dot(
                probs[:, i * tokens : (i + 1) * tokens], part, preferred_element_type=jnp.float32
            )
            for i, part in enumerate(values)
        )
        out.append(mixed.astype(jnp.bfloat16))
    mixed_ref[...] = jnp.concatenate(out, axis=1).reshape(mixed_ref.shape)


def sequence_view(values, count, micro, rows):
    return values.reshape(1, count, micro, rows, values.shape[-1])


def attend(core, starts, count, micro, rows, queries, kv_parts, q_pos, k_pos):
    n_ctx = len(kv_parts)

    def spec(columns):
        return pl.BlockSpec((1, count, 1, rows, columns), lambda m, s: (0, 0, m, 0, 0))

    view = partial(sequence_view, count=count, micro=micro, rows=rows)
    columns = queries.shape[1]
    mixed = pl.pallas_call(
        partial(attend_kernel, n_ctx, core),
        grid_spec=pltpu.PrefetchScalarGridSpec(
            num_scalar_prefetch=1,
            grid=(micro,),
            in_specs=[spec(kv_parts[0].shape[1])] * n_ctx
            + [
                spec(columns),
                pl.BlockSpec(q_pos.shape, lambda m, s: (0, 0)),
                pl.BlockSpec(k_pos.shape, lambda m, s: (0, 0)),
            ],
            out_specs=spec(columns),
        ),
        out_shape=jax.ShapeDtypeStruct(view(queries).shape, jnp.bfloat16),
        compiler_params=pltpu.CompilerParams(vmem_limit_bytes=16 << 20),
        name="attend",
    )(starts, *[view(part) for part in kv_parts], view(queries), q_pos, k_pos)
    return mixed.reshape(queries.shape)


def norm_turn_back(pre, d_turned, cosine, sine, gain):
    recip = recip_rms(pre)
    unit = pre * recip
    d_unit = d_turned * cosine + pltpu.roll(d_turned * sine, HEAD_SIZE // 2, 1)
    d_gain = jnp.sum(d_unit * unit, axis=0, keepdims=True)
    return norm_back(unit, recip, gain, d_unit), d_gain


def attend_back_kernel(n_ctx, core, starts_ref, *refs):
    kv_refs = refs[:n_ctx]
    queries_ref, pre_ref, d_mixed_ref, q_pos_ref, k_pos_ref, cos_ref, sin_ref, gain_ref = refs[
        n_ctx : n_ctx + 8
    ]
    d_queries_ref, sums_ref = refs[n_ctx + 8 : n_ctx + 10]
    d_kv_refs = refs[n_ctx + 10 :]
    block = queries_ref.shape
    tokens = block[1] * block[3]
    start = starts_ref[core, pl.program_id(0)]
    queries = queries_ref[...].reshape(tokens, block[4])
    d_mixed = d_mixed_ref[...].reshape(tokens, block[4])
    pre = pre_ref[...].reshape(tokens, pre_ref.shape[4])
    kv = [ref[...].reshape(tokens, ref.shape[4]) for ref in kv_refs]
    kv_cols = kv[0].shape[1] // 2
    group_width = block[4] // kv_cols
    scale = HEAD_SIZE ** (-0.5)
    down = (((0,), (0,)), ((), ()))
    across = (((1,), (1,)), ((), ()))
    f32 = jnp.float32
    d_queries, sums = [], 0.0
    d_keys, d_values = {}, {}
    for head in range(block[4] // HEAD_SIZE):
        key_start = head // group_width * HEAD_SIZE
        span = slice(head * HEAD_SIZE, (head + 1) * HEAD_SIZE)
        query, d_mix = queries[:, span], d_mixed[:, span]
        keys = [part[:, key_start : key_start + HEAD_SIZE] for part in kv]
        values = [
            part[:, kv_cols + key_start : kv_cols + key_start + HEAD_SIZE] for part in kv
        ]
        probs = head_probs(start, q_pos_ref, k_pos_ref, query, keys)
        d_probs = jnp.concatenate(
            [lax.dot_general(d_mix, part, across, preferred_element_type=f32) for part in values],
            axis=1,
        )
        row_dot = jnp.sum(probs * d_probs, axis=1, keepdims=True)
        d_scores = (probs * (d_probs - row_dot)).astype(jnp.bfloat16)
        probs_low = probs.astype(jnp.bfloat16)
        d_query = 0.0
        for i, key in enumerate(keys):
            piece = slice(i * tokens, (i + 1) * tokens)
            d_query += jnp.dot(d_scores[:, piece], key, preferred_element_type=f32)
            d_key = lax.dot_general(d_scores[:, piece], query, down, preferred_element_type=f32)
            d_value = lax.dot_general(
                probs_low[:, piece], d_mix, down, preferred_element_type=f32
            )
            at = (i, key_start)
            d_keys[at] = d_keys.get(at, 0.0) + d_key * scale
            d_values[at] = d_values.get(at, 0.0) + d_value
        d_pre, d_gain = norm_turn_back(
            pre[:, span],
            d_query * scale,
            cos_ref[...].reshape(tokens, HEAD_SIZE),
            sin_ref[...].reshape(tokens, HEAD_SIZE),
            gain_ref[...],
        )
        d_queries.append(d_pre.astype(jnp.bfloat16))
        sums += d_gain
    d_queries_ref[...] = jnp.concatenate(d_queries, axis=1).reshape(d_queries_ref.shape)
    for i, ref in enumerate(d_kv_refs):
        parts = [d_keys[at] for at in sorted(d_keys) if at[0] == i]
        parts += [d_values[at] for at in sorted(d_values) if at[0] == i]
        ref[...] = jnp.concatenate(parts, axis=1).astype(ref.dtype).reshape(ref.shape)
    add_sums(pl.program_id(0), sums_ref, jnp.broadcast_to(sums, sums_ref.shape))


def attend_back(
    core, starts, count, micro, rows, queries, pre, kv_parts, d_mixed, q_pos, k_pos, cosine, sine, gain
):
    n_ctx = len(kv_parts)
    view = partial(sequence_view, count=count, micro=micro, rows=rows)

    def spec(columns):
        return pl.BlockSpec((1, count, 1, rows, columns), lambda m, s: (0, 0, m, 0, 0))

    def whole(values):
        return pl.BlockSpec(values.shape, lambda m, s: (0, 0))

    columns, kv_columns = queries.shape[1], kv_parts[0].shape[1]
    gain = gain.reshape(1, HEAD_SIZE)
    view_shape = view(d_mixed).shape
    outs = pl.pallas_call(
        partial(attend_back_kernel, n_ctx, core),
        grid_spec=pltpu.PrefetchScalarGridSpec(
            num_scalar_prefetch=1,
            grid=(micro,),
            in_specs=[spec(kv_columns)] * n_ctx
            + [spec(columns), spec(pre.shape[1]), spec(columns)]
            + [whole(q_pos), whole(k_pos), spec(HEAD_SIZE), spec(HEAD_SIZE), whole(gain)],
            out_specs=[spec(columns), pl.BlockSpec((8, HEAD_SIZE), lambda m, s: (0, 0))]
            + [spec(kv_columns)] * n_ctx,
        ),
        out_shape=[
            jax.ShapeDtypeStruct(view_shape, jnp.bfloat16),
            jax.ShapeDtypeStruct((8, HEAD_SIZE), jnp.float32),
        ]
        + [
            jax.ShapeDtypeStruct(
                view_shape[:-1] + (kv_columns,), jnp.float32 if i == 0 else jnp.bfloat16
            )
            for i in range(n_ctx)
        ],
        compiler_params=pltpu.CompilerParams(vmem_limit_bytes=24 << 20),
        name="attend_back",
    )(
        starts,
        *[view(part) for part in kv_parts],
        view(queries),
        view(pre),
        view(d_mixed),
        q_pos,
        k_pos,
        view(cosine),
        view(sine),
        gain,
    )
    flat = [values.reshape(d_mixed.shape[0], -1) for values in outs[:1] + outs[2:]]
    return flat[0], outs[1][0], flat[1:]


def keys_back_kernel(n_got, q_cols, *refs):
    d_q_ref, own_ref = refs[:2]
    got_refs = refs[2 : 2 + n_got]
    pre_ref, cos_ref, sin_ref, gain_ref, out_ref, sums_ref = refs[2 + n_got :]
    total = own_ref[...]
    for ref in got_refs:
        total += ref[...].astype(jnp.float32)
    kv_cols = total.shape[1] // 2
    out_ref[:, :q_cols] = d_q_ref[...]
    out_ref[:, q_cols + kv_cols :] = total[:, kv_cols:].astype(jnp.bfloat16)
    sums = 0.0
    for start in range(0, kv_cols, HEAD_SIZE):
        span = slice(start, start + HEAD_SIZE)
        at = slice(q_cols + start, q_cols + start + HEAD_SIZE)
        d_pre, d_gain = norm_turn_back(
            pre_ref[:, at], total[:, span], cos_ref[...], sin_ref[...], gain_ref[...]
        )
        out_ref[:, at] = d_pre.astype(jnp.bfloat16)
        sums += d_gain
    sums_ref[...] = jnp.broadcast_to(sums, sums_ref.shape)


def keys_back(d_queries, own, got, pre, cosine, sine, gain):
    rows, q_cols = d_queries.shape
    out, sums = pl.pallas_call(
        partial(keys_back_kernel, len(got), q_cols),
        out_shape=[
            jax.ShapeDtypeStruct((rows, q_cols + own.shape[1]), jnp.bfloat16),
            jax.ShapeDtypeStruct((8, HEAD_SIZE), jnp.float32),
        ],
        name="keys_back",
    )(d_queries, own, *got, pre, cosine, sine, gain.reshape(1, HEAD_SIZE))
    return out, sums[0]


def head_gradients_kernel(count, at_ref, *refs):
    normed, branch = refs[: 2 * count], refs[2 * count : 4 * count]
    d_qkv, mixed = refs[4 * count : 4 * count + 2], refs[4 * count + 2 : 4 * count + 4]
    gains_ref = refs[4 * count + 4]
    down = (((0,), (0,)), ((), ()))
    slice_rows = normed[0].shape[1]
    for k, out_ref in enumerate(refs[4 * count + 5 :]):
        split = d_qkv[0].shape[1]
        out_ref[0, slice_rows:, :] = gains_ref[...]
        for columns, left, right in (
            (slice(0, split), normed, d_qkv),
            (slice(split, out_ref.shape[2]), branch, mixed),
        ):
            out_ref[0, :slice_rows, columns] = sum(
                lax.dot_general(
                    left[core * count + k][...],
                    right[core][...],
                    down,
                    preferred_element_type=jnp.float32,
                )
                for core in range(2)
            ).astype(jnp.bfloat16)


def head_gradients(at, n_part, n_shard, normed, d_branch, d_qkv, mixed, gains):
    rows, width = normed[0].shape
    slice_rows = width // (n_part * n_shard)
    columns = d_qkv[0].shape[1] + mixed[0].shape[1]

    def spec(k):
        return pl.BlockSpec(
            (rows, slice_rows),
            lambda j, at: (0, j * n_part + lax.rem(at[0] - k + n_part, n_part)),
        )

    def whole(values):
        return pl.BlockSpec(values.shape, lambda j, at: (0, 0))

    specs = [spec(k) for k in range(n_part)] * 2
    out_rows = slice_rows + gains.shape[0]
    out = pl.BlockSpec((1, out_rows, columns), lambda j, at: (j, 0, 0))
    return pl.pallas_call(
        partial(head_gradients_kernel, n_part),
        grid_spec=pltpu.PrefetchScalarGridSpec(
            num_scalar_prefetch=1,
            grid=(n_shard,),
            in_specs=specs + specs + [whole(values) for values in d_qkv + mixed + (gains,)],
            out_specs=[out] * n_part,
        ),
        out_shape=[jax.ShapeDtypeStruct((n_shard, out_rows, columns), jnp.bfloat16)] * n_part,
        compiler_params=pltpu.CompilerParams(vmem_limit_bytes=24 << 20),
        name="head_gradients",
    )(
        at,
        *[normed[0]] * n_part,
        *[normed[1]] * n_part,
        *[d_branch[0]] * n_part,
        *[d_branch[1]] * n_part,
        *d_qkv,
        *mixed,
        gains,
    )


def product_kernel(groups, has_got, *refs):
    count = sum(n for n, _ in groups)
    lefts, rights, rest = refs[:count], refs[count : 2 * count], refs[2 * count :]
    if has_got:
        got_ref, rest = rest[0], rest[1:]
    rows = rest[0].shape[1]
    at = 0
    for group, (n, contract) in enumerate(groups):
        total = sum(
            lax.dot_general(
                left[...],
                right[...],
                (((1,), (contract,)), ((), ())),
                preferred_element_type=jnp.float32,
            )
            for left, right in zip(lefts[at : at + n], rights[at : at + n])
        )
        at += n
        if has_got:
            total = total + got_ref[group].astype(jnp.float32)
        for k, ref in enumerate(rest):
            ref[group] = total[k * rows : (k + 1) * rows].astype(ref.dtype)


def product(groups, dtype=jnp.bfloat16, got=None, split=1):
    rows = groups[0][0][0].shape[0]
    columns = groups[0][1].shape[1 - groups[0][2]]
    block = 512 if columns % 512 == 0 else 256
    left_specs, right_specs, lefts, rights = [], [], [], []

    def right_spec(contract, depth, k):
        if contract:
            return pl.BlockSpec((block, depth), lambda j: (j, k))
        return pl.BlockSpec((depth, block), lambda j: (k, j))

    for terms, right, contract in groups:
        for k, term in enumerate(terms):
            depth = term.shape[1]
            left_specs.append(pl.BlockSpec((rows, depth), lambda j: (0, 0)))
            right_specs.append(right_spec(contract, depth, k))
            lefts.append(term)
            rights.append(right)
    n = len(groups)
    in_specs, args = left_specs + right_specs, lefts + rights
    if got is not None:
        in_specs = in_specs + [pl.BlockSpec((n, rows, block), lambda j: (0, 0, j))]
        args = args + [got]
    dtypes = [dtype] if got is None else [jnp.float32] + [jnp.bfloat16] * (split - 1)
    outs = pl.pallas_call(
        partial(
            product_kernel,
            [(len(terms), contract) for terms, _, contract in groups],
            got is not None,
        ),
        grid=(columns // block,),
        in_specs=in_specs,
        out_specs=[pl.BlockSpec((n, rows // split, block), lambda j: (0, 0, j))] * split,
        out_shape=[jax.ShapeDtypeStruct((n, rows // split, columns), kind) for kind in dtypes],
        compiler_params=pltpu.CompilerParams(vmem_limit_bytes=24 << 20),
        name="product",
    )(*args)
    return outs if got is not None else outs[0]


def ffn_gradients_kernel(*refs):
    ffn, cot, d_pre, inner = (refs[2 * i : 2 * i + 2] for i in range(4))
    out_ref = refs[8]
    down = (((0,), (0,)), ((), ()))
    start = 0
    for left, right in ((ffn, d_pre), (cot, inner)):
        stop = start + right[0].shape[1]
        out_ref[0, :, start:stop] = sum(
            lax.dot_general(
                left[core][...], right[core][...], down, preferred_element_type=jnp.float32
            )
            for core in range(2)
        ).astype(jnp.bfloat16)
        start = stop


def ffn_gradients(n_shard, ffn_in, cot, d_pre, inner):
    rows, width = ffn_in[0].shape
    ff = inner[0].shape[1]
    block = min(512, width // n_shard)
    per = width // (n_shard * block)
    left = pl.BlockSpec((rows, block), lambda j: (0, j))
    wide = pl.BlockSpec((rows, 2 * ff), lambda j: (0, 0))
    narrow = pl.BlockSpec((rows, ff), lambda j: (0, 0))
    return pl.pallas_call(
        ffn_gradients_kernel,
        grid=(width // block,),
        in_specs=[left] * 4 + [wide] * 2 + [narrow] * 2,
        out_specs=pl.BlockSpec((1, block, 3 * ff), lambda j: (j // per, j % per, 0)),
        out_shape=jax.ShapeDtypeStruct((n_shard, width // n_shard, 3 * ff), jnp.bfloat16),
        compiler_params=pltpu.CompilerParams(vmem_limit_bytes=50 << 20),
        name="ffn_gradients",
    )(*ffn_in, *cot, *d_pre, *inner)


def reorder_kernel(z_ref, in_ref, out_ref):
    out_ref[...] = in_ref[0]


def ring_order(rank, gathered):
    count, rows, width = gathered.shape
    return pl.pallas_call(
        reorder_kernel,
        grid_spec=pltpu.PrefetchScalarGridSpec(
            num_scalar_prefetch=1,
            grid=(count,),
            in_specs=[
                pl.BlockSpec(
                    (1, rows, width), lambda k, z: (lax.rem(z[0] - k + count, count), 0, 0)
                )
            ],
            out_specs=pl.BlockSpec((rows, width), lambda k, z: (k, 0)),
        ),
        out_shape=jax.ShapeDtypeStruct((count * rows, width), gathered.dtype),
        name="ring_order",
    )(rank.reshape(1), gathered)


def inner_kernel(ffn_ref, weight_ref, d_inner_ref, inner_ref, d_pre_ref):
    pre = jnp.dot(ffn_ref[...], weight_ref[...], preferred_element_type=jnp.float32)
    gate_pre, up_pre = pre[:, :FF_BLOCK], pre[:, FF_BLOCK:]
    d_inner = d_inner_ref[...]
    sigma = jax.nn.sigmoid(gate_pre)
    act_gate = gate_pre * sigma
    inner_ref[...] = (act_gate * up_pre).astype(jnp.bfloat16)
    d_gate = d_inner * up_pre * sigma * (1.0 + gate_pre * (1.0 - sigma))
    d_pre_ref[:, :FF_BLOCK] = d_gate.astype(jnp.bfloat16)
    d_pre_ref[:, FF_BLOCK:] = (d_inner * act_gate).astype(jnp.bfloat16)


def inner_parts(ffn_in, w_in, d_inner):
    rows, width = ffn_in.shape
    ff = w_in.shape[1] // 2
    narrow = pl.BlockSpec((rows, FF_BLOCK), lambda j: (0, j))
    wide = pl.BlockSpec((rows, 2 * FF_BLOCK), lambda j: (0, j))
    return pl.pallas_call(
        inner_kernel,
        grid=(ff // FF_BLOCK,),
        in_specs=[
            pl.BlockSpec((rows, width), lambda j: (0, 0)),
            pl.BlockSpec((width, 2 * FF_BLOCK), lambda j: (0, j)),
            narrow,
        ],
        out_specs=[narrow, wide],
        out_shape=[
            jax.ShapeDtypeStruct((rows, ff), jnp.bfloat16),
            jax.ShapeDtypeStruct((rows, 2 * ff), jnp.bfloat16),
        ],
        compiler_params=pltpu.CompilerParams(vmem_limit_bytes=20 << 20),
        name="inner_parts",
    )(ffn_in, w_in, d_inner)


def grouped_shards(
    n_hi,
    n_shard,
    n_ctx,
    tokens,
    span_starts,
    cotangent,
    w_query,
    key_weight,
    value_weight,
    w_out,
    attn_gain,
    query_gain,
    key_gain,
    w_gate,
    w_up,
    w_down,
    ffn_gain,
):
    bf16 = jnp.bfloat16
    f32 = jnp.float32
    z = lax.axis_index("shard")
    x = lax.axis_index("ctx")
    c = lax.axis_index("core")
    part = lax.axis_index(("hi", "ctx"))
    n_part = n_hi * n_ctx
    micro, _, rows, width = tokens.shape
    own = micro * rows
    group = n_shard * own
    n_tp = 2 * n_shard
    kv_local = KEY_VALUE_HEADS // n_tp
    q_local = QUERY_HEADS // n_tp
    group_width = QUERY_HEADS // KEY_VALUE_HEADS
    q_cols = q_local * HEAD_SIZE
    kv_cols = kv_local * HEAD_SIZE
    ff = w_down.shape[0] // 2

    slice_rows = w_query.shape[0] // n_part
    def exchange(pieces):
        return lax.all_to_all(pieces, "shard", 0, 0, tiled=True)

    def gather_plane(values):
        full = lax.all_gather(values, ("hi", "core", "ctx"), axis=0)
        return full.reshape((n_hi, 2, n_ctx) + values.shape)

    own_tokens = tokens.reshape(own, width)
    own_cot = cotangent.reshape(own, width)
    at = jnp.stack([part, c, z])
    gathered = lax.all_gather(own_tokens, "shard", axis=0)
    pieces_qkv = take_columns(at, n_part, n_shard, (w_query, key_weight, value_weight))
    pieces_in = take_columns(at, n_part, n_shard, (w_gate, w_up), FF_BLOCK)
    gain_sizes = (attn_gain.shape[0], query_gain.shape[0], key_gain.shape[0], ffn_gain.shape[0])
    gains = after(jnp.concatenate([attn_gain, query_gain, key_gain, ffn_gain]), pieces_qkv)
    gains = from_ring(gains, "shard", n_shard)
    starts = after(span_starts.reshape(micro), pieces_qkv)
    starts = jnp.stack([starts, swap(starts, "core")])
    got_qkv = after(exchange(pieces_qkv), pieces_in, gains, starts)
    gains = in_order(gains, z).astype(f32)
    w_out_rows = lax.dynamic_slice_in_dim(w_out, c * q_cols, q_cols, axis=0)
    w_down_rows = lax.dynamic_slice_in_dim(w_down, c * ff, ff, axis=0)
    ring_qkv = from_ring(got_qkv, ("hi", "ctx"), n_part)
    gathered = after(gathered, ring_qkv, gains, starts)
    ends = [0]
    for size in gain_sizes:
        ends.append(ends[-1] + size)
    gain_attn, gain_query, gain_key, gain_ffn = [
        gains[:, ends[i] : ends[i + 1]].reshape(-1) for i in range(4)
    ]

    blocks = jnp.arange(n_shard, dtype=jnp.int32)
    owners = (z - blocks) % n_shard

    def positions(ctx_rank):
        start = (owners * n_ctx + ctx_rank) * rows
        return (start[:, None] + jnp.arange(rows, dtype=jnp.int32)[None, :]).reshape(-1)

    query_pos = positions(x)
    key_pos = jnp.concatenate([positions((x - k) % n_ctx) for k in range(n_ctx)])
    cosine, sine = (table[:, 0, :] for table in spin_tables(query_pos))
    sine = jnp.where(jnp.arange(HEAD_SIZE) < HEAD_SIZE // 2, -1.0, 1.0) * sine

    def by_row(table):
        table = table.reshape(n_shard, 1, rows, HEAD_SIZE)
        return jnp.broadcast_to(table, (n_shard, micro, rows, HEAD_SIZE)).reshape(group, HEAD_SIZE)

    cosine, sine = by_row(cosine), by_row(sine)
    query_pos = query_pos[:, None]
    key_pos = key_pos[None, :]
    order = (n_shard, micro, rows)

    normed_mine = norm_group(z, gathered, gain_attn)
    normed_theirs = swap(normed_mine, "core")
    got_in = exchange_ring(after(pieces_in, gathered), z, n_shard)
    cot_all = lax.all_gather(after(own_cot, gathered), "shard", axis=0)
    turns = (cosine, sine, gain_query, gain_key)
    q_mine, kv_mine, pre_mine = project(at, q_cols, normed_mine, ring_qkv, *turns)
    q_theirs, kv_theirs, pre_theirs = project(
        at, q_cols, after(normed_theirs, kv_mine), ring_qkv, *turns
    )
    kv_parts = from_ring(jnp.concatenate([kv_mine, kv_theirs], axis=0), "ctx", n_ctx)
    kv_mine_parts = [values[:group] for values in kv_parts]
    kv_theirs_parts = [values[group:] for values in kv_parts]
    w_qkv = lay_order(at, after(ring_qkv, kv_theirs))
    mixed_mine = attend(
        0, starts, *order, after(q_mine, w_qkv), kv_mine_parts, query_pos, key_pos
    )
    mixed_theirs = attend(
        1, starts, *order, after(q_theirs, mixed_mine), kv_theirs_parts, query_pos, key_pos
    )
    def core_sum(mine, theirs, right, contract):
        got = swap(product([(theirs, right, contract)]), "core")
        pieces = product([(mine, right, contract)], got=got, split=n_shard)
        return [piece[0] for piece in pieces]

    branch_sent = core_sum([mixed_mine], [mixed_theirs], w_out_rows, 0)
    hidden_in = own_tokens.astype(f32)
    got_in = place(z, after(got_in, branch_sent))
    cot_all = after(cot_all, got_in)
    w_in = lax.all_gather(after(got_in, cot_all), ("hi", "ctx"), axis=1, tiled=True)
    w_in = w_in.reshape(width, -1)
    cot_mine = ring_order(z, cot_all)
    cot_theirs = swap(cot_mine, "core")
    branch_terms = send_terms(branch_sent, "shard", n_shard)
    middle = hidden_in + sum_terms(after(branch_terms, cot_mine))

    recip_m = recip_rms(middle)
    unit_m = middle * recip_m
    ffn_own = (unit_m * gain_ffn).astype(bf16)
    ffn_ring = from_ring(ffn_own, "shard", n_shard)
    d_inner_mine = product([([after(cot_mine, ffn_own)], w_down_rows, 1)], f32)[0]
    d_inner_theirs = product([([after(cot_theirs, d_inner_mine)], w_down_rows, 1)], f32)[0]
    ffn_mine = jnp.concatenate(after(ffn_ring, d_inner_theirs, w_in), axis=0)
    ffn_theirs = swap(ffn_mine, "core")
    inner_mine, d_pre_mine = inner_parts(ffn_mine, w_in, d_inner_mine)
    inner_theirs, d_pre_theirs = inner_parts(
        after(ffn_theirs, inner_mine), w_in, d_inner_theirs
    )
    grad_in = ffn_gradients(
        n_shard,
        (ffn_mine, ffn_theirs),
        (cot_mine, cot_theirs),
        (d_pre_mine, d_pre_theirs),
        (inner_mine, inner_theirs),
    )
    part_in = lax.psum_scatter(grad_in, ("hi", "ctx"), scatter_dimension=1, tiled=True)
    d_ffn_sent = core_sum([d_pre_mine], [after(d_pre_theirs, grad_in)], w_in, 1)
    d_ffn_in = sum_terms(send_terms(d_ffn_sent, "shard", n_shard))
    d_middle = own_cot.astype(f32) + norm_back(unit_m, recip_m, gain_ffn, d_ffn_in)

    d_branch_own = d_middle.astype(bf16)
    branch_ring = from_ring(d_branch_own, "shard", n_shard)
    branch_mine, part_in = lax.optimization_barrier((jnp.concatenate(branch_ring, axis=0), part_in))
    branch_theirs = swap(branch_mine, "core")
    d_mixed_mine = product([([branch_mine], w_out_rows, 1)])[0]
    tables = (query_pos, key_pos, cosine, sine, gain_query)
    d_q_mine, gain_q_mine, d_kv_mine = attend_back(
        0, starts, *order, q_mine, pre_mine, kv_mine_parts, d_mixed_mine, *tables
    )
    d_mixed_theirs = product([([after(branch_theirs, d_q_mine)], w_out_rows, 1)])[0]
    d_q_theirs, gain_q_theirs, d_kv_theirs = attend_back(
        1, starts, *order, q_theirs, pre_theirs, kv_theirs_parts, d_mixed_theirs, *tables
    )

    sent_in = exchange_ring(part_in[..., : 2 * ff], z, n_shard)
    full_down = gather_plane(part_in[..., 2 * ff :])

    def keys_gradient(d_queries, d_kv, pre, *others):
        got = [
            lax.ppermute(d_kv[n_ctx - k], "ctx", [(i, (i + k) % n_ctx) for i in range(n_ctx)])
            for k in range(1, n_ctx)
        ]
        got = [after(values, *others) for values in got]
        return keys_back(d_queries, d_kv[0], got, pre, cosine, sine, gain_key)

    d_qkv_mine, gain_k_mine = keys_gradient(d_q_mine, d_kv_mine, pre_mine, d_q_theirs)
    d_qkv_theirs, gain_k_theirs = keys_gradient(
        d_q_theirs, d_kv_theirs, pre_theirs, d_qkv_mine
    )
    sent_in = place(z, after(sent_in, d_qkv_theirs))
    full_in = gather_plane(after(sent_in, full_down))
    qkv_cols = q_cols + 2 * kv_cols
    head_columns = qkv_cols + q_cols
    head_gains = jnp.concatenate([gain_q_mine + gain_q_theirs, gain_k_mine + gain_k_theirs])
    head_gains = jnp.zeros((16, head_columns), f32).at[0, : 2 * HEAD_SIZE].set(head_gains)
    sent = head_gradients(
        at,
        n_part,
        n_shard,
        (normed_mine, normed_theirs),
        (branch_mine, branch_theirs),
        (after(d_qkv_mine, sent_in), d_qkv_theirs),
        (mixed_mine, mixed_theirs),
        head_gains.astype(bf16),
    )
    part_heads = send_terms(sent, ("hi", "ctx"), n_part)
    got = product([([after(d_qkv_theirs, sent)], w_qkv, 1), ([inner_theirs], w_down_rows, 0)])
    last = product(
        [([after(d_qkv_mine, got)], w_qkv, 1), ([inner_mine], w_down_rows, 0)],
        got=swap(got, "core"),
        split=n_shard,
    )
    part_heads = sum_terms(after(part_heads, last)).astype(bf16)
    ring_heads = exchange(part_heads[..., :qkv_cols])
    last = send_terms(after(last, part_heads), "shard", n_shard)
    part_heads = jnp.concatenate([ring_heads, part_heads[..., qkv_cols:]], axis=-1)
    mine_heads = from_ring(part_heads, ("hi", "ctx"), n_part)
    grad_down = lay_rows(after(full_down, part_heads))
    grad_gate, grad_up, ffn_sums = lay_in(after(full_in, grad_down), w_gate, w_up)
    mine_heads = after(mine_heads, grad_gate)
    theirs_heads = [swap(values, "core") for values in mine_heads]
    grad_query, grad_key, grad_value, grad_out, attn_sums, gain_sums = lay_heads(
        at, mine_heads, theirs_heads, w_query, key_weight, value_weight
    )
    last = sum_terms(after(last, mine_heads))
    recip_h = recip_rms(hidden_in)
    unit_h = hidden_in * recip_h
    input_grad = d_middle + norm_back(unit_h, recip_h, gain_attn, last[0])
    result = (middle + last[1]).astype(bf16)
    head_gains = gain_sums[0, : 2 * HEAD_SIZE].reshape(2, HEAD_SIZE)
    head_size = query_gain.shape[0]
    head_gains = lax.dynamic_slice_in_dim(head_gains, z * head_size, head_size, axis=1)
    grad_ffn_gain = jnp.sum(ffn_sums, axis=1) / ffn_gain.astype(f32)
    grad_attn_gain = jnp.sum(attn_sums, axis=1) / attn_gain.astype(f32)

    return (
        result.reshape(tokens.shape),
        input_grad.reshape(tokens.shape),
        grad_query,
        grad_key,
        grad_value,
        grad_out,
        grad_attn_gain,
        head_gains[0],
        head_gains[1],
        grad_gate,
        grad_up,
        grad_down,
        grad_ffn_gain,
    )


def solution(mesh):
    n_rep, n_shard, n_ctx = (mesh.shape[name] for name in ("rep", "shard", "ctx"))
    if n_rep % 2 == 0 and KEY_VALUE_HEADS % (2 * n_shard) == 0:
        mesh = Mesh(
            mesh.devices.reshape(n_rep // 2, 2, n_shard, n_ctx), ("hi", "core", "shard", "ctx")
        )
        rep = ("hi", "core")
        body = partial(grouped_shards, n_rep // 2, n_shard, n_ctx)
    else:
        rep = "rep"
        body = shards_general
    in_specs = (
        P(None, rep, ("shard", "ctx"), None),
        P(None, rep),
        P(None, rep, ("shard", "ctx"), None),
        P("shard", None),
        P("shard", None),
        P("shard", None),
        P("shard", None),
        P("shard"),
        P("shard"),
        P("shard"),
        P("shard", None),
        P("shard", None),
        P("shard", None),
        P("shard"),
    )
    out_specs = (
        P(None, rep, ("shard", "ctx"), None),
        P(None, rep, ("shard", "ctx"), None),
        P("shard", None),
        P("shard", None),
        P("shard", None),
        P("shard", None),
        P("shard"),
        P("shard"),
        P("shard"),
        P("shard", None),
        P("shard", None),
        P("shard", None),
        P("shard"),
    )
    return jax.shard_map(body, mesh=mesh, in_specs=in_specs, out_specs=out_specs, check_vma=False)
```
